32 devices in a mesh: groups: 2 (over x), dp: 8 (over z, y), expert: 2 (over core).
Axes of the slice: x: 2, y: 2, z: 4, core: 2. Of those that a mesh axis runs over, the one named last changes fastest.
Arguments:
- expert_ids: int32 [12288, 2], P(('groups', 'dp')), parts along dimension 0, may hold values from 0 to 7, all different within a row; in each aligned block of 768 rows (0 to 767, 768 to 1535, ...) at most 384 rows name the same one
- gates: float32 [12288, 2], P(('groups', 'dp')), parts along dimension 0, may hold values from 0.2 to 1
- expert_out: bfloat16 [49152, 3072], P(('groups', 'dp', 'expert')), parts along dimension 0, may hold values from -6 to 6
Outputs:
- moment: float32 [6144, 3072], P(('groups', 'dp'), 'expert'), parts along dimension 0
The draws below stay inside these ranges and needn't reach their ends.
There are 2 independent parts, one for each index of `groups`. The reference program is written for one: setup_inputs(seed, part) draws one part's arguments, and reference() takes and returns one part's arrays. A program takes and returns all parts, laid end to end along the dimension named above; each array names one. Nothing has to cross between parts.
Inputs may be any that keep to these rules, and one draw needn't show every extreme that they name: `expert_ids`: the two experts of a token differ; of the 768 tokens of one index of dp at most 384 name one expert, a bound that some block reaches.
All inputs are finite; a program needn't handle non-finite values.
Results may differ from the reference program's by a relative error of at most 0.0026.
Values may be sent and summed in bfloat16 or wider, within the bound.
No kernel may reach another device: no remote copies, remote signals or barrier semaphores. Data moves between devices by JAX's collectives and lax.ppermute only.
A program may use at most 128 MiB of HBM per device.

```python
import math
import jax
import jax.numpy as jnp
import numpy as np
from jax import lax

DW = 3072
EXPERTS = 8
TOP = 2
TOK_DEV = 768
CAP = 384
TOKENS = 6144
N_DP = 8


def with_spikes(entries, stream_key, source, target, blocks, factor):
    def block_of(position):
        return (jnp.arange(entries.shape[position]) // (entries.shape[position] // blocks)).reshape((-1,) + (1,) * (entries.ndim - 1 - position))

    one_side = jax.random.permutation(stream_key, blocks)[block_of(target)]
    far = (block_of(target) + blocks // 2) % blocks
    return jnp.where((block_of(source) == one_side) | (block_of(source) == far), factor * entries, entries)


def shard_levels(stream_key, extent, split, least, high):
    def one(dim, shards_of):
        heights = jax.random.uniform(jax.random.fold_in(jax.random.fold_in(stream_key, 6), dim), (shards_of,), jnp.float32, least / len(split), high / len(split))
        return jnp.repeat(jnp.exp(heights), extent[dim] // shards_of).reshape((-1,) + (1,) * (len(extent) - dim - 1))

    factor_of = one(*split[0])
    for cut in split[1:]:
        factor_of = factor_of * one(*cut)
    return factor_of


def assign_block(rng, own, number, rows, number_of, top, bound, slope):
    sequence = jax.random.permutation(rng, number_of)
    heavy_load, ordinary = load_shares(number_of, rows * top, bound, slope, True), load_shares(number_of, rows * top, bound, slope, False)
    places = jnp.arange(number_of)

    def named(lengths, rotation):
        used = int((lengths > 0).sum())
        fixed = max(1, used // 4)
        moved = fixed + (places - fixed + rotation * (used - fixed)) % max(1, number_of - fixed)
        return jnp.zeros((number_of,), jnp.int32).at[sequence[jnp.where(places < fixed, places, moved)]].set(jnp.asarray(lengths, jnp.int32))

    lengths = jnp.where(number % 4 == 0, named(heavy_load, number // 4), named(ordinary, number - number // 4 - 1))
    mixed = jax.random.permutation(jax.random.fold_in(own, 3), number_of)
    source_of, sink = mixed[0:number_of // 2 * 2:2], mixed[1:number_of // 2 * 2:2]
    margin = jnp.minimum(lengths[source_of] - 1, bound - lengths[sink]) // 2
    margin = jnp.where((source_of == sequence[0]) | (sink == sequence[0]) | (lengths[sink] == 0), 0, jnp.maximum(margin, 0))
    moved = jax.random.randint(jax.random.fold_in(own, 4), (number_of // 2,), 0, 1 << 20) % (margin + 1)
    lengths = lengths.at[source_of].add(-moved).at[sink].add(moved)
    items = jnp.searchsorted(jnp.cumsum(lengths), jnp.arange(rows * top), side="right").astype(jnp.int32)
    table = items.reshape(top, rows).T
    table = table[jax.random.permutation(jax.random.fold_in(own, 1), rows)]
    rotation = jax.random.randint(jax.random.fold_in(own, 2), (rows, 1), 0, top)
    return jnp.take_along_axis(table, (jnp.arange(top)[None, :] + rotation) % top, axis=1)


def load_shares(count, total, reach, skew, full):
    weights = [(1 << 20) // math.isqrt(standing ** skew) + 1 for standing in range(1, count + 1)]
    largest = reach if full else min(reach, max(-(-total // count), total * weights[0] // sum(weights)))
    least = 1 if total - largest >= count - 1 else 0
    given, rest = [largest] + [least] * (count - 1), total - largest - least * (count - 1)
    while rest > 0:
        candidates = [i for i in range(1, count) if given[i] < largest] or [i for i in range(1, count) if given[i] < reach]
        mass, remaining = sum([weights[i] for i in candidates]), rest
        for i in candidates:
            addition = min(reach - given[i], max(1, remaining * weights[i] // mass), rest)
            given[i] = given[i] + addition
            rest = rest - addition
    return np.array(given)


def heavy_noise(stream_key, dims, spread, limit, shards, heavy, held_as=jnp.bfloat16):
    values = spread * jax.random.normal(stream_key, dims, jnp.float32)
    if shards:
        values = values * shard_levels(stream_key, dims, shards, -0.22, 0.18)
    return jnp.clip(with_spikes(values, jax.random.fold_in(stream_key, 3), *heavy), -limit, limit).astype(held_as)


def setup_inputs(seed: int = 0, part: int = 0) -> dict:
    arg_keys = jax.random.split(jax.random.key(seed), 4)
    part_splits = jax.random.split(jax.random.fold_in(arg_keys[3], part), 4)
    expert_ids_keys = jax.random.split(jax.random.fold_in(part_splits[0], 1), TOKENS // TOK_DEV)
    expert_ids_turns = jax.random.permutation(jax.random.fold_in(part_splits[0], 3), TOKENS // TOK_DEV)
    expert_ids = jax.vmap(lambda own, number: assign_block(jax.random.fold_in(part_splits[0], 2), own, number, TOK_DEV, EXPERTS, TOP, CAP, 1))(expert_ids_keys, expert_ids_turns).reshape((TOKENS, TOP))
    gates = jnp.clip(jnp.exp(math.log(1.0) - 1.609438 * jax.random.uniform(part_splits[1], (TOKENS, TOP), jnp.float32) ** shard_levels(part_splits[1], (TOKENS, TOP), ((0, 8),), -0.2, 0.2)), 0.2, 1.0)
    expert_out = heavy_noise(part_splits[2], (N_DP * EXPERTS * CAP, DW), 1.0, 6.0, ((0, 16),), (0, 1, 16, 2.0))
    return dict(expert_ids=expert_ids, gates=gates, expert_out=expert_out)


def slot_rows(shard_ids):
    labels = jnp.arange(EXPERTS, dtype=jnp.int32)
    matches = (shard_ids[:, :, None] == labels[None, None, :]).astype(jnp.int32)
    named = jnp.sum(matches, axis=1)
    before = jnp.cumsum(named, axis=0) - named
    counts = jnp.sum(matches * before[:, None, :], axis=2)
    return shard_ids * CAP + counts


def reference(expert_ids, gates, expert_out):
    shard_ids = expert_ids.reshape(N_DP, TOK_DEV, TOP)
    row_index = jax.vmap(slot_rows)(shard_ids)
    offsets = (jnp.arange(N_DP, dtype=jnp.int32) * (EXPERTS * CAP))[:, None, None]
    flat_rows = (row_index + offsets).reshape(-1).astype(jnp.int32)
    picked = jnp.take(expert_out, flat_rows, axis=0).reshape(TOKENS, TOP, DW)
    combined = gates[:, 0:1] * picked[:, 0].astype(jnp.float32) + gates[:, 1:2] * picked[:, 1].astype(jnp.float32)
    combined = combined.astype(jnp.bfloat16)
    combined_f = combined.astype(jnp.float32)
    moment = jnp.dot(combined_f.T, combined_f, precision=lax.Precision.HIGHEST, preferred_element_type=jnp.float32)
    return moment / TOKENS
```

```python
import functools

import jax
import jax.numpy as jnp
import numpy as np
from jax import lax
from jax.experimental import pallas as pl
from jax.experimental.pallas import tpu as pltpu
from jax.sharding import PartitionSpec as P

EXPERTS = 8
CAP = 384
SNAKE = (0, 2, 4, 6, 7, 5, 3, 1)
F32, BF16 = jnp.float32, jnp.bfloat16


def dot_tn(a, b):
    return lax.dot_general(a, b, (((0,), (0,)), ((), ())), preferred_element_type=F32)


def select_kernel(final, scalars, ids_ref, gates_ref, rows_ref, *refs):
    if final:
        acc_ref, out_ref, sel_ref = refs
    else:
        out_ref, sel_ref = refs
    tokens = ids_ref.shape[0]
    depth = rows_ref.shape[0]

    @pl.when(pl.program_id(0) == 0)
    def _():
        lanes = lax.broadcasted_iota(jnp.int32, (tokens, 128), 1)
        hits = [ids_ref[:, k : k + 1] == lanes for k in range(2)]
        named = (hits[0] | hits[1]).astype(F32).astype(BF16)
        earlier = (
            lax.broadcasted_iota(jnp.int32, (tokens, tokens), 1)
            < lax.broadcasted_iota(jnp.int32, (tokens, tokens), 0)
        ).astype(F32).astype(BF16)
        before = jnp.dot(earlier, named, preferred_element_type=F32)
        for k in range(2):
            count = jnp.sum(jnp.where(hits[k], before, 0.0), axis=1, keepdims=True)
            row = ids_ref[:, k : k + 1] * CAP + count.astype(jnp.int32) - scalars[1]
            here = lax.broadcasted_iota(jnp.int32, (tokens, depth), 1) == row
            sel_ref[k * tokens : (k + 1) * tokens, :] = here.astype(F32).astype(BF16)

    picked = jnp.dot(sel_ref[...], rows_ref[...], preferred_element_type=F32)
    total = gates_ref[:, 0:1] * picked[:tokens] + gates_ref[:, 1:2] * picked[tokens:]
    if final:
        total = total + acc_ref[...]
    out_ref[...] = total.astype(out_ref.dtype)


def gated_half(ids, gates, rows, column_block, first_row, width, acc=None, tile=512):
    tokens, depth = ids.shape[0], rows.shape[0]
    steps = width // tile
    scalars = jnp.stack([column_block * steps, first_row]).astype(jnp.int32)
    whole = lambda j, s: (0, 0)
    in_specs = [
        pl.BlockSpec((tokens, 2), whole),
        pl.BlockSpec((tokens, 2), whole),
        pl.BlockSpec((depth, tile), lambda j, s: (0, s[0] + j)),
    ]
    args = [ids, gates, rows]
    if acc is not None:
        in_specs.append(pl.BlockSpec((tokens, tile), lambda j, s: (0, j)))
        args.append(acc)
    return pl.pallas_call(
        functools.partial(select_kernel, acc is not None),
        out_shape=jax.ShapeDtypeStruct((tokens, width), F32 if acc is None else BF16),
        grid_spec=pltpu.PrefetchScalarGridSpec(
            num_scalar_prefetch=1,
            grid=(steps,),
            in_specs=in_specs,
            out_specs=pl.BlockSpec((tokens, tile), lambda j, s: (0, j)),
            scratch_shapes=[pltpu.VMEM((2 * tokens, depth), BF16)],
        ),
        cost_estimate=pl.CostEstimate(
            flops=4 * tokens * depth * width, bytes_accessed=depth * width * 2 + tokens * width * 6, transcendentals=0
        ),
        compiler_params=pltpu.CompilerParams(vmem_limit_bytes=48 << 20),
        name="gated_first" if acc is None else "gated_second",
    )(scalars, *args)


def blocks_kernel(jobs, mine_ref, other_ref, out_ref, turned_ref):
    n = pl.program_id(0)
    width = out_ref.shape[1]

    @pl.when(jobs[n, 3] == 1)
    def _():
        at = pl.ds(pl.multiple_of(jobs[n, 1] * width, 128), width)

        @pl.when(jobs[n, 0] == 1)
        def _():
            turned_ref[...] = mine_ref[:, at].T

        @pl.when(jobs[n, 0] == 0)
        def _():
            turned_ref[...] = other_ref[:, at].T

    at = pl.ds(pl.multiple_of(jobs[n, 2] * width, 128), width)
    out_ref[0] = jnp.dot(turned_ref[...], mine_ref[:, at], preferred_element_type=F32).astype(out_ref.dtype)


def moment_blocks(jobs, mine, other, width, dtype):
    tokens = mine.shape[0]
    count = jobs.shape[0]
    whole = pl.BlockSpec(mine.shape, lambda n, s: (0, 0))
    return pl.pallas_call(
        blocks_kernel,
        out_shape=jax.ShapeDtypeStruct((count, width, width), dtype),
        grid_spec=pltpu.PrefetchScalarGridSpec(
            num_scalar_prefetch=1,
            grid=(count,),
            in_specs=[whole, whole],
            out_specs=pl.BlockSpec((1, width, width), lambda n, s: (n, 0, 0)),
            scratch_shapes=[pltpu.VMEM((width, tokens), BF16)],
        ),
        cost_estimate=pl.CostEstimate(
            flops=2 * count * tokens * width * width,
            bytes_accessed=4 * mine.size + count * width * width * 4,
            transcendentals=0,
        ),
        compiler_params=pltpu.CompilerParams(vmem_limit_bytes=40 << 20),
        name="blocks_first" if dtype == BF16 else "blocks_rest",
    )(jobs, mine, other)


def is_diagonal(b, e):
    return b // 4 == e


def owns_extra(b, e):
    return (b, e) in ((0, 0), (3, 0), (4, 1), (7, 1))


def owned_columns(b, e):
    shift = 0 if is_diagonal(b, e) or e == 1 else 1
    return [(b + shift) % 4, (b + shift + 1) % 4, (b + 2) % 4]


FIRST = ((1, 3), (0, 4), (1, 4), (2, 4), (0, 5), (2, 5))
REST = tuple((x, t) for t in (3, 2, 6, 5, 1, 7, 0) for x in range(3) if (x, t) not in FIRST)


def job_table(which):
    table = np.zeros((8, 2, len(which), 4), np.int32)
    for p, b in enumerate(SNAKE):
        for e in range(2):
            last = None
            for n, (x, t) in enumerate(which):
                q = SNAKE[(p + t) % 8]
                table[b, e, n] = (q // 4 == e, q % 4, owned_columns(q, e)[x], q != last)
                last = q
    return table


def ring_perm(x, distance, direction):
    pairs = []
    for q, b in enumerate(SNAKE):
        for e in range(2):
            if x == 2 and not owns_extra(b, e):
                continue
            source = SNAKE[(q - direction * distance) % 8]
            target = SNAKE[(q - direction * (distance - 1)) % 8]
            pairs.append((source * 2 + e, target * 2 + e))
    return pairs


def mirror_perms():
    perms = [[], [], []]
    for b in range(8):
        for e in range(2):
            here = b * 2 + e
            if is_diagonal(b, e):
                perms[1].append((here, (b // 4 * 4 + (b + 1) % 4) * 2 + e))
                if owns_extra(b, e):
                    perms[2].append((here, (b // 4 * 4 + (b + 2) % 4) * 2 + e))
            elif e == 1:
                perms[0].append((here, (4 + b) * 2))
                perms[1].append((here, (4 + (b + 1) % 4) * 2))
            else:
                perms[0].append((here, (b + 1) % 4 * 2 + 1))
                perms[1].append((here, (b + 2) % 4 * 2 + 1))
    return perms


def place_table():
    table = np.zeros((8, 2, 5), np.int32)
    for b in range(8):
        for e in range(2):
            own = owned_columns(b, e)
            if is_diagonal(b, e):
                table[b, e] = (own[0], own[1], (b + 3) % 4, (b + 2) % 4, 1 if owns_extra(b, e) else 2)
            elif e == 1:
                table[b, e] = (own[0], own[1], (b + 2) % 4, (b + 3) % 4, 0)
            else:
                table[b, e] = (own[0], own[1], (b + 3) % 4, b % 4, 0)
    return table


def finish_kernel(scale, place, parts_ref, right0, left0, right1, left1, right2, left2, w0, w1, w2, out_ref):
    width = w0.shape[0]

    def put(n, value):
        out_ref[:, pl.ds(pl.multiple_of(place[n] * width, 128), width)] = value

    def owned(n, right, left):
        return (parts_ref[n] + right[...].astype(F32) + left[...].astype(F32)) * scale

    put(0, owned(0, right0, left0))
    put(1, owned(1, right1, left1))
    put(2, w1[...].astype(F32).T)

    @pl.when(place[4] == 0)
    def _():
        put(3, w0[...].astype(F32).T)

    @pl.when(place[4] == 1)
    def _():
        put(3, owned(2, right2, left2))

    @pl.when(place[4] == 2)
    def _():
        put(3, w2[...].astype(F32).T)


def symmetric_moment(mine, other, total_tokens):
    width = mine.shape[1] // 4
    both = ("dp", "expert")
    dp, e = lax.axis_index("dp"), lax.axis_index("expert")
    first = moment_blocks(jnp.asarray(job_table(FIRST))[dp, e], mine, other, width, BF16)
    rest = moment_blocks(jnp.asarray(job_table(REST))[dp, e], mine, other, width, F32)
    scale = 1.0 / total_tokens

    arrived = {}
    chains = []
    for x in range(3):
        right_steps = 3 if x == 1 else 4
        chains.append((x, 1, right_steps))
        chains.append((x, -1, 7 - right_steps))
    for x, direction, steps in chains:
        at = lambda d: (x, d if direction == 1 else 8 - d)
        value = first[FIRST.index(at(steps))]
        for distance in range(steps, 0, -1):
            value = lax.ppermute(value, both, ring_perm(x, distance, direction))
            if distance > 1:
                value = (value.astype(F32) + rest[REST.index(at(distance - 1))]).astype(BF16)
        arrived[x, direction] = value

    own = [REST.index((x, 0)) for x in range(3)]
    mirrored = []
    for x, perm in enumerate(mirror_perms()):
        done = rest[own[x]] + arrived[x, 1].astype(F32) + arrived[x, -1].astype(F32)
        mirrored.append(lax.ppermute((done * scale).astype(BF16), both, perm))

    assert own == [own[0], own[0] + 1, own[0] + 2] and own[0] % 3 == 0
    block = pl.BlockSpec((width, width), lambda i, s: (0, 0))
    return pl.pallas_call(
        functools.partial(finish_kernel, scale),
        out_shape=jax.ShapeDtypeStruct((width, 4 * width), F32),
        grid_spec=pltpu.PrefetchScalarGridSpec(
            num_scalar_prefetch=1,
            grid=(1,),
            in_specs=[pl.BlockSpec((3, width, width), lambda i, s: (own[0] // 3, 0, 0))] + [block] * 9,
            out_specs=pl.BlockSpec((width, 4 * width), lambda i, s: (0, 0)),
        ),
        compiler_params=pltpu.CompilerParams(vmem_limit_bytes=32 << 20),
        name="finish",
    )(
        jnp.asarray(place_table())[dp, e],
        rest,
        *[arrived[x, direction] for x in range(3) for direction in (1, -1)],
        *mirrored,
    )


def per_device(expert_ids, gates, expert_out):
    tokens = expert_ids.shape[0]
    channels = expert_out.shape[1]
    depth = expert_out.shape[0]
    members = lax.axis_size("expert")
    dp_size = lax.axis_size("dp")
    member = lax.axis_index("expert")
    half = channels // members
    swap = [(0, 1), (1, 0)]

    peer_rows = lax.ppermute(
        lax.dynamic_slice_in_dim(expert_out, (1 - member) * half, half, 1), "expert", swap
    )
    part = gated_half(expert_ids, gates, expert_out, member, member * depth, half)
    mine = gated_half(
        expert_ids, gates, peer_rows, jnp.zeros_like(member), (1 - member) * depth, half, acc=part
    )
    other = lax.ppermute(mine, "expert", swap)

    total_tokens = tokens * dp_size
    if dp_size == 8 and channels == 8 * 384:
        return symmetric_moment(mine, other, total_tokens)
    low = jnp.where(member == 0, mine, other)
    high = jnp.where(member == 0, other, mine)
    slab = dot_tn(jnp.concatenate([low, high], axis=1), mine)
    return lax.psum_scatter(slab, "dp", scatter_dimension=0, tiled=True) / total_tokens


def solution(mesh):
    assert mesh.shape["expert"] == 2
    in_specs = (
        P(("groups", "dp"), None),
        P(("groups", "dp"), None),
        P(("groups", "dp", "expert"), None),
    )
    out_specs = P(("groups", "dp"), "expert")
    return jax.shard_map(
        per_device, mesh=mesh, in_specs=in_specs, out_specs=out_specs, check_vma=False
    )
```

```python
import functools

import jax
import jax.numpy as jnp
import numpy as np
from jax import lax
from jax.experimental import pallas as pl
from jax.experimental.pallas import tpu as pltpu
from jax.sharding import PartitionSpec as P

EXPERTS = 8
CAP = 384
BATCH = 96
WINDOW = 128
SNAKE = (0, 2, 4, 6, 7, 5, 3, 1)
F32, BF16, I32 = jnp.float32, jnp.bfloat16, jnp.int32


def plan_kernel(member, ids_ref, gates_ref, pick_ref, starts_ref, coef_ref):
    tokens = ids_ref.shape[0]
    local = EXPERTS // 2
    lanes = lax.broadcasted_iota(I32, (tokens, 128), 1)
    ids = [ids_ref[:, k : k + 1] for k in range(2)]
    hits = [ids[k] == lanes for k in range(2)]
    named = jnp.where(hits[0] | hits[1], 1.0, 0.0).astype(BF16)
    earlier = jnp.where(
        lax.broadcasted_iota(I32, (tokens, tokens), 1) < lax.broadcasted_iota(I32, (tokens, tokens), 0), 1.0, 0.0
    ).astype(BF16)
    before = jnp.dot(earlier, named, preferred_element_type=F32)

    slots = [ids[k] - member[0] * local for k in range(2)]
    here = [jnp.where((slots[k] >= 0) & (slots[k] < local), 1.0, 0.0) for k in range(2)]
    gates = [gates_ref[:, k : k + 1] for k in range(2)]
    both = here[0] * here[1]
    neither = (1.0 - here[0]) * (1.0 - here[1])
    mixed = 1.0 - both - neither
    weights = [here[k] * jnp.where(both > 0.5, gates[k], 1.0) for k in range(2)]
    ours = here[0] * gates[0] + here[1] * gates[1]
    theirs = (1.0 - here[0]) * gates[0] + (1.0 - here[1]) * gates[1]
    ours = jnp.where(mixed > 0.5, ours, both)
    theirs = jnp.where(mixed > 0.5, theirs, neither)
    coef_ref[...] = jnp.where(
        lanes == 0, weights[0], jnp.where(lanes == 1, weights[1], jnp.where(lanes == 2, ours, theirs))
    )

    columns = lax.broadcasted_iota(I32, (BATCH, local * WINDOW), 1)
    for b in range(tokens // BATCH):
        rows = slice(b * BATCH, (b + 1) * BATCH)
        start = before[b * BATCH : b * BATCH + 1, :].astype(I32)
        start = jnp.minimum((start >> 4) << 4, CAP - WINDOW)
        starts_ref[b : b + 1, :] = start
        ahead = before[rows] - start.astype(F32)
        for k in range(2):
            offset = jnp.sum(jnp.where(hits[k][rows], ahead, 0.0), axis=1, keepdims=True).astype(I32)
            at = jnp.where(here[k][rows] > 0.5, slots[k][rows] * WINDOW + offset, -1)
            pick_ref[(2 * b + k) * BATCH : (2 * b + k + 1) * BATCH, :] = jnp.where(columns == at, 1.0, 0.0).astype(BF16)


def plan(ids, gates, member):
    tokens = ids.shape[0]
    whole = lambda shape: pl.BlockSpec(shape, lambda i, s: (0, 0))
    shapes = [((2 * tokens, EXPERTS // 2 * WINDOW), BF16), ((tokens // BATCH, 128), I32), ((tokens, 128), F32)]
    return pl.pallas_call(
        plan_kernel,
        out_shape=[jax.ShapeDtypeStruct(*s) for s in shapes],
        grid_spec=pltpu.PrefetchScalarGridSpec(
            num_scalar_prefetch=1,
            grid=(1,),
            in_specs=[whole(ids.shape), whole(gates.shape)],
            out_specs=[whole(s[0]) for s in shapes],
        ),
        compiler_params=pltpu.CompilerParams(vmem_limit_bytes=32 << 20),
        name="plan",
    )(member.reshape(1).astype(I32), ids, gates)


def pick_kernel(where_, starts, pick_ref, coef_ref, rows_ref, out_ref):
    local = EXPERTS // 2
    for b in range(out_ref.shape[0] // BATCH):
        windows = []
        for k in range(local):
            first = k * CAP + starts[b, where_[1] * local + k]
            windows.append(rows_ref[pl.ds(pl.multiple_of(first, 16), WINDOW), :])
        picked = jnp.dot(
            pick_ref[2 * b * BATCH : 2 * (b + 1) * BATCH, :],
            jnp.concatenate(windows, axis=0),
            preferred_element_type=F32,
        )
        rows = slice(b * BATCH, (b + 1) * BATCH)
        total = coef_ref[rows, 0:1] * picked[:BATCH] + coef_ref[rows, 1:2] * picked[BATCH:]
        out_ref[rows, :] = total.astype(BF16)


def pick_half(where_, starts, pick, coef, rows, width, tile=512):
    tokens = coef.shape[0]
    steps = width // tile
    whole = lambda shape: pl.BlockSpec(shape, lambda j, w, s: (0, 0))
    return pl.pallas_call(
        pick_kernel,
        out_shape=jax.ShapeDtypeStruct((tokens, width), BF16),
        grid_spec=pltpu.PrefetchScalarGridSpec(
            num_scalar_prefetch=2,
            grid=(steps,),
            in_specs=[
                whole(pick.shape),
                whole(coef.shape),
                pl.BlockSpec((rows.shape[0], tile), lambda j, w, s: (0, w[0] * steps + j)),
            ],
            out_specs=pl.BlockSpec((tokens, tile), lambda j, w, s: (0, j)),
        ),
        cost_estimate=pl.CostEstimate(
            flops=2 * pick.size * width, bytes_accessed=2 * (rows.shape[0] + tokens) * width, transcendentals=0
        ),
        compiler_params=pltpu.CompilerParams(vmem_limit_bytes=60 << 20),
        name="pick",
    )(where_, starts, pick, coef, rows)


def merge_kernel(first, coef_ref, ours_ref, theirs_ref, *refs):
    total = coef_ref[:, 2:3] * ours_ref[...].astype(F32) + coef_ref[:, 3:4] * theirs_ref[...].astype(F32)
    total = total.astype(BF16)
    if first:
        refs[0][...] = total
    refs[-1][...] = total.T


def merge(coef, ours, theirs, turned=None, tile=384):
    tokens, width = ours.shape
    first = turned is None
    steps = width // tile
    tall = pl.BlockSpec((tokens, tile), lambda j: (0, j))
    flat = pl.BlockSpec((tile, tokens), lambda j: (j if first else j + steps, 0))
    in_specs = [pl.BlockSpec(coef.shape, lambda j: (0, 0)), tall, tall]
    args = [coef, ours, theirs]
    out_shape = [jax.ShapeDtypeStruct((2 * width, tokens), BF16)]
    out_specs = [flat]
    if first:
        out_shape.insert(0, jax.ShapeDtypeStruct((tokens, width), BF16))
        out_specs.insert(0, tall)
    else:
        in_specs.append(pl.BlockSpec(memory_space=pl.ANY))
        args.append(turned)
    return pl.pallas_call(
        functools.partial(merge_kernel, first),
        out_shape=out_shape,
        grid=(steps,),
        in_specs=in_specs,
        out_specs=out_specs,
        input_output_aliases={} if first else {3: 0},
        compiler_params=pltpu.CompilerParams(vmem_limit_bytes=32 << 20),
        cost_estimate=pl.CostEstimate(flops=4 * ours.size, bytes_accessed=6 * ours.size, transcendentals=0),
        name="merge_first" if first else "merge_second",
    )(*args)


def blocks_kernel(jobs, turned_ref, mine_ref, *refs):
    width = refs[-1].shape[0]
    for n, out_ref in enumerate(refs[-jobs.shape[0] :]):

        @pl.when(jobs[n, 0] >= 0)
        def _(n=n, out_ref=out_ref):
            down = pl.ds(pl.multiple_of(jobs[n, 0] * width, 128), width)
            along = pl.ds(pl.multiple_of(jobs[n, 1] * width, 128), width)
            block = jnp.dot(turned_ref[down, :], mine_ref[:, along], preferred_element_type=F32)
            out_ref[...] = block.astype(out_ref.dtype)


def moment_blocks(jobs, turned, mine, width, dtype, name, after=()):
    count = jobs.shape[0]
    whole = lambda shape: pl.BlockSpec(shape, lambda i, s: (0, 0))
    return pl.pallas_call(
        blocks_kernel,
        out_shape=[jax.ShapeDtypeStruct((width, width), dtype)] * count,
        grid_spec=pltpu.PrefetchScalarGridSpec(
            num_scalar_prefetch=1,
            grid=(1,),
            in_specs=[whole(turned.shape), whole(mine.shape)] + [pl.BlockSpec(memory_space=pl.ANY)] * len(after),
            out_specs=[whole((width, width))] * count,
        ),
        cost_estimate=pl.CostEstimate(
            flops=2 * count * mine.shape[0] * width * width,
            bytes_accessed=2 * turned.size + 2 * mine.size + count * width * width * 4,
            transcendentals=0,
        ),
        compiler_params=pltpu.CompilerParams(vmem_limit_bytes=40 << 20),
        name=name,
    )(jobs, turned, mine, *after)


def is_diagonal(b, e):
    return b // 4 == e


EXTRA = ((0, 0), (3, 0), (4, 1), (7, 1))


def owned_columns(b, e):
    shift = 0 if is_diagonal(b, e) or e == 1 else 1
    return [(b + shift) % 4, (b + shift + 1) % 4, (b + 2) % 4]


def extra_role(p, e, d):
    for b, core in EXTRA:
        q = SNAKE.index(b)
        if core == e and (q - p) % 8 == d:
            return b, 1
        if core == e and d >= 2 and (p - q) % 8 == d - 1:
            return b, -1
    return None


FIRST = ((0, 4), (0, 5), (1, 4), (1, 3), (2, 4))
SECOND = ((0, 3), (0, 6), (1, 5), (1, 2), (2, 3))
REST = ((0, 2), (0, 7), (1, 6), (1, 1), (2, 2), (0, 1), (1, 7), (2, 1), (0, 0), (1, 0), (2, 0))


def job_table(which):
    table = np.full((8, 2, len(which), 2), -1, np.int32)
    for p, b in enumerate(SNAKE):
        for e in range(2):
            for n, (x, t) in enumerate(which):
                if x < 2:
                    q = SNAKE[(p + t) % 8]
                else:
                    role = extra_role(p, e, t)
                    if role is None:
                        continue
                    q = role[0]
                table[b, e, n] = (q % 4 + (0 if q // 4 == e else 4), owned_columns(q, e)[x])
    return table


def ring_perm(distance, direction):
    pairs = [(SNAKE[p], SNAKE[(p + direction) % 8]) for p in range(8)]
    return [(a * 2 + e, b * 2 + e) for a, b in pairs for e in range(2)]


def extra_perm(d):
    pairs = []
    for p in range(8):
        for e in range(2):
            role = extra_role(p, e, d)
            if role is not None:
                pairs.append((SNAKE[p] * 2 + e, SNAKE[(p + role[1]) % 8] * 2 + e))
    return pairs


def mirror_perms():
    one, other = [], []
    for b in range(8):
        for e in range(2):
            here = b * 2 + e
            if is_diagonal(b, e):
                one.append((here, (b // 4 * 4 + (b + 1) % 4) * 2 + e))
                if (b, e) in EXTRA:
                    other.append((here, (b // 4 * 4 + (b + 2) % 4) * 2 + e))
            elif e == 1:
                other.append((here, (4 + b) * 2))
                one.append((here, (4 + (b + 1) % 4) * 2))
            else:
                other.append((here, (b + 1) % 4 * 2 + 1))
                one.append((here, (b + 2) % 4 * 2 + 1))
    return one, other


def place_table():
    table = np.zeros((8, 2, 6), np.int32)
    for b in range(8):
        for e in range(2):
            own = owned_columns(b, e)
            if is_diagonal(b, e):
                table[b, e] = (own[0], own[1], (b + 3) % 4, (b + 2) % 4, (b, e) in EXTRA, 1)
            elif e == 1:
                table[b, e] = (own[0], own[1], (b + 2) % 4, (b + 3) % 4, 0, 0)
            else:
                table[b, e] = (own[0], own[1], (b + 3) % 4, b % 4, 0, 0)
    return table


def finish_kernel(scale, place, own0, own1, own2, right0, left0, right1, left1, right2, left2, one, other, out_ref):
    width = one.shape[0]

    def put(n, value):
        out_ref[:, pl.ds(pl.multiple_of(place[n] * width, 128), width)] = value

    def owned(own, right, left):
        return (own[...] + right[...].astype(F32) + left[...].astype(F32)) * scale

    put(0, owned(own0, right0, left0))
    put(1, owned(own1, right1, left1))
    put(2, one[...].astype(F32).T)

    @pl.when(place[4] == 1)
    def _():
        put(3, owned(own2, right2, left2))

    @pl.when(place[4] == 0)
    def _():
        put(3, other[...].astype(F32).T)


def symmetric_moment(mine, turned, total_tokens):
    width = mine.shape[1] // 4
    both = ("dp", "expert")
    dp, e = lax.axis_index("dp"), lax.axis_index("expert")
    blocks = {}

    def compute(which, dtype, name, after=()):
        jobs = jnp.asarray(job_table(which))[dp, e]
        blocks.update(zip(which, moment_blocks(jobs, turned, mine, width, dtype, name, after)))

    def send(value, perm):
        return lax.ppermute(value, both, perm)

    def join(value, key):
        return (value.astype(F32) + blocks[key]).astype(BF16)

    compute(FIRST, BF16, "blocks_first")
    right = [send(blocks[0, 4], ring_perm(4, 1)), send(blocks[1, 3], ring_perm(3, 1))]
    left = [send(blocks[0, 5], ring_perm(3, -1)), send(blocks[1, 4], ring_perm(4, -1))]
    extra = send(blocks[2, 4], extra_perm(4))

    compute(SECOND, F32, "blocks_second")
    right = [send(join(right[0], (0, 3)), ring_perm(3, 1)), send(join(right[1], (1, 2)), ring_perm(2, 1))]
    left = [send(join(left[0], (0, 6)), ring_perm(2, -1)), send(join(left[1], (1, 5)), ring_perm(3, -1))]
    extra = send(join(extra, (2, 3)), extra_perm(3))

    compute(REST, F32, "blocks_rest")
    right = [send(join(right[0], (0, 2)), ring_perm(2, 1)), send(join(right[1], (1, 1)), ring_perm(1, 1))]
    left = [send(join(left[0], (0, 7)), ring_perm(1, -1)), send(join(left[1], (1, 6)), ring_perm(2, -1))]
    left2 = send(join(extra, (2, 2)), extra_perm(2))

    right[0] = send(join(right[0], (0, 1)), ring_perm(1, 1))
    left[1] = send(join(left[1], (1, 7)), ring_perm(1, -1))
    right2 = send(join(left2, (2, 1)), extra_perm(1))

    scale = 1.0 / total_tokens
    place = jnp.asarray(place_table())[dp, e]

    def done(x, r, l):
        return blocks[x, 0] + r.astype(F32) + l.astype(F32)

    perm_one, perm_other = mirror_perms()
    other = jnp.where(place[5] == 1, done(2, right2, left2), done(0, right[0], left[0]))
    other = send((other * scale).astype(BF16), perm_other)
    one = send((done(1, right[1], left[1]) * scale).astype(BF16), perm_one)

    block = pl.BlockSpec((width, width), lambda i, s: (0, 0))
    return pl.pallas_call(
        functools.partial(finish_kernel, scale),
        out_shape=jax.ShapeDtypeStruct((width, 4 * width), F32),
        grid_spec=pltpu.PrefetchScalarGridSpec(
            num_scalar_prefetch=1,
            grid=(1,),
            in_specs=[block] * 11,
            out_specs=pl.BlockSpec((width, 4 * width), lambda i, s: (0, 0)),
        ),
        compiler_params=pltpu.CompilerParams(vmem_limit_bytes=32 << 20),
        name="finish",
    )(
        place,
        *[blocks[x, 0] for x in range(3)],
        right[0],
        left[0],
        right[1],
        left[1],
        right2,
        left2,
        one,
        other,
    )


def per_device(expert_ids, gates, expert_out):
    tokens, channels = expert_ids.shape[0], expert_out.shape[1]
    dp_size = lax.axis_size("dp")
    member = lax.axis_index("expert")
    half = channels // 2
    swap = [(0, 1), (1, 0)]

    pick, starts, coef = plan(expert_ids, gates, member)
    mine, theirs = [], []
    for column_half in (1 - member, member):
        where_ = jnp.stack([column_half, member]).astype(I32)
        mine.append(pick_half(where_, starts, pick, coef, expert_out, half))
        theirs.append(lax.ppermute(mine[-1], "expert", swap))
    rows, turned = merge(coef, mine[1], theirs[0])
    (turned,) = merge(coef, mine[0], theirs[1], turned)

    total_tokens = tokens * dp_size
    if dp_size == 8 and channels == 8 * 384:
        return symmetric_moment(rows, turned, total_tokens)
    slab = jnp.dot(turned, rows, preferred_element_type=F32)
    slab = jnp.where(member == 0, slab, jnp.roll(slab, half, axis=0))
    return lax.psum_scatter(slab, "dp", scatter_dimension=0, tiled=True) / total_tokens


def solution(mesh):
    assert mesh.shape["expert"] == 2
    in_specs = (
        P(("groups", "dp"), None),
        P(("groups", "dp"), None),
        P(("groups", "dp", "expert"), None),
    )
    out_specs = P(("groups", "dp"), "expert")
    return jax.shard_map(
        per_device, mesh=mesh, in_specs=in_specs, out_specs=out_specs, check_vma=False
    )
```

```python
import functools

import jax
import jax.numpy as jnp
import numpy as np
from jax import lax
from jax.experimental import pallas as pl
from jax.experimental.pallas import tpu as pltpu
from jax.sharding import PartitionSpec as P

EXPERTS = 8
CAP = 384
BATCH = 96
WINDOW = 128
SNAKE = (0, 2, 4, 6, 7, 5, 3, 1)
F32, BF16, I32 = jnp.float32, jnp.bfloat16, jnp.int32


def plan_kernel(member, ids_ref, gates_ref, pick_ref, starts_ref, coef_ref):
    tokens = ids_ref.shape[0]
    local = EXPERTS // 2
    lanes = lax.broadcasted_iota(I32, (tokens, 128), 1)
    ids = [ids_ref[:, k : k + 1] for k in range(2)]
    hits = [ids[k] == lanes for k in range(2)]
    named = jnp.where(hits[0] | hits[1], 1.0, 0.0).astype(BF16)
    earlier = jnp.where(
        lax.broadcasted_iota(I32, (tokens, tokens), 1) < lax.broadcasted_iota(I32, (tokens, tokens), 0), 1.0, 0.0
    ).astype(BF16)
    before = jnp.dot(earlier, named, preferred_element_type=F32)

    slots = [ids[k] - member[0] * local for k in range(2)]
    here = [jnp.where((slots[k] >= 0) & (slots[k] < local), 1.0, 0.0) for k in range(2)]
    gates = [gates_ref[:, k : k + 1] for k in range(2)]
    both = here[0] * here[1]
    neither = (1.0 - here[0]) * (1.0 - here[1])
    mixed = 1.0 - both - neither
    weights = [here[k] * jnp.where(both > 0.5, gates[k], 1.0) for k in range(2)]
    ours = here[0] * gates[0] + here[1] * gates[1]
    theirs = (1.0 - here[0]) * gates[0] + (1.0 - here[1]) * gates[1]
    ours = jnp.where(mixed > 0.5, ours, both)
    theirs = jnp.where(mixed > 0.5, theirs, neither)
    coef_ref[...] = jnp.where(
        lanes == 0, weights[0], jnp.where(lanes == 1, weights[1], jnp.where(lanes == 2, ours, theirs))
    )

    columns = lax.broadcasted_iota(I32, (BATCH, local * WINDOW), 1)
    for b in range(tokens // BATCH):
        rows = slice(b * BATCH, (b + 1) * BATCH)
        start = before[b * BATCH : b * BATCH + 1, :].astype(I32)
        start = jnp.minimum((start >> 4) << 4, CAP - WINDOW)
        starts_ref[b : b + 1, :] = start
        ahead = before[rows] - start.astype(F32)
        for k in range(2):
            offset = jnp.sum(jnp.where(hits[k][rows], ahead, 0.0), axis=1, keepdims=True).astype(I32)
            at = jnp.where(here[k][rows] > 0.5, slots[k][rows] * WINDOW + offset, -1)
            pick_ref[(2 * b + k) * BATCH : (2 * b + k + 1) * BATCH, :] = jnp.where(columns == at, 1.0, 0.0).astype(BF16)


def plan(ids, gates, member):
    tokens = ids.shape[0]
    whole = lambda shape: pl.BlockSpec(shape, lambda i, s: (0, 0))
    shapes = [((2 * tokens, EXPERTS // 2 * WINDOW), BF16), ((tokens // BATCH, 128), I32), ((tokens, 128), F32)]
    return pl.pallas_call(
        plan_kernel,
        out_shape=[jax.ShapeDtypeStruct(*s) for s in shapes],
        grid_spec=pltpu.PrefetchScalarGridSpec(
            num_scalar_prefetch=1,
            grid=(1,),
            in_specs=[whole(ids.shape), whole(gates.shape)],
            out_specs=[whole(s[0]) for s in shapes],
        ),
        compiler_params=pltpu.CompilerParams(vmem_limit_bytes=32 << 20),
        name="plan",
    )(member.reshape(1).astype(I32), ids, gates)


def pick_kernel(where_, starts, pick_ref, coef_ref, rows_ref, out_ref):
    local = EXPERTS // 2
    for b in range(out_ref.shape[0] // BATCH):
        windows = []
        for k in range(local):
            first = k * CAP + starts[b, where_[1] * local + k]
            windows.append(rows_ref[pl.ds(pl.multiple_of(first, 16), WINDOW), :])
        picked = jnp.dot(
            pick_ref[2 * b * BATCH : 2 * (b + 1) * BATCH, :],
            jnp.concatenate(windows, axis=0),
            preferred_element_type=F32,
        )
        rows = slice(b * BATCH, (b + 1) * BATCH)
        total = coef_ref[rows, 0:1] * picked[:BATCH] + coef_ref[rows, 1:2] * picked[BATCH:]
        out_ref[rows, :] = total.astype(BF16)


def pick_half(where_, starts, pick, coef, rows, width, tile=512):
    tokens = coef.shape[0]
    steps = width // tile
    whole = lambda shape: pl.BlockSpec(shape, lambda j, w, s: (0, 0))
    return pl.pallas_call(
        pick_kernel,
        out_shape=jax.ShapeDtypeStruct((tokens, width), BF16),
        grid_spec=pltpu.PrefetchScalarGridSpec(
            num_scalar_prefetch=2,
            grid=(steps,),
            in_specs=[
                whole(pick.shape),
                whole(coef.shape),
                pl.BlockSpec((rows.shape[0], tile), lambda j, w, s: (0, w[0] * steps + j)),
            ],
            out_specs=pl.BlockSpec((tokens, tile), lambda j, w, s: (0, j)),
        ),
        cost_estimate=pl.CostEstimate(
            flops=2 * pick.size * width, bytes_accessed=2 * (rows.shape[0] + tokens) * width, transcendentals=0
        ),
        compiler_params=pltpu.CompilerParams(vmem_limit_bytes=60 << 20),
        name="pick",
    )(where_, starts, pick, coef, rows)


def merge_kernel(first, coef_ref, ours_ref, theirs_ref, *refs):
    total = coef_ref[:, 2:3] * ours_ref[...].astype(F32) + coef_ref[:, 3:4] * theirs_ref[...].astype(F32)
    total = total.astype(BF16)
    if first:
        refs[0][...] = total
    refs[-1][...] = total.T


def merge(coef, ours, theirs, turned=None, tile=384):
    tokens, width = ours.shape
    first = turned is None
    steps = width // tile
    tall = pl.BlockSpec((tokens, tile), lambda j: (0, j))
    flat = pl.BlockSpec((tile, tokens), lambda j: (j if first else j + steps, 0))
    in_specs = [pl.BlockSpec(coef.shape, lambda j: (0, 0)), tall, tall]
    args = [coef, ours, theirs]
    out_shape = [jax.ShapeDtypeStruct((2 * width, tokens), BF16)]
    out_specs = [flat]
    if first:
        out_shape.insert(0, jax.ShapeDtypeStruct((tokens, width), BF16))
        out_specs.insert(0, tall)
    else:
        in_specs.append(pl.BlockSpec(memory_space=pl.ANY))
        args.append(turned)
    return pl.pallas_call(
        functools.partial(merge_kernel, first),
        out_shape=out_shape,
        grid=(steps,),
        in_specs=in_specs,
        out_specs=out_specs,
        input_output_aliases={} if first else {3: 0},
        compiler_params=pltpu.CompilerParams(vmem_limit_bytes=32 << 20),
        cost_estimate=pl.CostEstimate(flops=4 * ours.size, bytes_accessed=6 * ours.size, transcendentals=0),
        name="merge_first" if first else "merge_second",
    )(*args)


def blocks_kernel(jobs, turned_ref, mine_ref, *refs):
    tall, width = refs[-1].shape
    strip = tall - width
    for n, out_ref in enumerate(refs[-jobs.shape[0] :]):
        parts = ((0, width, width), (width, strip, strip))
        for k, (at, rows, unit) in enumerate(parts):

            @pl.when(jobs[n, 2 * k] >= 0)
            def _(n=n, k=k, out_ref=out_ref, at=at, rows=rows, unit=unit):
                down = pl.ds(pl.multiple_of(jobs[n, 2 * k] * unit, 32), rows)
                along = pl.ds(pl.multiple_of(jobs[n, 2 * k + 1] * width, 128), width)
                block = jnp.dot(turned_ref[down, :], mine_ref[:, along], preferred_element_type=F32)
                out_ref[at : at + rows, :] = block.astype(out_ref.dtype)

        @pl.when(jobs[n, 2] < 0)
        def _(out_ref=out_ref):
            out_ref[width:, :] = jnp.zeros((strip, width), out_ref.dtype)


def moment_blocks(jobs, turned, mine, width, strip, dtype, name, after=()):
    count = jobs.shape[0]
    whole = lambda shape: pl.BlockSpec(shape, lambda i, s: (0, 0))
    piece = (width + strip, width)
    return pl.pallas_call(
        blocks_kernel,
        out_shape=[jax.ShapeDtypeStruct(piece, dtype)] * count,
        grid_spec=pltpu.PrefetchScalarGridSpec(
            num_scalar_prefetch=1,
            grid=(1,),
            in_specs=[whole(turned.shape), whole(mine.shape)] + [pl.BlockSpec(memory_space=pl.ANY)] * len(after),
            out_specs=[whole(piece)] * count,
        ),
        cost_estimate=pl.CostEstimate(
            flops=2 * count * mine.shape[0] * width * width,
            bytes_accessed=2 * turned.size + 2 * mine.size + count * width * width * 4,
            transcendentals=0,
        ),
        compiler_params=pltpu.CompilerParams(vmem_limit_bytes=40 << 20),
        name=name,
    )(jobs, turned, mine, *after)


STRIP = 96


def is_diagonal(b, e):
    return b // 4 == e


def owned_columns(b, e):
    shift = 0 if is_diagonal(b, e) or e == 1 else 1
    return [(b + shift) % 4, (b + shift + 1) % 4]


def leads(b):
    return b % 4 < 2


ROUNDS = (
    ((0, 4), (1, 4), (1, 3), (0, 5)),
    ((0, 3), (1, 5), (1, 2), (0, 6)),
    ((0, 2), (1, 6), (1, 1), (0, 7)),
    ((0, 1), (1, 7), (0, 0), (1, 0)),
)


def job_table(which, width):
    table = np.full((8, 2, len(which), 4), -1, np.int32)
    for p, b in enumerate(SNAKE):
        for e in range(2):
            for n, (x, t) in enumerate(which):
                q = SNAKE[(p + t) % 8]
                table[b, e, n, :2] = (q % 4 + (0 if q // 4 == e else 4), owned_columns(q, e)[x])
                if is_diagonal(q, e):
                    lead, other = (q % 4, (q + 2) % 4) if leads(q) else ((q + 2) % 4, q % 4)
                    first = lead * width + (0 if leads(q) else width // 2) + x * STRIP
                    table[b, e, n, 2:] = (first // STRIP, other)
    return table


def ring_perm(direction):
    pairs = [(SNAKE[p], SNAKE[(p + direction) % 8]) for p in range(8)]
    return [(a * 2 + e, b * 2 + e) for a, b in pairs for e in range(2)]


def mirror_perms():
    one, other = [], []
    for b in range(8):
        for e in range(2):
            here = b * 2 + e
            if is_diagonal(b, e):
                one.append((here, (b // 4 * 4 + (b + 1) % 4) * 2 + e))
                other.append((here, (b // 4 * 4 + (b + 2) % 4) * 2 + e))
            elif e == 1:
                other.append((here, (4 + b) * 2))
                one.append((here, (4 + (b + 1) % 4) * 2))
            else:
                other.append((here, (b + 1) % 4 * 2 + 1))
                one.append((here, (b + 2) % 4 * 2 + 1))
    return one, other


def place_table():
    table = np.zeros((8, 2, 5), np.int32)
    for b in range(8):
        for e in range(2):
            own = owned_columns(b, e)
            if is_diagonal(b, e):
                table[b, e] = (own[0], own[1], (b + 3) % 4, (b + 2) % 4, 1 if leads(b) else 2)
            elif e == 1:
                table[b, e] = (own[0], own[1], (b + 2) % 4, (b + 3) % 4, 0)
            else:
                table[b, e] = (own[0], own[1], (b + 3) % 4, b % 4, 0)
    return table


def finish_kernel(scale, place, own0, own1, right0, left0, right1, left1, one, other, out_ref):
    width = one.shape[0]

    def put(n, value):
        out_ref[:, pl.ds(pl.multiple_of(place[n] * width, 128), width)] = value

    def owned(own, right, left, rows):
        return (own[rows, :] + right[rows, :].astype(F32) + left[rows, :].astype(F32)) * scale

    put(0, owned(own0, right0, left0, slice(0, width)))
    put(1, owned(own1, right1, left1, slice(0, width)))
    put(2, one[...].astype(F32).T)

    def share():
        rows = slice(width, width + STRIP)
        return [owned(own0, right0, left0, rows), owned(own1, right1, left1, rows)]

    @pl.when(place[4] == 0)
    def _():
        put(3, other[...].astype(F32).T)

    @pl.when(place[4] == 1)
    def _():
        put(3, jnp.concatenate(share() + [other[: width // 2, :].astype(F32)], axis=0))

    @pl.when(place[4] == 2)
    def _():
        put(3, jnp.concatenate([other[: width // 2, :].astype(F32)] + share(), axis=0).T)


def symmetric_moment(mine, turned, total_tokens):
    width = mine.shape[1] // 4
    both = ("dp", "expert")
    dp, e = lax.axis_index("dp"), lax.axis_index("expert")
    blocks = {}

    def compute(n, dtype, after=()):
        which = ROUNDS[n]
        jobs = jnp.asarray(job_table(which, width))[dp, e]
        blocks.update(zip(which, moment_blocks(jobs, turned, mine, width, STRIP, dtype, f"blocks{n}", after)))

    def hop(value, key):
        return lax.ppermute(value, both, ring_perm(1 if key[1] <= (4 if key[0] == 0 else 3) else -1))

    compute(0, BF16)
    moving = {key: blocks[key] for key in ROUNDS[0]}
    arrived = {}
    for n in range(4):
        landed = {}
        for key in ROUNDS[n]:
            if key in moving:
                landed[key] = hop(moving[key], key)
        if n < 3:
            compute(n + 1, F32, after=(landed[ROUNDS[n][0]],))
        moving = {}
        for (x, t), value in landed.items():
            rightwards = t <= (4 if x == 0 else 3)
            t = t - 1 if rightwards else (t + 1) % 8
            if t == 0:
                arrived[x, rightwards] = value
            else:
                moving[x, t] = (value.astype(F32) + blocks[x, t]).astype(BF16)

    scale = 1.0 / total_tokens
    place = jnp.asarray(place_table())[dp, e]

    def done(x, rows):
        pieces = (blocks[x, 0], arrived[x, True], arrived[x, False])
        return sum(piece[rows].astype(F32) for piece in pieces) * scale

    perm_one, perm_other = mirror_perms()
    own, share = slice(0, width), slice(width, width + STRIP)
    third = jnp.concatenate([done(0, share), done(1, share), jnp.zeros((width // 2, width), F32)], axis=0)
    other = jnp.where(place[4] > 0, third, done(0, own))
    one = lax.ppermute(done(1, own).astype(BF16), both, perm_one)
    other = lax.ppermute(other.astype(BF16), both, perm_other)

    piece = pl.BlockSpec((width + STRIP, width), lambda i, s: (0, 0))
    block = pl.BlockSpec((width, width), lambda i, s: (0, 0))
    return pl.pallas_call(
        functools.partial(finish_kernel, scale),
        out_shape=jax.ShapeDtypeStruct((width, 4 * width), F32),
        grid_spec=pltpu.PrefetchScalarGridSpec(
            num_scalar_prefetch=1,
            grid=(1,),
            in_specs=[piece] * 6 + [block] * 2,
            out_specs=pl.BlockSpec((width, 4 * width), lambda i, s: (0, 0)),
        ),
        compiler_params=pltpu.CompilerParams(vmem_limit_bytes=32 << 20),
        name="finish",
    )(
        place,
        blocks[0, 0],
        blocks[1, 0],
        arrived[0, True],
        arrived[0, False],
        arrived[1, True],
        arrived[1, False],
        one,
        other,
    )


def per_device(expert_ids, gates, expert_out):
    tokens, channels = expert_ids.shape[0], expert_out.shape[1]
    dp_size = lax.axis_size("dp")
    member = lax.axis_index("expert")
    half = channels // 2
    swap = [(0, 1), (1, 0)]

    pick, starts, coef = plan(expert_ids, gates, member)
    mine, theirs = [], []
    for column_half in (1 - member, member):
        where_ = jnp.stack([column_half, member]).astype(I32)
        mine.append(pick_half(where_, starts, pick, coef, expert_out, half))
        theirs.append(lax.ppermute(mine[-1], "expert", swap))
    rows, turned = merge(coef, mine[1], theirs[0])
    (turned,) = merge(coef, mine[0], theirs[1], turned)

    total_tokens = tokens * dp_size
    if dp_size == 8 and channels == 8 * 384:
        return symmetric_moment(rows, turned, total_tokens)
    slab = jnp.dot(turned, rows, preferred_element_type=F32)
    slab = jnp.where(member == 0, slab, jnp.roll(slab, half, axis=0))
    return lax.psum_scatter(slab, "dp", scatter_dimension=0, tiled=True) / total_tokens


def solution(mesh):
    assert mesh.shape["expert"] == 2
    in_specs = (
        P(("groups", "dp"), None),
        P(("groups", "dp"), None),
        P(("groups", "dp", "expert"), None),
    )
    out_specs = P(("groups", "dp"), "expert")
    return jax.shard_map(
        per_device, mesh=mesh, in_specs=in_specs, out_specs=out_specs, check_vma=False
    )
```

```python
import functools

import jax
import jax.numpy as jnp
import numpy as np
from jax import lax
from jax.experimental import pallas as pl
from jax.experimental.pallas import tpu as pltpu
from jax.sharding import PartitionSpec as P

EXPERTS = 8
CAP = 384
BATCH = 96
WINDOW = 128
SNAKE = (0, 2, 4, 6, 7, 5, 3, 1)
F32, BF16, I32 = jnp.float32, jnp.bfloat16, jnp.int32


def plan_tokens(ids_ref, gates_ref, pick_ref, starts_ref, coef_ref):
    tokens = ids_ref.shape[1]
    local = EXPERTS // 2
    lanes = lax.broadcasted_iota(I32, (tokens, 128), 1)
    rows = jnp.concatenate([ids_ref[...].astype(F32), gates_ref[...], jnp.zeros((4, tokens), F32)], axis=0).T
    ids = [rows[:, k : k + 1].astype(I32) for k in range(2)]
    gates = [rows[:, k : k + 1] for k in (2, 3)]
    hits = [ids[k] == lanes for k in range(2)]
    named = jnp.where(hits[0] | hits[1], 1.0, 0.0).astype(BF16)
    earlier = jnp.where(
        lax.broadcasted_iota(I32, (tokens, tokens), 1) < lax.broadcasted_iota(I32, (tokens, tokens), 0), 1.0, 0.0
    ).astype(BF16)
    before = jnp.dot(earlier, named, preferred_element_type=F32)

    slots = [ids[k] - lax.axis_index("expert") * local for k in range(2)]
    here = [jnp.where((slots[k] >= 0) & (slots[k] < local), 1.0, 0.0) for k in range(2)]
    both = here[0] * here[1]
    neither = (1.0 - here[0]) * (1.0 - here[1])
    mixed = 1.0 - both - neither
    weights = [here[k] * jnp.where(both > 0.5, gates[k], 1.0) for k in range(2)]
    ours = here[0] * gates[0] + here[1] * gates[1]
    theirs = (1.0 - here[0]) * gates[0] + (1.0 - here[1]) * gates[1]
    ours = jnp.where(mixed > 0.5, ours, both)
    theirs = jnp.where(mixed > 0.5, theirs, neither)
    coef_ref[...] = jnp.where(
        lanes == 0, weights[0], jnp.where(lanes == 1, weights[1], jnp.where(lanes == 2, ours, theirs))
    )

    columns = lax.broadcasted_iota(I32, (BATCH, local * WINDOW), 1)
    for b in range(tokens // BATCH):
        rows = slice(b * BATCH, (b + 1) * BATCH)
        start = before[b * BATCH : b * BATCH + 1, :].astype(I32)
        start = jnp.minimum((start >> 4) << 4, CAP - WINDOW)
        starts_ref[b : b + 1, :] = start
        ahead = before[rows] - start.astype(F32)
        for k in range(2):
            offset = jnp.sum(jnp.where(hits[k][rows], ahead, 0.0), axis=1, keepdims=True).astype(I32)
            at = jnp.where(here[k][rows] > 0.5, slots[k][rows] * WINDOW + offset, -1)
            pick_ref[(2 * b + k) * BATCH : (2 * b + k + 1) * BATCH, :] = jnp.where(columns == at, 1.0, 0.0).astype(BF16)


def pick_kernel(first, *refs):
    if first:
        ids_ref, gates_ref, rows_ref, out_ref, pick_ref, starts_ref, coef_ref = refs[:7]
        held, made, in_sems, out_sems, starts, starts_sem = refs[7:]
    else:
        starts, pick_ref, coef_ref, rows_ref, out_ref, held, made, in_sems, out_sems = refs
    tokens, width = out_ref.shape
    tiles, _, tile = held.shape
    local = EXPERTS // 2
    member = lax.axis_index("expert")
    base = (1 - member if first else member) * width

    loads = []
    for j in range(tiles):
        at = pl.ds(pl.multiple_of(base + j * tile, 128), tile)
        loads.append(pltpu.make_async_copy(rows_ref.at[:, at], held.at[j], in_sems.at[j]))
        loads[-1].start()
    if first:
        plan_tokens(ids_ref, gates_ref, pick_ref, starts_ref, coef_ref)
        copy = pltpu.make_async_copy(starts_ref, starts, starts_sem)
        copy.start()
        copy.wait()
    stores = []
    for j in range(tiles):
        loads[j].wait()
        for b in range(tokens // BATCH):
            windows = []
            for k in range(local):
                at = k * CAP + starts[b, member * local + k]
                windows.append(held[j, pl.ds(pl.multiple_of(at, 16), WINDOW), :])
            picked = jnp.dot(
                pick_ref[2 * b * BATCH : 2 * (b + 1) * BATCH, :],
                jnp.concatenate(windows, axis=0),
                preferred_element_type=F32,
            )
            rows = slice(b * BATCH, (b + 1) * BATCH)
            total = coef_ref[rows, 0:1] * picked[:BATCH] + coef_ref[rows, 1:2] * picked[BATCH:]
            made[j, rows, :] = total.astype(BF16)
        stores.append(
            pltpu.make_async_copy(made.at[j], out_ref.at[:, j * tile : (j + 1) * tile], out_sems.at[j])
        )
        stores[-1].start()
    for store in stores:
        store.wait()


def pick_half(args, rows, tokens, width, first, tile=512):
    tiles = width // tile
    depth = EXPERTS // 2 * WINDOW
    any_, vmem = pl.BlockSpec(memory_space=pl.ANY), pl.BlockSpec(memory_space=pltpu.VMEM)
    out_shape = [jax.ShapeDtypeStruct((tokens, width), BF16)]
    scratch = [
        pltpu.VMEM((tiles, rows.shape[0], tile), BF16),
        pltpu.VMEM((tiles, tokens, tile), BF16),
        pltpu.SemaphoreType.DMA((tiles,)),
        pltpu.SemaphoreType.DMA((tiles,)),
    ]
    if first:
        out_shape += [
            jax.ShapeDtypeStruct((2 * tokens, depth), BF16),
            jax.ShapeDtypeStruct((tokens // BATCH, 128), I32),
            jax.ShapeDtypeStruct((tokens, 128), F32),
        ]
        in_specs = [vmem, vmem, any_]
        scratch += [pltpu.SMEM((tokens // BATCH, 128), I32), pltpu.SemaphoreType.DMA]
    else:
        in_specs = [pl.BlockSpec(memory_space=pltpu.SMEM), vmem, vmem, any_]
    return pl.pallas_call(
        functools.partial(pick_kernel, first),
        out_shape=out_shape,
        in_specs=in_specs,
        out_specs=[any_] + [vmem] * (len(out_shape) - 1),
        scratch_shapes=scratch,
        cost_estimate=pl.CostEstimate(
            flops=4 * tokens * depth * width, bytes_accessed=2 * (rows.shape[0] + tokens) * width, transcendentals=0
        ),
        compiler_params=pltpu.CompilerParams(vmem_limit_bytes=56 << 20),
        name="pick_first" if first else "pick_second",
    )(*args, rows)


def merge_kernel(first, coef_ref, ours_ref, theirs_ref, *refs):
    total = coef_ref[:, 2:3] * ours_ref[...].astype(F32) + coef_ref[:, 3:4] * theirs_ref[...].astype(F32)
    total = total.astype(BF16)
    if first:
        refs[0][...] = total
    refs[-1][...] = total.T


def merge(coef, ours, theirs, turned=None, tile=384):
    tokens, width = ours.shape
    first = turned is None
    steps = width // tile
    tall = pl.BlockSpec((tokens, tile), lambda j: (0, j))
    flat = pl.BlockSpec((tile, tokens), lambda j: (j if first else j + steps, 0))
    in_specs = [pl.BlockSpec(coef.shape, lambda j: (0, 0)), tall, tall]
    args = [coef, ours, theirs]
    out_shape = [jax.ShapeDtypeStruct((2 * width, tokens), BF16)]
    out_specs = [flat]
    if first:
        out_shape.insert(0, jax.ShapeDtypeStruct((tokens, width), BF16))
        out_specs.insert(0, tall)
    else:
        in_specs.append(pl.BlockSpec(memory_space=pl.ANY))
        args.append(turned)
    return pl.pallas_call(
        functools.partial(merge_kernel, first),
        out_shape=out_shape,
        grid=(steps,),
        in_specs=in_specs,
        out_specs=out_specs,
        input_output_aliases={} if first else {3: 0},
        compiler_params=pltpu.CompilerParams(vmem_limit_bytes=32 << 20),
        cost_estimate=pl.CostEstimate(flops=4 * ours.size, bytes_accessed=6 * ours.size, transcendentals=0),
        name="merge_first" if first else "merge_second",
    )(*args)


def my_row():
    return lax.axis_index("dp") * 2 + lax.axis_index("expert")


def blocks_kernel(count, table, turned_ref, mine_ref, *refs):
    tall, width = refs[-1].shape
    strip = tall - width
    me = my_row()
    for n, out_ref in enumerate(refs[-count:]):
        jobs = [table[me, 4 * n + k] for k in range(4)]
        parts = ((0, width, width), (width, strip, strip))
        for k, (at, rows, unit) in enumerate(parts):

            @pl.when(jobs[2 * k] >= 0)
            def _(jobs=jobs, k=k, out_ref=out_ref, at=at, rows=rows, unit=unit):
                down = pl.ds(pl.multiple_of(jobs[2 * k] * unit, 32), rows)
                along = pl.ds(pl.multiple_of(jobs[2 * k + 1] * width, 128), width)
                block = jnp.dot(turned_ref[down, :], mine_ref[:, along], preferred_element_type=F32)
                out_ref[at : at + rows, :] = block.astype(out_ref.dtype)

        @pl.when(jobs[2] < 0)
        def _(out_ref=out_ref):
            out_ref[width:, :] = jnp.zeros((strip, width), out_ref.dtype)


def moment_blocks(table, turned, mine, width, strip, dtype, name, after=()):
    count = table.shape[1] // 4
    whole = lambda shape: pl.BlockSpec(shape, lambda i, s: (0, 0))
    piece = (width + strip, width)
    return pl.pallas_call(
        functools.partial(blocks_kernel, count),
        out_shape=[jax.ShapeDtypeStruct(piece, dtype)] * count,
        grid_spec=pltpu.PrefetchScalarGridSpec(
            num_scalar_prefetch=1,
            grid=(1,),
            in_specs=[whole(turned.shape), whole(mine.shape)] + [pl.BlockSpec(memory_space=pl.ANY)] * len(after),
            out_specs=[whole(piece)] * count,
        ),
        cost_estimate=pl.CostEstimate(
            flops=2 * count * mine.shape[0] * width * width,
            bytes_accessed=2 * turned.size + 2 * mine.size + count * width * width * 4,
            transcendentals=0,
        ),
        compiler_params=pltpu.CompilerParams(vmem_limit_bytes=40 << 20),
        name=name,
    )(table, turned, mine, *after)


STRIP = 96


def is_diagonal(b, e):
    return b // 4 == e


def owned_columns(b, e):
    shift = 0 if is_diagonal(b, e) or e == 1 else 1
    return [(b + shift) % 4, (b + shift + 1) % 4]


def leads(b):
    return b % 4 < 2


ROUNDS = (
    ((0, 4), (1, 4), (1, 3), (0, 5)),
    ((0, 3), (1, 5), (1, 2), (0, 6)),
    ((0, 2), (1, 6), (1, 1), (0, 7)),
    ((0, 1), (1, 7), (0, 0), (1, 0)),
)


def job_table(which, width):
    table = np.full((8, 2, len(which), 4), -1, np.int32)
    for p, b in enumerate(SNAKE):
        for e in range(2):
            for n, (x, t) in enumerate(which):
                q = SNAKE[(p + t) % 8]
                table[b, e, n, :2] = (q % 4 + (0 if q // 4 == e else 4), owned_columns(q, e)[x])
                if is_diagonal(q, e):
                    lead, other = (q % 4, (q + 2) % 4) if leads(q) else ((q + 2) % 4, q % 4)
                    first = lead * width + (0 if leads(q) else width // 2) + x * STRIP
                    table[b, e, n, 2:] = (first // STRIP, other)
    return table.reshape(16, -1)


def ring_perm(direction):
    pairs = [(SNAKE[p], SNAKE[(p + direction) % 8]) for p in range(8)]
    return [(a * 2 + e, b * 2 + e) for a, b in pairs for e in range(2)]


def mirror_perms():
    one, other = [], []
    for b in range(8):
        for e in range(2):
            here = b * 2 + e
            if is_diagonal(b, e):
                one.append((here, (b // 4 * 4 + (b + 1) % 4) * 2 + e))
                other.append((here, (b // 4 * 4 + (b + 2) % 4) * 2 + e))
            elif e == 1:
                other.append((here, (4 + b) * 2))
                one.append((here, (4 + (b + 1) % 4) * 2))
            else:
                other.append((here, (b + 1) % 4 * 2 + 1))
                one.append((here, (b + 2) % 4 * 2 + 1))
    return one, other


def place_table():
    table = np.zeros((8, 2, 5), np.int32)
    for b in range(8):
        for e in range(2):
            own = owned_columns(b, e)
            if is_diagonal(b, e):
                table[b, e] = (own[0], own[1], (b + 3) % 4, (b + 2) % 4, 1 if leads(b) else 2)
            elif e == 1:
                table[b, e] = (own[0], own[1], (b + 2) % 4, (b + 3) % 4, 0)
            else:
                table[b, e] = (own[0], own[1], (b + 3) % 4, b % 4, 0)
    return table


def total_kernel(scale, place, own0, own1, right0, left0, right1, left1, out_ref, one, other, share, made, sems):
    width = one.shape[0]
    me = my_row()

    def total(own, right, left, rows):
        return (own[rows, :] + right[rows, :].astype(F32) + left[rows, :].astype(F32)) * scale

    block, strip = slice(0, width), slice(width, width + STRIP)
    made[0] = total(own0, right0, left0, block)
    made[1] = total(own1, right1, left1, block)
    copies = []
    for n in range(2):
        at = pl.ds(pl.multiple_of(place[me, n] * width, 128), width)
        copies.append(pltpu.make_async_copy(made.at[n], out_ref.at[:, at], sems.at[n]))
        copies[-1].start()
    one[...] = made[1].astype(BF16)
    share[:STRIP, :] = total(own0, right0, left0, strip)
    share[STRIP:, :] = total(own1, right1, left1, strip)

    @pl.when(place[me, 4] == 0)
    def _():
        other[...] = made[0].astype(BF16)

    @pl.when(place[me, 4] > 0)
    def _():
        other[: width // 2, :] = share[...].astype(BF16)
        other[width // 2 :, :] = jnp.zeros((width - width // 2, width), BF16)

    for copy in copies:
        copy.wait()


def mirror_kernel(place, share, one, other, result_ref, out_ref, made, sems):
    width = one.shape[0]
    me = my_row()
    made[0] = one[...].astype(F32).T
    copies = []
    for n in range(2):
        at = pl.ds(pl.multiple_of(place[me, 2 + n] * width, 128), width)
        copies.append(pltpu.make_async_copy(made.at[n], out_ref.at[:, at], sems.at[n]))
    copies[0].start()

    @pl.when(place[me, 4] == 0)
    def _():
        made[1] = other[...].astype(F32).T

    @pl.when(place[me, 4] == 1)
    def _():
        made[1, : width // 2, :] = share[...]
        made[1, width // 2 :, :] = other[: width // 2, :].astype(F32)

    @pl.when(place[me, 4] == 2)
    def _():
        made[1] = jnp.concatenate([other[: width // 2, :].astype(F32), share[...]], axis=0).T

    copies[1].start()
    for copy in copies:
        copy.wait()


def symmetric_moment(mine, turned, total_tokens):
    width = mine.shape[1] // 4
    both = ("dp", "expert")
    blocks = {}

    def compute(n, dtype, after=()):
        which = ROUNDS[n]
        table = jnp.asarray(job_table(which, width))
        blocks.update(zip(which, moment_blocks(table, turned, mine, width, STRIP, dtype, f"blocks{n}", after)))

    def hop(value, key):
        return lax.ppermute(value, both, ring_perm(1 if key[1] <= (4 if key[0] == 0 else 3) else -1))

    compute(0, BF16)
    moving = {key: blocks[key] for key in ROUNDS[0]}
    arrived = {}
    for n in range(4):
        landed = {}
        for key in ROUNDS[n]:
            if key in moving:
                landed[key] = hop(moving[key], key)
        if n < 3:
            compute(n + 1, F32, after=(landed[ROUNDS[n][0]],))
        moving = {}
        for (x, t), value in landed.items():
            rightwards = t <= (4 if x == 0 else 3)
            t = t - 1 if rightwards else (t + 1) % 8
            if t == 0:
                arrived[x, rightwards] = value
            else:
                moving[x, t] = (value.astype(F32) + blocks[x, t]).astype(BF16)

    place = jnp.asarray(place_table().reshape(16, -1))
    smem, vmem, any_ = [pl.BlockSpec(memory_space=m) for m in (pltpu.SMEM, pltpu.VMEM, pl.ANY)]
    scratch = [pltpu.VMEM((2, width, width), F32), pltpu.SemaphoreType.DMA((2,))]
    block = jax.ShapeDtypeStruct((width, width), BF16)
    result = jax.ShapeDtypeStruct((width, 4 * width), F32)
    result, one, other, share = pl.pallas_call(
        functools.partial(total_kernel, 1.0 / total_tokens),
        out_shape=[result, block, block, jax.ShapeDtypeStruct((2 * STRIP, width), F32)],
        in_specs=[smem] + [vmem] * 6,
        out_specs=[any_, vmem, vmem, vmem],
        scratch_shapes=scratch,
        compiler_params=pltpu.CompilerParams(vmem_limit_bytes=32 << 20),
        name="total",
    )(
        place,
        blocks[0, 0],
        blocks[1, 0],
        arrived[0, True],
        arrived[0, False],
        arrived[1, True],
        arrived[1, False],
    )
    perm_one, perm_other = mirror_perms()
    other = lax.ppermute(other, both, perm_other)
    one = lax.ppermute(one, both, perm_one)
    return pl.pallas_call(
        mirror_kernel,
        out_shape=jax.ShapeDtypeStruct((width, 4 * width), F32),
        in_specs=[smem, vmem, vmem, vmem, any_],
        out_specs=any_,
        scratch_shapes=scratch,
        input_output_aliases={4: 0},
        compiler_params=pltpu.CompilerParams(vmem_limit_bytes=32 << 20),
        name="mirror",
    )(place, share, one, other, result)


def per_device(expert_ids, gates, expert_out):
    tokens, channels = expert_ids.shape[0], expert_out.shape[1]
    dp_size = lax.axis_size("dp")
    member = lax.axis_index("expert")
    half = channels // 2
    swap = [(0, 1), (1, 0)]

    sent, pick, starts, coef = pick_half((expert_ids.T, gates.T), expert_out, tokens, half, True)
    from_peer = lax.ppermute(sent, "expert", swap)
    (kept,) = pick_half((starts, pick, coef), expert_out, tokens, half, False)
    from_peer_too = lax.ppermute(kept, "expert", swap)
    rows, turned = merge(coef, kept, from_peer)
    (turned,) = merge(coef, sent, from_peer_too, turned)

    total_tokens = tokens * dp_size
    if dp_size == 8 and channels == 8 * 384:
        return symmetric_moment(rows, turned, total_tokens)
    slab = jnp.dot(turned, rows, preferred_element_type=F32)
    slab = jnp.where(member == 0, slab, jnp.roll(slab, half, axis=0))
    return lax.psum_scatter(slab, "dp", scatter_dimension=0, tiled=True) / total_tokens


def solution(mesh):
    assert mesh.shape["expert"] == 2
    in_specs = (
        P(("groups", "dp"), None),
        P(("groups", "dp"), None),
        P(("groups", "dp", "expert"), None),
    )
    out_specs = P(("groups", "dp"), "expert")
    return jax.shard_map(
        per_device, mesh=mesh, in_specs=in_specs, out_specs=out_specs, check_vma=False
    )
```

```python
import functools

import jax
import jax.numpy as jnp
import numpy as np
from jax import lax
from jax.experimental import pallas as pl
from jax.experimental.pallas import tpu as pltpu
from jax.sharding import PartitionSpec as P

EXPERTS = 8
CAP = 384
BATCH = 48
WINDOW = 64
SNAKE = (0, 2, 4, 6, 7, 5, 3, 1)
F32, BF16, I32 = jnp.float32, jnp.bfloat16, jnp.int32


def plan_tokens(ids_ref, gates_ref, pick_ref, starts_ref, coef_ref):
    tokens = ids_ref.shape[1]
    local = EXPERTS // 2
    lanes = lax.broadcasted_iota(I32, (tokens, 128), 1)
    rows = jnp.concatenate([ids_ref[...].astype(F32), gates_ref[...], jnp.zeros((4, tokens), F32)], axis=0).T
    ids = [rows[:, k : k + 1].astype(I32) for k in range(2)]
    gates = [rows[:, k : k + 1] for k in (2, 3)]
    hits = [ids[k] == lanes for k in range(2)]
    named = jnp.where(hits[0] | hits[1], 1.0, 0.0).astype(BF16)
    earlier = jnp.where(
        lax.broadcasted_iota(I32, (tokens, tokens), 1) < lax.broadcasted_iota(I32, (tokens, tokens), 0), 1.0, 0.0
    ).astype(BF16)
    before = jnp.dot(earlier, named, preferred_element_type=F32)

    slots = [ids[k] - lax.axis_index("expert") * local for k in range(2)]
    here = [jnp.where((slots[k] >= 0) & (slots[k] < local), 1.0, 0.0) for k in range(2)]
    both = here[0] * here[1]
    neither = (1.0 - here[0]) * (1.0 - here[1])
    mixed = 1.0 - both - neither
    weights = [here[k] * jnp.where(both > 0.5, gates[k], 1.0) for k in range(2)]
    ours = here[0] * gates[0] + here[1] * gates[1]
    theirs = (1.0 - here[0]) * gates[0] + (1.0 - here[1]) * gates[1]
    ours = jnp.where(mixed > 0.5, ours, both)
    theirs = jnp.where(mixed > 0.5, theirs, neither)
    coef_ref[...] = jnp.where(
        lanes == 0, weights[0], jnp.where(lanes == 1, weights[1], jnp.where(lanes == 2, ours, theirs))
    )

    columns = lax.broadcasted_iota(I32, (BATCH, local * WINDOW), 1)
    for b in range(tokens // BATCH):
        rows = slice(b * BATCH, (b + 1) * BATCH)
        start = before[b * BATCH : b * BATCH + 1, :].astype(I32)
        start = jnp.minimum((start >> 4) << 4, CAP - WINDOW)
        starts_ref[b : b + 1, :] = start
        ahead = before[rows] - start.astype(F32)
        for k in range(2):
            offset = jnp.sum(jnp.where(hits[k][rows], ahead, 0.0), axis=1, keepdims=True).astype(I32)
            at = jnp.where(here[k][rows] > 0.5, slots[k][rows] * WINDOW + offset, -1)
            pick_ref[(2 * b + k) * BATCH : (2 * b + k + 1) * BATCH, :] = jnp.where(columns == at, 1.0, 0.0).astype(BF16)


def pick_kernel(first, *refs):
    if first:
        ids_ref, gates_ref, rows_ref, out_ref, pick_ref, starts_ref, coef_ref = refs[:7]
        held, made, in_sems, out_sems, starts, starts_sem = refs[7:]
    else:
        starts, pick_ref, coef_ref, rows_ref, out_ref, held, made, in_sems, out_sems = refs
    tokens, width = out_ref.shape
    tiles, _, tile = held.shape
    local = EXPERTS // 2
    member = lax.axis_index("expert")
    base = (1 - member if first else member) * width

    loads = []
    for j in range(tiles):
        at = pl.ds(pl.multiple_of(base + j * tile, 128), tile)
        loads.append(pltpu.make_async_copy(rows_ref.at[:, at], held.at[j], in_sems.at[j]))
        loads[-1].start()
    if first:
        plan_tokens(ids_ref, gates_ref, pick_ref, starts_ref, coef_ref)
        copy = pltpu.make_async_copy(starts_ref, starts, starts_sem)
        copy.start()
        copy.wait()
    stores = []
    for j in range(tiles):
        loads[j].wait()
        for b in range(tokens // BATCH):
            windows = []
            for k in range(local):
                at = k * CAP + starts[b, member * local + k]
                windows.append(held[j, pl.ds(pl.multiple_of(at, 16), WINDOW), :])
            picked = jnp.dot(
                pick_ref[2 * b * BATCH : 2 * (b + 1) * BATCH, :],
                jnp.concatenate(windows, axis=0),
                preferred_element_type=F32,
            )
            rows = slice(b * BATCH, (b + 1) * BATCH)
            total = coef_ref[rows, 0:1] * picked[:BATCH] + coef_ref[rows, 1:2] * picked[BATCH:]
            made[j, rows, :] = total.astype(BF16)
        stores.append(
            pltpu.make_async_copy(made.at[j], out_ref.at[:, j * tile : (j + 1) * tile], out_sems.at[j])
        )
        stores[-1].start()
    for store in stores:
        store.wait()


def pick_half(args, rows, tokens, width, first, tile=512):
    tiles = width // tile
    depth = EXPERTS // 2 * WINDOW
    any_, vmem = pl.BlockSpec(memory_space=pl.ANY), pl.BlockSpec(memory_space=pltpu.VMEM)
    out_shape = [jax.ShapeDtypeStruct((tokens, width), BF16)]
    scratch = [
        pltpu.VMEM((tiles, rows.shape[0], tile), BF16),
        pltpu.VMEM((tiles, tokens, tile), BF16),
        pltpu.SemaphoreType.DMA((tiles,)),
        pltpu.SemaphoreType.DMA((tiles,)),
    ]
    if first:
        out_shape += [
            jax.ShapeDtypeStruct((2 * tokens, depth), BF16),
            jax.ShapeDtypeStruct((tokens // BATCH, 128), I32),
            jax.ShapeDtypeStruct((tokens, 128), F32),
        ]
        in_specs = [vmem, vmem, any_]
        scratch += [pltpu.SMEM((tokens // BATCH, 128), I32), pltpu.SemaphoreType.DMA]
    else:
        in_specs = [pl.BlockSpec(memory_space=pltpu.SMEM), vmem, vmem, any_]
    return pl.pallas_call(
        functools.partial(pick_kernel, first),
        out_shape=out_shape,
        in_specs=in_specs,
        out_specs=[any_] + [vmem] * (len(out_shape) - 1),
        scratch_shapes=scratch,
        cost_estimate=pl.CostEstimate(
            flops=4 * tokens * depth * width, bytes_accessed=2 * (rows.shape[0] + tokens) * width, transcendentals=0
        ),
        compiler_params=pltpu.CompilerParams(vmem_limit_bytes=24 << 20),
        name="pick_first" if first else "pick_second",
    )(*args, pltpu.with_memory_space_constraint(rows, pltpu.HBM))


def merge_kernel(first, coef_ref, ours_ref, theirs_ref, *refs):
    total = coef_ref[:, 2:3] * ours_ref[...].astype(F32) + coef_ref[:, 3:4] * theirs_ref[...].astype(F32)
    total = total.astype(BF16)
    if first:
        refs[0][...] = total
    refs[-1][...] = total.T


def merge(coef, ours, theirs, turned=None, tile=384):
    tokens, width = ours.shape
    first = turned is None
    steps = width // tile
    tall = pl.BlockSpec((tokens, tile), lambda j: (0, j))
    flat = pl.BlockSpec((tile, tokens), lambda j: (j if first else j + steps, 0))
    in_specs = [pl.BlockSpec(coef.shape, lambda j: (0, 0)), tall, tall]
    args = [coef, ours, theirs]
    out_shape = [jax.ShapeDtypeStruct((2 * width, tokens), BF16)]
    out_specs = [flat]
    if first:
        out_shape.insert(0, jax.ShapeDtypeStruct((tokens, width), BF16))
        out_specs.insert(0, tall)
    else:
        in_specs.append(pl.BlockSpec(memory_space=pl.ANY))
        args.append(turned)
    return pl.pallas_call(
        functools.partial(merge_kernel, first),
        out_shape=out_shape,
        grid=(steps,),
        in_specs=in_specs,
        out_specs=out_specs,
        input_output_aliases={} if first else {3: 0},
        compiler_params=pltpu.CompilerParams(vmem_limit_bytes=32 << 20),
        cost_estimate=pl.CostEstimate(flops=4 * ours.size, bytes_accessed=6 * ours.size, transcendentals=0),
        name="merge_first" if first else "merge_second",
    )(*args)


def my_row():
    return lax.axis_index("dp") * 2 + lax.axis_index("expert")


def blocks_kernel(count, table, turned_ref, mine_ref, *refs):
    tall, width = refs[-1].shape
    strip = tall - width
    me = my_row()
    for n, out_ref in enumerate(refs[-count:]):
        jobs = [table[me, 4 * n + k] for k in range(4)]
        parts = ((0, width, width), (width, strip, strip))
        for k, (at, rows, unit) in enumerate(parts):

            @pl.when(jobs[2 * k] >= 0)
            def _(jobs=jobs, k=k, out_ref=out_ref, at=at, rows=rows, unit=unit):
                down = pl.ds(pl.multiple_of(jobs[2 * k] * unit, 32), rows)
                along = pl.ds(pl.multiple_of(jobs[2 * k + 1] * width, 128), width)
                block = jnp.dot(turned_ref[down, :], mine_ref[:, along], preferred_element_type=F32)
                out_ref[at : at + rows, :] = block.astype(out_ref.dtype)

        @pl.when(jobs[2] < 0)
        def _(out_ref=out_ref):
            out_ref[width:, :] = jnp.zeros((strip, width), out_ref.dtype)


def moment_blocks(table, turned, mine, width, strip, dtype, name, after=()):
    count = table.shape[1] // 4
    whole = lambda shape: pl.BlockSpec(shape, lambda i, s: (0, 0))
    piece = (width + strip, width)
    return pl.pallas_call(
        functools.partial(blocks_kernel, count),
        out_shape=[jax.ShapeDtypeStruct(piece, dtype)] * count,
        grid_spec=pltpu.PrefetchScalarGridSpec(
            num_scalar_prefetch=1,
            grid=(1,),
            in_specs=[whole(turned.shape), whole(mine.shape)] + [pl.BlockSpec(memory_space=pl.ANY)] * len(after),
            out_specs=[whole(piece)] * count,
        ),
        cost_estimate=pl.CostEstimate(
            flops=2 * count * mine.shape[0] * width * width,
            bytes_accessed=2 * turned.size + 2 * mine.size + count * width * width * 4,
            transcendentals=0,
        ),
        compiler_params=pltpu.CompilerParams(vmem_limit_bytes=40 << 20),
        name=name,
    )(table, turned, mine, *after)


STRIP = 96


def is_diagonal(b, e):
    return b // 4 == e


def owned_columns(b, e):
    shift = 0 if is_diagonal(b, e) or e == 1 else 1
    return [(b + shift) % 4, (b + shift + 1) % 4]


def leads(b):
    return b % 4 < 2


def fourth_column(b, e):
    if is_diagonal(b, e):
        return (b + 2) % 4
    return (b + 3) % 4 if e == 1 else b % 4


ROUNDS = (
    ((0, 4), (1, 4), (1, 3), (0, 5)),
    ((0, 3), (1, 5), (1, 2), (0, 6)),
    ((0, 2), (1, 6), (1, 1), (0, 7)),
    ((0, 1), (1, 7), (0, 0), (1, 0)),
)


def job_table(which, width):
    table = np.full((8, 2, len(which), 4), -1, np.int32)
    for p, b in enumerate(SNAKE):
        for e in range(2):
            for n, (x, t) in enumerate(which):
                q = SNAKE[(p + t) % 8]
                table[b, e, n, :2] = (q % 4 + (0 if q // 4 == e else 4), owned_columns(q, e)[x])
                if is_diagonal(q, e):
                    lead, other = (q % 4, (q + 2) % 4) if leads(q) else ((q + 2) % 4, q % 4)
                    first = lead * width + (0 if leads(q) else width // 2)
                else:
                    first, other = (4 + q % 4) * width, fourth_column(q, e)
                table[b, e, n, 2:] = (first // STRIP + x, other)
    return table.reshape(16, -1)


def ring_perm(direction):
    pairs = [(SNAKE[p], SNAKE[(p + direction) % 8]) for p in range(8)]
    return [(a * 2 + e, b * 2 + e) for a, b in pairs for e in range(2)]


def mirror_perms():
    one, other = [], []
    for b in range(8):
        for e in range(2):
            here = b * 2 + e
            if is_diagonal(b, e):
                one.append((here, (b // 4 * 4 + (b + 1) % 4) * 2 + e))
                other.append((here, (b // 4 * 4 + (b + 2) % 4) * 2 + e))
            elif e == 1:
                other.append((here, (4 + b) * 2))
                one.append((here, (4 + (b + 1) % 4) * 2))
            else:
                other.append((here, (b + 1) % 4 * 2 + 1))
                one.append((here, (b + 2) % 4 * 2 + 1))
    return one, other


def place_table():
    table = np.zeros((8, 2, 5), np.int32)
    for b in range(8):
        for e in range(2):
            diagonal = is_diagonal(b, e)
            mirrored = (b + 2) % 4 if not diagonal and e == 1 else (b + 3) % 4
            kind = (1 if leads(b) else 2) if diagonal else 0
            table[b, e] = (*owned_columns(b, e), mirrored, fourth_column(b, e), kind)
    return table


def total(own, right, left, rows):
    return own[rows, :] + right[rows, :].astype(F32) + left[rows, :].astype(F32)


def outgoing_kernel(scale, place, own0, own1, right0, left0, right1, left1, one, other, share):
    width = one.shape[0]
    kind = place[my_row(), 4]
    block, strip = slice(0, width), slice(width, width + STRIP)
    one[...] = (total(own1, right1, left1, block) * scale).astype(BF16)
    share[:STRIP, :] = total(own0, right0, left0, strip) * scale
    share[STRIP:, :] = total(own1, right1, left1, strip) * scale

    @pl.when(kind == 0)
    def _():
        other[...] = ((total(own0, right0, left0, block) * scale).T[width // 2 :, :]).astype(BF16)

    @pl.when(kind > 0)
    def _():
        other[...] = share[...].astype(BF16)


def put(place, n, made, out_ref, sem):
    width = made.shape[0]
    at = pl.ds(pl.multiple_of(place[my_row(), n] * width, 128), width)
    return pltpu.make_async_copy(made, out_ref.at[:, at], sem)


def own_kernel(scale, place, own0, own1, right0, left0, right1, left1, out_ref, made, sems):
    block = slice(0, made.shape[1])
    copies = []
    for n, parts in enumerate(((own0, right0, left0), (own1, right1, left1))):
        made[n] = total(*parts, block) * scale
        copies.append(put(place, n, made.at[n], out_ref, sems.at[n]))
        copies[-1].start()
    for copy in copies:
        copy.wait()


def one_kernel(place, one, result_ref, out_ref, made, sem):
    made[...] = one[...].astype(F32).T
    copy = put(place, 2, made, out_ref, sem)
    copy.start()
    copy.wait()


def other_kernel(place, share, other, result_ref, out_ref, made, sem):
    kind = place[my_row(), 4]
    half = other.shape[0]

    @pl.when(kind < 2)
    def _():
        made[:half, :] = share[...]
        made[half:, :] = other[...].astype(F32)

    @pl.when(kind == 2)
    def _():
        made[...] = jnp.concatenate([other[...].astype(F32), share[...]], axis=0).T

    copy = put(place, 3, made, out_ref, sem)
    copy.start()
    copy.wait()


def symmetric_moment(mine, turned, total_tokens):
    width = mine.shape[1] // 4
    both = ("dp", "expert")
    blocks = {}

    def compute(n, dtype, after=()):
        which = ROUNDS[n]
        table = jnp.asarray(job_table(which, width))
        blocks.update(zip(which, moment_blocks(table, turned, mine, width, STRIP, dtype, f"blocks{n}", after)))

    def hop(value, key):
        return lax.ppermute(value, both, ring_perm(1 if key[1] <= (4 if key[0] == 0 else 3) else -1))

    compute(0, BF16)
    moving = {key: blocks[key] for key in ROUNDS[0]}
    arrived = {}
    for n in range(4):
        landed = {}
        for key in ROUNDS[n]:
            if key in moving:
                landed[key] = hop(moving[key], key)
        if n < 3:
            compute(n + 1, F32, after=(landed[ROUNDS[n][0]],))
        moving = {}
        for (x, t), value in landed.items():
            rightwards = t <= (4 if x == 0 else 3)
            t = t - 1 if rightwards else (t + 1) % 8
            if t == 0:
                arrived[x, rightwards] = value
            else:
                moving[x, t] = (value.astype(F32) + blocks[x, t]).astype(BF16)

    place = jnp.asarray(place_table().reshape(16, -1))
    smem, vmem, any_ = [pl.BlockSpec(memory_space=m) for m in (pltpu.SMEM, pltpu.VMEM, pl.ANY)]
    result = jax.ShapeDtypeStruct((width, 4 * width), F32)
    params = pltpu.CompilerParams(vmem_limit_bytes=24 << 20)
    sums = (blocks[0, 0], blocks[1, 0], arrived[0, True], arrived[0, False], arrived[1, True], arrived[1, False])
    scale = 1.0 / total_tokens
    one, other, share = pl.pallas_call(
        functools.partial(outgoing_kernel, scale),
        out_shape=[
            jax.ShapeDtypeStruct((width, width), BF16),
            jax.ShapeDtypeStruct((2 * STRIP, width), BF16),
            jax.ShapeDtypeStruct((2 * STRIP, width), F32),
        ],
        in_specs=[smem] + [vmem] * 6,
        out_specs=[vmem] * 3,
        compiler_params=params,
        name="outgoing",
    )(place, *sums)
    perm_one, perm_other = mirror_perms()
    one = lax.ppermute(one, both, perm_one)
    other = lax.ppermute(other, both, perm_other)
    partial_result = pl.pallas_call(
        functools.partial(own_kernel, scale),
        out_shape=result,
        in_specs=[smem] + [vmem] * 6,
        out_specs=any_,
        scratch_shapes=[pltpu.VMEM((2, width, width), F32), pltpu.SemaphoreType.DMA((2,))],
        compiler_params=params,
        name="own",
    )(place, *sums)
    for kernel, args, name in ((one_kernel, (one,), "one"), (other_kernel, (share, other), "other")):
        partial_result = pl.pallas_call(
            kernel,
            out_shape=result,
            in_specs=[smem] + [vmem] * len(args) + [any_],
            out_specs=any_,
            scratch_shapes=[pltpu.VMEM((width, width), F32), pltpu.SemaphoreType.DMA],
            input_output_aliases={len(args) + 1: 0},
            compiler_params=params,
            name=name,
        )(place, *args, partial_result)
    return partial_result


def per_device(expert_ids, gates, expert_out):
    tokens, channels = expert_ids.shape[0], expert_out.shape[1]
    dp_size = lax.axis_size("dp")
    member = lax.axis_index("expert")
    half = channels // 2
    swap = [(0, 1), (1, 0)]

    sent, pick, starts, coef = pick_half((expert_ids.T, gates.T), expert_out, tokens, half, True)
    from_peer = lax.ppermute(sent, "expert", swap)
    (kept,) = pick_half((starts, pick, coef), expert_out, tokens, half, False)
    from_peer_too = lax.ppermute(kept, "expert", swap)
    rows, turned = merge(coef, kept, from_peer)
    (turned,) = merge(coef, sent, from_peer_too, turned)

    total_tokens = tokens * dp_size
    if dp_size == 8 and channels == 8 * 384:
        return symmetric_moment(rows, turned, total_tokens)
    slab = jnp.dot(turned, rows, preferred_element_type=F32)
    slab = jnp.where(member == 0, slab, jnp.roll(slab, half, axis=0))
    return lax.psum_scatter(slab, "dp", scatter_dimension=0, tiled=True) / total_tokens


def solution(mesh):
    assert mesh.shape["expert"] == 2
    in_specs = (
        P(("groups", "dp"), None),
        P(("groups", "dp"), None),
        P(("groups", "dp", "expert"), None),
    )
    out_specs = P(("groups", "dp"), "expert")
    return jax.shard_map(
        per_device, mesh=mesh, in_specs=in_specs, out_specs=out_specs, check_vma=False
    )
```

```python
import functools

import jax
import jax.numpy as jnp
import numpy as np
from jax import lax
from jax.experimental import pallas as pl
from jax.experimental.pallas import tpu as pltpu
from jax.sharding import PartitionSpec as P

EXPERTS = 8
CAP = 384
BATCH = 48
WINDOW = 64
SNAKE = (0, 2, 4, 6, 7, 5, 3, 1)
F32, BF16, I32 = jnp.float32, jnp.bfloat16, jnp.int32


def plan_tokens(ids_ref, gates_ref, pick_ref, starts_ref, coef_ref):
    tokens = ids_ref.shape[1]
    local = EXPERTS // 2
    lanes = lax.broadcasted_iota(I32, (tokens, 128), 1)
    rows = jnp.concatenate([ids_ref[...].astype(F32), gates_ref[...], jnp.zeros((4, tokens), F32)], axis=0).T
    ids = [rows[:, k : k + 1].astype(I32) for k in range(2)]
    gates = [rows[:, k : k + 1] for k in (2, 3)]
    hits = [ids[k] == lanes for k in range(2)]
    named = jnp.where(hits[0] | hits[1], 1.0, 0.0).astype(BF16)
    earlier = jnp.where(
        lax.broadcasted_iota(I32, (tokens, tokens), 1) < lax.broadcasted_iota(I32, (tokens, tokens), 0), 1.0, 0.0
    ).astype(BF16)
    before = jnp.dot(earlier, named, preferred_element_type=F32)

    slots = [ids[k] - lax.axis_index("expert") * local for k in range(2)]
    here = [jnp.where((slots[k] >= 0) & (slots[k] < local), 1.0, 0.0) for k in range(2)]
    both = here[0] * here[1]
    neither = (1.0 - here[0]) * (1.0 - here[1])
    mixed = 1.0 - both - neither
    weights = [here[k] * jnp.where(both > 0.5, gates[k], 1.0) for k in range(2)]
    ours = here[0] * gates[0] + here[1] * gates[1]
    theirs = (1.0 - here[0]) * gates[0] + (1.0 - here[1]) * gates[1]
    ours = jnp.where(mixed > 0.5, ours, both)
    theirs = jnp.where(mixed > 0.5, theirs, neither)
    coef_ref[...] = jnp.where(
        lanes == 0, weights[0], jnp.where(lanes == 1, weights[1], jnp.where(lanes == 2, ours, theirs))
    )

    columns = lax.broadcasted_iota(I32, (BATCH, local * WINDOW), 1)
    for b in range(tokens // BATCH):
        rows = slice(b * BATCH, (b + 1) * BATCH)
        start = before[b * BATCH : b * BATCH + 1, :].astype(I32)
        start = jnp.minimum((start >> 4) << 4, CAP - WINDOW)
        starts_ref[b : b + 1, :] = start
        ahead = before[rows] - start.astype(F32)
        for k in range(2):
            offset = jnp.sum(jnp.where(hits[k][rows], ahead, 0.0), axis=1, keepdims=True).astype(I32)
            at = jnp.where(here[k][rows] > 0.5, slots[k][rows] * WINDOW + offset, -1)
            pick_ref[(2 * b + k) * BATCH : (2 * b + k + 1) * BATCH, :] = jnp.where(columns == at, 1.0, 0.0).astype(BF16)


def pick_kernel(first, *refs):
    if first:
        ids_hbm, gates_hbm, rows_ref, out_ref, pick_ref, starts_ref, coef_ref = refs[:7]
        held, in_sems, starts, ids_ref, gates_ref, small_sems = refs[7:]
    else:
        starts, pick_ref, coef_ref, rows_ref, out_ref, held, in_sems = refs
    tokens, width = out_ref.shape
    tiles, _, tile = held.shape
    local = EXPERTS // 2
    member = lax.axis_index("expert")
    base = (1 - member if first else member) * width

    if first:
        small = [
            pltpu.make_async_copy(ids_hbm, ids_ref, small_sems.at[0]),
            pltpu.make_async_copy(gates_hbm, gates_ref, small_sems.at[1]),
        ]
        for copy in small:
            copy.start()
    loads = []
    for j in range(tiles):
        at = pl.ds(pl.multiple_of(base + j * tile, 128), tile)
        loads.append(pltpu.make_async_copy(rows_ref.at[:, at], held.at[j], in_sems.at[j]))
        loads[-1].start()
    if first:
        for copy in small:
            copy.wait()
        plan_tokens(ids_ref, gates_ref, pick_ref, starts_ref, coef_ref)
        copy = pltpu.make_async_copy(starts_ref, starts, small_sems.at[2])
        copy.start()
        copy.wait()
    for j in range(tiles):
        loads[j].wait()
        for b in range(tokens // BATCH):
            windows = []
            for k in range(local):
                at = k * CAP + starts[b, member * local + k]
                windows.append(held[j, pl.ds(pl.multiple_of(at, 16), WINDOW), :])
            picked = jnp.dot(
                pick_ref[2 * b * BATCH : 2 * (b + 1) * BATCH, :],
                jnp.concatenate(windows, axis=0),
                preferred_element_type=F32,
            )
            rows = slice(b * BATCH, (b + 1) * BATCH)
            total = coef_ref[rows, 0:1] * picked[:BATCH] + coef_ref[rows, 1:2] * picked[BATCH:]
            out_ref[rows, j * tile : (j + 1) * tile] = total.astype(BF16)


def pick_half(args, rows, tokens, width, first, tile=512):
    tiles = width // tile
    depth = EXPERTS // 2 * WINDOW
    any_, vmem = pl.BlockSpec(memory_space=pl.ANY), pl.BlockSpec(memory_space=pltpu.VMEM)
    in_hbm = lambda x: pltpu.with_memory_space_constraint(x, pltpu.HBM)
    out_shape = [jax.ShapeDtypeStruct((tokens, width), BF16)]
    scratch = [pltpu.VMEM((tiles, rows.shape[0], tile), BF16), pltpu.SemaphoreType.DMA((tiles,))]
    if first:
        out_shape += [
            jax.ShapeDtypeStruct((2 * tokens, depth), BF16),
            jax.ShapeDtypeStruct((tokens // BATCH, 128), I32),
            jax.ShapeDtypeStruct((tokens, 128), F32),
        ]
        args = [in_hbm(x) for x in args]
        in_specs = [any_] * 3
        scratch += [
            pltpu.SMEM((tokens // BATCH, 128), I32),
            pltpu.VMEM((2, tokens), I32),
            pltpu.VMEM((2, tokens), F32),
            pltpu.SemaphoreType.DMA((3,)),
        ]
    else:
        in_specs = [pl.BlockSpec(memory_space=pltpu.SMEM), vmem, vmem, any_]
    return pl.pallas_call(
        functools.partial(pick_kernel, first),
        out_shape=out_shape,
        in_specs=in_specs,
        out_specs=[vmem] * len(out_shape),
        scratch_shapes=scratch,
        cost_estimate=pl.CostEstimate(
            flops=4 * tokens * depth * width, bytes_accessed=2 * (rows.shape[0] + tokens) * width, transcendentals=0
        ),
        compiler_params=pltpu.CompilerParams(vmem_limit_bytes=24 << 20),
        name="pick_first" if first else "pick_second",
    )(*args, in_hbm(rows))


def merge_kernel(first, coef_ref, ours_ref, theirs_ref, *refs):
    tokens, width = ours_ref.shape
    tile = 384
    ours = jnp.broadcast_to(coef_ref[:, 2:3], (tokens, tile))
    theirs = jnp.broadcast_to(coef_ref[:, 3:4], (tokens, tile))
    for j in range(width // tile):
        at = slice(j * tile, (j + 1) * tile)
        total = (ours * ours_ref[:, at].astype(F32) + theirs * theirs_ref[:, at].astype(F32)).astype(BF16)
        if first:
            refs[0][:, at] = total
            refs[-1][at, :] = total.T
        else:
            refs[-1][width + j * tile : width + (j + 1) * tile, :] = total.T


def merge(coef, ours, theirs, turned=None):
    tokens, width = ours.shape
    first = turned is None
    vmem = pl.BlockSpec(memory_space=pltpu.VMEM)
    args = [coef, ours, theirs] + ([] if first else [turned])
    out_shape = [jax.ShapeDtypeStruct((2 * width, tokens), BF16)]
    if first:
        out_shape.insert(0, jax.ShapeDtypeStruct((tokens, width), BF16))
    return pl.pallas_call(
        functools.partial(merge_kernel, first),
        out_shape=out_shape,
        in_specs=[vmem] * len(args),
        out_specs=[vmem] * len(out_shape),
        input_output_aliases={} if first else {3: 0},
        compiler_params=pltpu.CompilerParams(vmem_limit_bytes=24 << 20),
        cost_estimate=pl.CostEstimate(flops=4 * ours.size, bytes_accessed=6 * ours.size, transcendentals=0),
        name="merge_first" if first else "merge_second",
    )(*args)


def my_row():
    return lax.axis_index("dp") * 2 + lax.axis_index("expert")


def blocks_kernel(count, table, turned_ref, mine_ref, *refs):
    tall, width = refs[-1].shape
    strip = tall - width
    me = my_row()
    for n, out_ref in enumerate(refs[-count:]):
        jobs = [table[me, 4 * n + k] for k in range(4)]
        parts = ((0, width, width), (width, strip, strip))
        for k, (at, rows, unit) in enumerate(parts):

            @pl.when(jobs[2 * k] >= 0)
            def _(jobs=jobs, k=k, out_ref=out_ref, at=at, rows=rows, unit=unit):
                down = pl.ds(pl.multiple_of(jobs[2 * k] * unit, 32), rows)
                along = pl.ds(pl.multiple_of(jobs[2 * k + 1] * width, 128), width)
                block = jnp.dot(turned_ref[down, :], mine_ref[:, along], preferred_element_type=F32)
                out_ref[at : at + rows, :] = block.astype(out_ref.dtype)

        @pl.when(jobs[2] < 0)
        def _(out_ref=out_ref):
            out_ref[width:, :] = jnp.zeros((strip, width), out_ref.dtype)


def moment_blocks(table, turned, mine, width, strip, dtype, name, after=()):
    count = table.shape[1] // 4
    smem, vmem, any_ = [pl.BlockSpec(memory_space=m) for m in (pltpu.SMEM, pltpu.VMEM, pl.ANY)]
    piece = (width + strip, width)
    return pl.pallas_call(
        functools.partial(blocks_kernel, count),
        out_shape=[jax.ShapeDtypeStruct(piece, dtype)] * count,
        in_specs=[smem, vmem, vmem] + [any_] * len(after),
        out_specs=[vmem] * count,
        cost_estimate=pl.CostEstimate(
            flops=2 * count * mine.shape[0] * width * piece[0],
            bytes_accessed=2 * turned.size + 2 * mine.size + count * width * piece[0] * 4,
            transcendentals=0,
        ),
        compiler_params=pltpu.CompilerParams(vmem_limit_bytes=24 << 20),
        name=name,
    )(table, turned, mine, *after)


STRIP = 96


def is_diagonal(b, e):
    return b // 4 == e


def owned_columns(b, e):
    shift = 0 if is_diagonal(b, e) or e == 1 else 1
    return [(b + shift) % 4, (b + shift + 1) % 4]


def leads(b):
    return b % 4 < 2


def fourth_column(b, e):
    if is_diagonal(b, e):
        return (b + 2) % 4
    return (b + 3) % 4 if e == 1 else b % 4


ROUNDS = (
    ((0, 4), (1, 4), (1, 3), (0, 5)),
    ((0, 3), (1, 5), (1, 2), (0, 6)),
    ((0, 2), (1, 6), (1, 1), (0, 7)),
    ((0, 1), (1, 7), (0, 0), (1, 0)),
)


def job_table(which, width):
    table = np.full((8, 2, len(which), 4), -1, np.int32)
    for p, b in enumerate(SNAKE):
        for e in range(2):
            for n, (x, t) in enumerate(which):
                q = SNAKE[(p + t) % 8]
                table[b, e, n, :2] = (q % 4 + (0 if q // 4 == e else 4), owned_columns(q, e)[x])
                if is_diagonal(q, e):
                    lead, other = (q % 4, (q + 2) % 4) if leads(q) else ((q + 2) % 4, q % 4)
                    first = lead * width + (0 if leads(q) else width // 2)
                else:
                    first, other = (4 + q % 4) * width, fourth_column(q, e)
                table[b, e, n, 2:] = (first // STRIP + x, other)
    return table.reshape(16, -1)


def ring_perm(direction):
    pairs = [(SNAKE[p], SNAKE[(p + direction) % 8]) for p in range(8)]
    return [(a * 2 + e, b * 2 + e) for a, b in pairs for e in range(2)]


def mirror_perms():
    one, other = [], []
    for b in range(8):
        for e in range(2):
            here = b * 2 + e
            if is_diagonal(b, e):
                one.append((here, (b // 4 * 4 + (b + 1) % 4) * 2 + e))
                other.append((here, (b // 4 * 4 + (b + 2) % 4) * 2 + e))
            elif e == 1:
                other.append((here, (4 + b) * 2))
                one.append((here, (4 + (b + 1) % 4) * 2))
            else:
                other.append((here, (b + 1) % 4 * 2 + 1))
                one.append((here, (b + 2) % 4 * 2 + 1))
    return one, other


def place_table():
    table = np.zeros((8, 2, 5), np.int32)
    for b in range(8):
        for e in range(2):
            diagonal = is_diagonal(b, e)
            mirrored = (b + 2) % 4 if not diagonal and e == 1 else (b + 3) % 4
            kind = (1 if leads(b) else 2) if diagonal else 0
            table[b, e] = (*owned_columns(b, e), mirrored, fourth_column(b, e), kind)
    return table


def total(own, right, left, rows):
    return own[rows, :] + right[rows, :].astype(F32) + left[rows, :].astype(F32)


def outgoing_kernel(scale, place, own0, own1, right0, left0, right1, left1, one, other, share):
    width = one.shape[0]
    kind = place[my_row(), 4]
    block, strip = slice(0, width), slice(width, width + STRIP)
    one[...] = (total(own1, right1, left1, block) * scale).astype(BF16)
    share[:STRIP, :] = total(own0, right0, left0, strip) * scale
    share[STRIP:, :] = total(own1, right1, left1, strip) * scale

    @pl.when(kind == 0)
    def _():
        other[...] = ((total(own0, right0, left0, block) * scale).T[width // 2 :, :]).astype(BF16)

    @pl.when(kind > 0)
    def _():
        other[...] = share[...].astype(BF16)


def put(place, n, made, out_ref, sem):
    width = made.shape[0]
    at = pl.ds(pl.multiple_of(place[my_row(), n] * width, 128), width)
    return pltpu.make_async_copy(made, out_ref.at[:, at], sem)


def own_kernel(scale, place, own0, own1, right0, left0, right1, left1, out_ref, made, sems):
    block = slice(0, made.shape[1])
    copies = []
    for n, parts in enumerate(((own0, right0, left0), (own1, right1, left1))):
        made[n] = total(*parts, block) * scale
        copies.append(put(place, n, made.at[n], out_ref, sems.at[n]))
        copies[-1].start()
    for copy in copies:
        copy.wait()


def one_kernel(place, one, result_ref, out_ref, made, sem):
    made[...] = one[...].astype(F32).T
    copy = put(place, 2, made, out_ref, sem)
    copy.start()
    copy.wait()


def other_kernel(place, share, other, result_ref, out_ref, made, sem):
    kind = place[my_row(), 4]
    half = other.shape[0]

    @pl.when(kind < 2)
    def _():
        made[:half, :] = share[...]
        made[half:, :] = other[...].astype(F32)

    @pl.when(kind == 2)
    def _():
        made[...] = jnp.concatenate([other[...].astype(F32), share[...]], axis=0).T

    copy = put(place, 3, made, out_ref, sem)
    copy.start()
    copy.wait()


def symmetric_moment(mine, turned, total_tokens):
    width = mine.shape[1] // 4
    both = ("dp", "expert")
    blocks = {}

    def compute(which, name, dtype, after=()):
        table = jnp.asarray(job_table(which, width))
        blocks.update(zip(which, moment_blocks(table, turned, mine, width, STRIP, dtype, name, after)))

    def hop(value, key):
        return lax.ppermute(value, both, ring_perm(1 if key[1] <= (4 if key[0] == 0 else 3) else -1))

    compute(ROUNDS[0][:2], "blocks0", BF16)
    compute(ROUNDS[0][2:], "blocks0b", BF16)
    moving = {key: blocks[key] for key in ROUNDS[0]}
    arrived = {}
    for n in range(4):
        landed = {}
        for key in ROUNDS[n]:
            if key in moving:
                landed[key] = hop(moving[key], key)
        if n < 3:
            compute(ROUNDS[n + 1], f"blocks{n + 1}", F32, after=(landed[ROUNDS[n][0]],))
        moving = {}
        for (x, t), value in landed.items():
            rightwards = t <= (4 if x == 0 else 3)
            t = t - 1 if rightwards else (t + 1) % 8
            if t == 0:
                arrived[x, rightwards] = value
            else:
                moving[x, t] = (value.astype(F32) + blocks[x, t]).astype(BF16)

    place = jnp.asarray(place_table().reshape(16, -1))
    smem, vmem, any_ = [pl.BlockSpec(memory_space=m) for m in (pltpu.SMEM, pltpu.VMEM, pl.ANY)]
    result = jax.ShapeDtypeStruct((width, 4 * width), F32)
    params = pltpu.CompilerParams(vmem_limit_bytes=24 << 20)
    sums = (blocks[0, 0], blocks[1, 0], arrived[0, True], arrived[0, False], arrived[1, True], arrived[1, False])
    scale = 1.0 / total_tokens
    one, other, share = pl.pallas_call(
        functools.partial(outgoing_kernel, scale),
        out_shape=[
            jax.ShapeDtypeStruct((width, width), BF16),
            jax.ShapeDtypeStruct((2 * STRIP, width), BF16),
            jax.ShapeDtypeStruct((2 * STRIP, width), F32),
        ],
        in_specs=[smem] + [vmem] * 6,
        out_specs=[vmem] * 3,
        compiler_params=params,
        name="outgoing",
    )(place, *sums)
    perm_one, perm_other = mirror_perms()
    one = lax.ppermute(one, both, perm_one)
    other = lax.ppermute(other, both, perm_other)
    partial_result = pl.pallas_call(
        functools.partial(own_kernel, scale),
        out_shape=result,
        in_specs=[smem] + [vmem] * 6,
        out_specs=any_,
        scratch_shapes=[pltpu.VMEM((2, width, width), F32), pltpu.SemaphoreType.DMA((2,))],
        compiler_params=params,
        name="own",
    )(place, *sums)
    for kernel, args, name in ((one_kernel, (one,), "one"), (other_kernel, (share, other), "other")):
        partial_result = pl.pallas_call(
            kernel,
            out_shape=result,
            in_specs=[smem] + [vmem] * len(args) + [any_],
            out_specs=any_,
            scratch_shapes=[pltpu.VMEM((width, width), F32), pltpu.SemaphoreType.DMA],
            input_output_aliases={len(args) + 1: 0},
            compiler_params=params,
            name=name,
        )(place, *args, partial_result)
    return partial_result


def per_device(expert_ids, gates, expert_out):
    tokens, channels = expert_ids.shape[0], expert_out.shape[1]
    dp_size = lax.axis_size("dp")
    member = lax.axis_index("expert")
    half = channels // 2
    swap = [(0, 1), (1, 0)]

    sent, pick, starts, coef = pick_half((expert_ids.T, gates.T), expert_out, tokens, half, True)
    from_peer = lax.ppermute(sent, "expert", swap)
    (kept,) = pick_half((starts, pick, coef), expert_out, tokens, half, False)
    from_peer_too = lax.ppermute(kept, "expert", swap)
    rows, turned = merge(coef, kept, from_peer)
    (turned,) = merge(coef, sent, from_peer_too, turned)

    total_tokens = tokens * dp_size
    if dp_size == 8 and channels == 8 * 384:
        return symmetric_moment(rows, turned, total_tokens)
    slab = jnp.dot(turned, rows, preferred_element_type=F32)
    slab = jnp.where(member == 0, slab, jnp.roll(slab, half, axis=0))
    return lax.psum_scatter(slab, "dp", scatter_dimension=0, tiled=True) / total_tokens


def solution(mesh):
    assert mesh.shape["expert"] == 2
    in_specs = (
        P(("groups", "dp"), None),
        P(("groups", "dp"), None),
        P(("groups", "dp", "expert"), None),
    )
    out_specs = P(("groups", "dp"), "expert")
    return jax.shard_map(
        per_device, mesh=mesh, in_specs=in_specs, out_specs=out_specs, check_vma=False
    )
```

```python
import functools

import jax
import jax.numpy as jnp
import numpy as np
from jax import lax
from jax.experimental import pallas as pl
from jax.experimental.pallas import tpu as pltpu
from jax.sharding import PartitionSpec as P

EXPERTS = 8
CAP = 384
BATCH = 48
WINDOW = 64
SNAKE = (0, 2, 4, 6, 7, 5, 3, 1)
F32, BF16, I32 = jnp.float32, jnp.bfloat16, jnp.int32


def plan_tokens(ids_ref, gates_ref, pick_ref, starts_ref, coef_ref):
    tokens = ids_ref.shape[1]
    local = EXPERTS // 2
    lanes = lax.broadcasted_iota(I32, (tokens, 128), 1)
    rows = jnp.concatenate([ids_ref[...].astype(F32), gates_ref[...], jnp.zeros((4, tokens), F32)], axis=0).T
    ids = [rows[:, k : k + 1].astype(I32) for k in range(2)]
    gates = [rows[:, k : k + 1] for k in (2, 3)]
    hits = [ids[k] == lanes for k in range(2)]
    named = jnp.where(hits[0] | hits[1], 1.0, 0.0).astype(BF16)
    earlier = jnp.where(
        lax.broadcasted_iota(I32, (tokens, tokens), 1) < lax.broadcasted_iota(I32, (tokens, tokens), 0), 1.0, 0.0
    ).astype(BF16)
    before = jnp.dot(earlier, named, preferred_element_type=F32)

    slots = [ids[k] - lax.axis_index("expert") * local for k in range(2)]
    here = [jnp.where((slots[k] >= 0) & (slots[k] < local), 1.0, 0.0) for k in range(2)]
    both = here[0] * here[1]
    neither = (1.0 - here[0]) * (1.0 - here[1])
    mixed = 1.0 - both - neither
    weights = [here[k] * jnp.where(both > 0.5, gates[k], 1.0) for k in range(2)]
    ours = here[0] * gates[0] + here[1] * gates[1]
    theirs = (1.0 - here[0]) * gates[0] + (1.0 - here[1]) * gates[1]
    ours = jnp.where(mixed > 0.5, ours, both)
    theirs = jnp.where(mixed > 0.5, theirs, neither)
    coef_ref[...] = jnp.where(
        lanes == 0, weights[0], jnp.where(lanes == 1, weights[1], jnp.where(lanes == 2, ours, theirs))
    )

    columns = lax.broadcasted_iota(I32, (BATCH, local * WINDOW), 1)
    for b in range(tokens // BATCH):
        rows = slice(b * BATCH, (b + 1) * BATCH)
        start = before[b * BATCH : b * BATCH + 1, :].astype(I32)
        start = jnp.minimum((start >> 4) << 4, CAP - WINDOW)
        starts_ref[b : b + 1, :] = start
        ahead = before[rows] - start.astype(F32)
        for k in range(2):
            offset = jnp.sum(jnp.where(hits[k][rows], ahead, 0.0), axis=1, keepdims=True).astype(I32)
            at = jnp.where(here[k][rows] > 0.5, slots[k][rows] * WINDOW + offset, -1)
            pick_ref[(2 * b + k) * BATCH : (2 * b + k + 1) * BATCH, :] = jnp.where(columns == at, 1.0, 0.0).astype(BF16)


def pick_kernel(first, *refs):
    if first:
        ids_hbm, gates_hbm, rows_ref, out_ref, pick_ref, starts_ref, coef_ref = refs[:7]
        held, in_sems, starts, ids_ref, gates_ref, small_sems = refs[7:]
    else:
        starts, pick_ref, coef_ref, rows_ref, out_ref, held, in_sems = refs
    tokens, width = out_ref.shape
    tiles, _, tile = held.shape
    local = EXPERTS // 2
    member = lax.axis_index("expert")
    base = (1 - member if first else member) * width

    if first:
        small = [
            pltpu.make_async_copy(ids_hbm, ids_ref, small_sems.at[0]),
            pltpu.make_async_copy(gates_hbm, gates_ref, small_sems.at[1]),
        ]
        for copy in small:
            copy.start()
    loads = []
    for j in range(tiles):
        at = pl.ds(pl.multiple_of(base + j * tile, 128), tile)
        loads.append(pltpu.make_async_copy(rows_ref.at[:, at], held.at[j], in_sems.at[j]))
        loads[-1].start()
    if first:
        for copy in small:
            copy.wait()
        plan_tokens(ids_ref, gates_ref, pick_ref, starts_ref, coef_ref)
        copy = pltpu.make_async_copy(starts_ref, starts, small_sems.at[2])
        copy.start()
        copy.wait()
    for j in range(tiles):
        loads[j].wait()
        for b in range(tokens // BATCH):
            windows = []
            for k in range(local):
                at = k * CAP + starts[b, member * local + k]
                windows.append(held[j, pl.ds(pl.multiple_of(at, 16), WINDOW), :])
            picked = jnp.dot(
                pick_ref[2 * b * BATCH : 2 * (b + 1) * BATCH, :],
                jnp.concatenate(windows, axis=0),
                preferred_element_type=F32,
            )
            rows = slice(b * BATCH, (b + 1) * BATCH)
            total = coef_ref[rows, 0:1] * picked[:BATCH] + coef_ref[rows, 1:2] * picked[BATCH:]
            out_ref[rows, j * tile : (j + 1) * tile] = total.astype(BF16)


def pick_half(args, rows, tokens, width, first, tile=512):
    tiles = width // tile
    depth = EXPERTS // 2 * WINDOW
    any_, vmem = pl.BlockSpec(memory_space=pl.ANY), pl.BlockSpec(memory_space=pltpu.VMEM)
    in_hbm = lambda x: pltpu.with_memory_space_constraint(x, pltpu.HBM)
    out_shape = [jax.ShapeDtypeStruct((tokens, width), BF16)]
    scratch = [pltpu.VMEM((tiles, rows.shape[0], tile), BF16), pltpu.SemaphoreType.DMA((tiles,))]
    if first:
        out_shape += [
            jax.ShapeDtypeStruct((2 * tokens, depth), BF16),
            jax.ShapeDtypeStruct((tokens // BATCH, 128), I32),
            jax.ShapeDtypeStruct((tokens, 128), F32),
        ]
        args = [in_hbm(x) for x in args]
        in_specs = [any_] * 3
        scratch += [
            pltpu.SMEM((tokens // BATCH, 128), I32),
            pltpu.VMEM((2, tokens), I32),
            pltpu.VMEM((2, tokens), F32),
            pltpu.SemaphoreType.DMA((3,)),
        ]
    else:
        in_specs = [pl.BlockSpec(memory_space=pltpu.SMEM), vmem, vmem, any_]
    return pl.pallas_call(
        functools.partial(pick_kernel, first),
        out_shape=out_shape,
        in_specs=in_specs,
        out_specs=[vmem] * len(out_shape),
        scratch_shapes=scratch,
        cost_estimate=pl.CostEstimate(
            flops=4 * tokens * depth * width, bytes_accessed=2 * (rows.shape[0] + tokens) * width, transcendentals=0
        ),
        compiler_params=pltpu.CompilerParams(vmem_limit_bytes=24 << 20),
        name="pick_first" if first else "pick_second",
    )(*args, in_hbm(rows))


def merge_kernel(first, coef_ref, ours_ref, theirs_ref, *refs):
    tokens, width = ours_ref.shape
    tile = 384
    ours = jnp.broadcast_to(coef_ref[:, 2:3], (tokens, tile))
    theirs = jnp.broadcast_to(coef_ref[:, 3:4], (tokens, tile))
    for j in range(width // tile):
        at = slice(j * tile, (j + 1) * tile)
        total = (ours * ours_ref[:, at].astype(F32) + theirs * theirs_ref[:, at].astype(F32)).astype(BF16)
        if first:
            refs[0][:, at] = total
            refs[-1][at, :] = total.T
        else:
            refs[-1][width + j * tile : width + (j + 1) * tile, :] = total.T


def merge(coef, ours, theirs, turned=None):
    tokens, width = ours.shape
    first = turned is None
    vmem = pl.BlockSpec(memory_space=pltpu.VMEM)
    args = [coef, ours, theirs] + ([] if first else [turned])
    out_shape = [jax.ShapeDtypeStruct((2 * width, tokens), BF16)]
    if first:
        out_shape.insert(0, jax.ShapeDtypeStruct((tokens, width), BF16))
    return pl.pallas_call(
        functools.partial(merge_kernel, first),
        out_shape=out_shape,
        in_specs=[vmem] * len(args),
        out_specs=[vmem] * len(out_shape),
        input_output_aliases={} if first else {3: 0},
        compiler_params=pltpu.CompilerParams(vmem_limit_bytes=24 << 20),
        cost_estimate=pl.CostEstimate(flops=4 * ours.size, bytes_accessed=6 * ours.size, transcendentals=0),
        name="merge_first" if first else "merge_second",
    )(*args)


def my_row():
    return lax.axis_index("dp") * 2 + lax.axis_index("expert")


def blocks_kernel(count, table, turned_ref, mine_ref, *refs):
    tall, width = refs[-1].shape
    strip = tall - width
    me = my_row()
    for n, out_ref in enumerate(refs[-count:]):
        jobs = [table[me, 4 * n + k] for k in range(4)]
        parts = ((0, width, width), (width, strip, strip))
        for k, (at, rows, unit) in enumerate(parts):

            @pl.when(jobs[2 * k] >= 0)
            def _(jobs=jobs, k=k, out_ref=out_ref, at=at, rows=rows, unit=unit):
                down = pl.ds(pl.multiple_of(jobs[2 * k] * unit, 32), rows)
                along = pl.ds(pl.multiple_of(jobs[2 * k + 1] * width, 128), width)
                block = jnp.dot(turned_ref[down, :], mine_ref[:, along], preferred_element_type=F32)
                out_ref[at : at + rows, :] = block.astype(out_ref.dtype)

        @pl.when(jobs[2] < 0)
        def _(out_ref=out_ref):
            out_ref[width:, :] = jnp.zeros((strip, width), out_ref.dtype)


def moment_blocks(table, turned, mine, width, strip, dtype, name, after=()):
    count = table.shape[1] // 4
    smem, vmem, any_ = [pl.BlockSpec(memory_space=m) for m in (pltpu.SMEM, pltpu.VMEM, pl.ANY)]
    piece = (width + strip, width)
    return pl.pallas_call(
        functools.partial(blocks_kernel, count),
        out_shape=[jax.ShapeDtypeStruct(piece, dtype)] * count,
        in_specs=[smem, vmem, vmem] + [any_] * len(after),
        out_specs=[vmem] * count,
        cost_estimate=pl.CostEstimate(
            flops=2 * count * mine.shape[0] * width * piece[0],
            bytes_accessed=2 * turned.size + 2 * mine.size + count * width * piece[0] * 4,
            transcendentals=0,
        ),
        compiler_params=pltpu.CompilerParams(vmem_limit_bytes=24 << 20),
        name=name,
    )(table, turned, mine, *after)


STRIP = 96


def is_diagonal(b, e):
    return b // 4 == e


def owned_columns(b, e):
    shift = 0 if is_diagonal(b, e) or e == 1 else 1
    return [(b + shift) % 4, (b + shift + 1) % 4]


def leads(b):
    return b % 4 < 2


def fourth_column(b, e):
    if is_diagonal(b, e):
        return (b + 2) % 4
    return (b + 3) % 4 if e == 1 else b % 4


ROUNDS = (
    ((0, 4), (1, 4), (1, 3), (0, 5)),
    ((0, 3), (1, 5), (1, 2), (0, 6)),
    ((0, 2), (1, 6), (1, 1), (0, 7)),
    ((0, 1), (1, 7), (0, 0), (1, 0)),
)


def job_table(which, width):
    table = np.full((8, 2, len(which), 4), -1, np.int32)
    for p, b in enumerate(SNAKE):
        for e in range(2):
            for n, (x, t) in enumerate(which):
                q = SNAKE[(p + t) % 8]
                table[b, e, n, :2] = (q % 4 + (0 if q // 4 == e else 4), owned_columns(q, e)[x])
                if is_diagonal(q, e):
                    lead, other = (q % 4, (q + 2) % 4) if leads(q) else ((q + 2) % 4, q % 4)
                    first = lead * width + (0 if leads(q) else width // 2)
                else:
                    first, other = (4 + q % 4) * width, fourth_column(q, e)
                table[b, e, n, 2:] = (first // STRIP + x, other)
    return table.reshape(16, -1)


def ring_perm(direction):
    pairs = [(SNAKE[p], SNAKE[(p + direction) % 8]) for p in range(8)]
    return [(a * 2 + e, b * 2 + e) for a, b in pairs for e in range(2)]


def mirror_perms():
    one, other = [], []
    for b in range(8):
        for e in range(2):
            here = b * 2 + e
            if is_diagonal(b, e):
                one.append((here, (b // 4 * 4 + (b + 1) % 4) * 2 + e))
                other.append((here, (b // 4 * 4 + (b + 2) % 4) * 2 + e))
            elif e == 1:
                other.append((here, (4 + b) * 2))
                one.append((here, (4 + (b + 1) % 4) * 2))
            else:
                other.append((here, (b + 1) % 4 * 2 + 1))
                one.append((here, (b + 2) % 4 * 2 + 1))
    return one, other


def place_table():
    table = np.zeros((8, 2, 5), np.int32)
    for b in range(8):
        for e in range(2):
            diagonal = is_diagonal(b, e)
            mirrored = (b + 2) % 4 if not diagonal and e == 1 else (b + 3) % 4
            kind = (1 if leads(b) else 2) if diagonal else 0
            table[b, e] = (*owned_columns(b, e), mirrored, fourth_column(b, e), kind)
    return table


def total(own, right, left, rows):
    return own[rows, :] + right[rows, :].astype(F32) + left[rows, :].astype(F32)


def outgoing_kernel(scale, place, own0, own1, right0, left1, right1, left0, one, other, share):
    width = one.shape[0]
    kind = place[my_row(), 4]
    block, strip = slice(0, width), slice(width, width + STRIP)
    one[...] = (total(own1, right1, left1, block) * scale).astype(BF16)
    share[:STRIP, :] = total(own0, right0, left0, strip) * scale
    share[STRIP:, :] = total(own1, right1, left1, strip) * scale

    @pl.when(kind == 0)
    def _():
        other[...] = ((total(own0, right0, left0, block) * scale).T[width // 2 :, :]).astype(BF16)

    @pl.when(kind > 0)
    def _():
        other[...] = share[...].astype(BF16)


def put(place, n, made, out_ref, sem):
    width = made.shape[0]
    at = pl.ds(pl.multiple_of(place[my_row(), n] * width, 128), width)
    return pltpu.make_async_copy(made, out_ref.at[:, at], sem)


def own_kernel(scale, place, own0, own1, right0, left1, right1, left0, out_ref, made, sems):
    block = slice(0, made.shape[1])
    copies = []
    for n, parts in enumerate(((own0, right0, left0), (own1, right1, left1))):
        made[n] = total(*parts, block) * scale
        copies.append(put(place, n, made.at[n], out_ref, sems.at[n]))
        copies[-1].start()
    for copy in copies:
        copy.wait()


def one_kernel(place, one, result_ref, out_ref, made, sem):
    made[...] = one[...].astype(F32).T
    copy = put(place, 2, made, out_ref, sem)
    copy.start()
    copy.wait()


def other_kernel(place, share, other, result_ref, out_ref, made, sem):
    kind = place[my_row(), 4]
    half = other.shape[0]

    @pl.when(kind < 2)
    def _():
        made[:half, :] = share[...]
        made[half:, :] = other[...].astype(F32)

    @pl.when(kind == 2)
    def _():
        made[...] = jnp.concatenate([other[...].astype(F32), share[...]], axis=0).T

    copy = put(place, 3, made, out_ref, sem)
    copy.start()
    copy.wait()


def symmetric_moment(mine, turned, total_tokens):
    width = mine.shape[1] // 4
    both = ("dp", "expert")
    blocks = {}

    def compute(which, name, dtype, after=()):
        table = jnp.asarray(job_table(which, width))
        blocks.update(zip(which, moment_blocks(table, turned, mine, width, STRIP, dtype, name, after)))

    def hop(value, key):
        return lax.ppermute(value, both, ring_perm(1 if key[1] <= (4 if key[0] == 0 else 3) else -1))

    compute(ROUNDS[0][:2], "blocks0", BF16)
    compute(ROUNDS[0][2:], "blocks0b", BF16)
    compute(ROUNDS[1], "blocks1", F32)
    moving = {key: blocks[key] for key in ROUNDS[0]}
    arrived = {}
    for n in range(4):
        landed = {}
        for key in ROUNDS[n]:
            if key in moving:
                landed[key] = hop(moving[key], key)
        if n < 2:
            compute(ROUNDS[n + 2], f"blocks{n + 2}", F32, after=(landed[ROUNDS[n][0]],))
        moving = {}
        for (x, t), value in landed.items():
            rightwards = t <= (4 if x == 0 else 3)
            t = t - 1 if rightwards else (t + 1) % 8
            if t == 0:
                arrived[x, rightwards] = value
            else:
                moving[x, t] = (value.astype(F32) + blocks[x, t]).astype(BF16)

    place = jnp.asarray(place_table().reshape(16, -1))
    smem, vmem, any_ = [pl.BlockSpec(memory_space=m) for m in (pltpu.SMEM, pltpu.VMEM, pl.ANY)]
    result = jax.ShapeDtypeStruct((width, 4 * width), F32)
    params = pltpu.CompilerParams(vmem_limit_bytes=24 << 20)
    sums = (blocks[0, 0], blocks[1, 0], arrived[0, True], arrived[1, False], arrived[1, True], arrived[0, False])
    scale = 1.0 / total_tokens
    one, other, share = pl.pallas_call(
        functools.partial(outgoing_kernel, scale),
        out_shape=[
            jax.ShapeDtypeStruct((width, width), BF16),
            jax.ShapeDtypeStruct((2 * STRIP, width), BF16),
            jax.ShapeDtypeStruct((2 * STRIP, width), F32),
        ],
        in_specs=[smem] + [vmem] * 6,
        out_specs=[vmem] * 3,
        compiler_params=params,
        name="outgoing",
    )(place, *sums)
    perm_one, perm_other = mirror_perms()
    one = lax.ppermute(one, both, perm_one)
    other = lax.ppermute(other, both, perm_other)
    partial_result = pl.pallas_call(
        functools.partial(own_kernel, scale),
        out_shape=result,
        in_specs=[smem] + [vmem] * 6,
        out_specs=any_,
        scratch_shapes=[pltpu.VMEM((2, width, width), F32), pltpu.SemaphoreType.DMA((2,))],
        compiler_params=params,
        name="own",
    )(place, *sums)
    for kernel, args, name in ((one_kernel, (one,), "one"), (other_kernel, (share, other), "other")):
        partial_result = pl.pallas_call(
            kernel,
            out_shape=result,
            in_specs=[smem] + [vmem] * len(args) + [any_],
            out_specs=any_,
            scratch_shapes=[pltpu.VMEM((width, width), F32), pltpu.SemaphoreType.DMA],
            input_output_aliases={len(args) + 1: 0},
            compiler_params=params,
            name=name,
        )(place, *args, partial_result)
    return partial_result


def per_device(expert_ids, gates, expert_out):
    tokens, channels = expert_ids.shape[0], expert_out.shape[1]
    dp_size = lax.axis_size("dp")
    member = lax.axis_index("expert")
    half = channels // 2
    swap = [(0, 1), (1, 0)]

    sent, pick, starts, coef = pick_half((expert_ids.T, gates.T), expert_out, tokens, half, True)
    from_peer = lax.ppermute(sent, "expert", swap)
    (kept,) = pick_half((starts, pick, coef), expert_out, tokens, half, False)
    from_peer_too = lax.ppermute(kept, "expert", swap)
    rows, turned = merge(coef, kept, from_peer)
    (turned,) = merge(coef, sent, from_peer_too, turned)

    total_tokens = tokens * dp_size
    if dp_size == 8 and channels == 8 * 384:
        return symmetric_moment(rows, turned, total_tokens)
    slab = jnp.dot(turned, rows, preferred_element_type=F32)
    slab = jnp.where(member == 0, slab, jnp.roll(slab, half, axis=0))
    return lax.psum_scatter(slab, "dp", scatter_dimension=0, tiled=True) / total_tokens


def solution(mesh):
    assert mesh.shape["expert"] == 2
    in_specs = (
        P(("groups", "dp"), None),
        P(("groups", "dp"), None),
        P(("groups", "dp", "expert"), None),
    )
    out_specs = P(("groups", "dp"), "expert")
    return jax.shard_map(
        per_device, mesh=mesh, in_specs=in_specs, out_specs=out_specs, check_vma=False
    )
```

```python
import functools

import jax
import jax.numpy as jnp
import numpy as np
from jax import lax
from jax.experimental import pallas as pl
from jax.experimental.pallas import tpu as pltpu
from jax.sharding import PartitionSpec as P

EXPERTS = 8
CAP = 384
BATCH = 48
WINDOW = 64
SNAKE = (0, 2, 4, 6, 7, 5, 3, 1)
F32, BF16, I32 = jnp.float32, jnp.bfloat16, jnp.int32


def plan_tokens(ids_ref, gates_ref, pick_ref, starts_ref, coef_ref):
    tokens = ids_ref.shape[1]
    local = EXPERTS // 2
    lanes = lax.broadcasted_iota(I32, (tokens, 128), 1)
    rows = jnp.concatenate([ids_ref[...].astype(F32), gates_ref[...], jnp.zeros((4, tokens), F32)], axis=0).T
    ids = [rows[:, k : k + 1].astype(I32) for k in range(2)]
    gates = [rows[:, k : k + 1] for k in (2, 3)]
    hits = [ids[k] == lanes for k in range(2)]
    named = jnp.where(hits[0] | hits[1], 1.0, 0.0).astype(BF16)
    earlier = jnp.where(
        lax.broadcasted_iota(I32, (tokens, tokens), 1) < lax.broadcasted_iota(I32, (tokens, tokens), 0), 1.0, 0.0
    ).astype(BF16)
    before = jnp.dot(earlier, named, preferred_element_type=F32)

    slots = [ids[k] - lax.axis_index("expert") * local for k in range(2)]
    here = [jnp.where((slots[k] >= 0) & (slots[k] < local), 1.0, 0.0) for k in range(2)]
    both = here[0] * here[1]
    neither = (1.0 - here[0]) * (1.0 - here[1])
    mixed = 1.0 - both - neither
    weights = [here[k] * jnp.where(both > 0.5, gates[k], 1.0) for k in range(2)]
    ours = here[0] * gates[0] + here[1] * gates[1]
    theirs = (1.0 - here[0]) * gates[0] + (1.0 - here[1]) * gates[1]
    ours = jnp.where(mixed > 0.5, ours, both)
    theirs = jnp.where(mixed > 0.5, theirs, neither)
    coef_ref[...] = jnp.where(
        lanes == 0, weights[0], jnp.where(lanes == 1, weights[1], jnp.where(lanes == 2, ours, theirs))
    )

    columns = lax.broadcasted_iota(I32, (BATCH, local * WINDOW), 1)
    for b in range(tokens // BATCH):
        rows = slice(b * BATCH, (b + 1) * BATCH)
        start = before[b * BATCH : b * BATCH + 1, :].astype(I32)
        start = jnp.minimum((start >> 4) << 4, CAP - WINDOW)
        starts_ref[b : b + 1, :] = start
        ahead = before[rows] - start.astype(F32)
        for k in range(2):
            offset = jnp.sum(jnp.where(hits[k][rows], ahead, 0.0), axis=1, keepdims=True).astype(I32)
            at = jnp.where(here[k][rows] > 0.5, slots[k][rows] * WINDOW + offset, -1)
            pick_ref[(2 * b + k) * BATCH : (2 * b + k + 1) * BATCH, :] = jnp.where(columns == at, 1.0, 0.0).astype(BF16)


def pick_kernel(first, *refs):
    if first:
        ids_hbm, gates_hbm, rows_ref, out_ref, pick_ref, starts_ref, coef_ref = refs[:7]
        held, in_sems, starts, ids_ref, gates_ref, small_sems = refs[7:]
    else:
        starts, pick_ref, coef_ref, rows_ref, out_ref, held, in_sems = refs
    tokens, width = out_ref.shape
    tiles, _, tile = held.shape
    local = EXPERTS // 2
    member = lax.axis_index("expert")
    base = (1 - member if first else member) * width

    if first:
        small = [
            pltpu.make_async_copy(ids_hbm, ids_ref, small_sems.at[0]),
            pltpu.make_async_copy(gates_hbm, gates_ref, small_sems.at[1]),
        ]
        for copy in small:
            copy.start()
    loads = []
    for j in range(tiles):
        at = pl.ds(pl.multiple_of(base + j * tile, 128), tile)
        loads.append(pltpu.make_async_copy(rows_ref.at[:, at], held.at[j], in_sems.at[j]))
        loads[-1].start()
    if first:
        for copy in small:
            copy.wait()
        plan_tokens(ids_ref, gates_ref, pick_ref, starts_ref, coef_ref)
        copy = pltpu.make_async_copy(starts_ref, starts, small_sems.at[2])
        copy.start()
        copy.wait()
    for j in range(tiles):
        loads[j].wait()
        for b in range(tokens // BATCH):
            windows = []
            for k in range(local):
                at = k * CAP + starts[b, member * local + k]
                windows.append(held[j, pl.ds(pl.multiple_of(at, 16), WINDOW), :])
            picked = jnp.dot(
                pick_ref[2 * b * BATCH : 2 * (b + 1) * BATCH, :],
                jnp.concatenate(windows, axis=0),
                preferred_element_type=F32,
            )
            rows = slice(b * BATCH, (b + 1) * BATCH)
            total = coef_ref[rows, 0:1] * picked[:BATCH] + coef_ref[rows, 1:2] * picked[BATCH:]
            out_ref[rows, j * tile : (j + 1) * tile] = total.astype(BF16)


def pick_half(args, rows, tokens, width, first, tile=512):
    tiles = width // tile
    depth = EXPERTS // 2 * WINDOW
    any_, vmem = pl.BlockSpec(memory_space=pl.ANY), pl.BlockSpec(memory_space=pltpu.VMEM)
    in_hbm = lambda x: pltpu.with_memory_space_constraint(x, pltpu.HBM)
    out_shape = [jax.ShapeDtypeStruct((tokens, width), BF16)]
    scratch = [pltpu.VMEM((tiles, rows.shape[0], tile), BF16), pltpu.SemaphoreType.DMA((tiles,))]
    if first:
        out_shape += [
            jax.ShapeDtypeStruct((2 * tokens, depth), BF16),
            jax.ShapeDtypeStruct((tokens // BATCH, 128), I32),
            jax.ShapeDtypeStruct((tokens, 128), F32),
        ]
        args = [in_hbm(x) for x in args]
        in_specs = [any_] * 3
        scratch += [
            pltpu.SMEM((tokens // BATCH, 128), I32),
            pltpu.VMEM((2, tokens), I32),
            pltpu.VMEM((2, tokens), F32),
            pltpu.SemaphoreType.DMA((3,)),
        ]
    else:
        in_specs = [pl.BlockSpec(memory_space=pltpu.SMEM), vmem, vmem, any_]
    return pl.pallas_call(
        functools.partial(pick_kernel, first),
        out_shape=out_shape,
        in_specs=in_specs,
        out_specs=[vmem] * len(out_shape),
        scratch_shapes=scratch,
        cost_estimate=pl.CostEstimate(
            flops=4 * tokens * depth * width, bytes_accessed=2 * (rows.shape[0] + tokens) * width, transcendentals=0
        ),
        compiler_params=pltpu.CompilerParams(vmem_limit_bytes=24 << 20),
        name="pick_first" if first else "pick_second",
    )(*args, in_hbm(rows))


def merge_kernel(first, coef_ref, ours_ref, theirs_ref, *refs):
    tokens, width = ours_ref.shape
    tile = 384
    ours = jnp.broadcast_to(coef_ref[:, 2:3], (tokens, tile))
    theirs = jnp.broadcast_to(coef_ref[:, 3:4], (tokens, tile))
    for j in range(width // tile):
        at = slice(j * tile, (j + 1) * tile)
        total = (ours * ours_ref[:, at].astype(F32) + theirs * theirs_ref[:, at].astype(F32)).astype(BF16)
        if first:
            refs[0][:, at] = total
            refs[-1][at, :] = total.T
        else:
            refs[-1][width + j * tile : width + (j + 1) * tile, :] = total.T


def merge(coef, ours, theirs, turned=None):
    tokens, width = ours.shape
    first = turned is None
    vmem = pl.BlockSpec(memory_space=pltpu.VMEM)
    args = [coef, ours, theirs] + ([] if first else [turned])
    out_shape = [jax.ShapeDtypeStruct((2 * width, tokens), BF16)]
    if first:
        out_shape.insert(0, jax.ShapeDtypeStruct((tokens, width), BF16))
    return pl.pallas_call(
        functools.partial(merge_kernel, first),
        out_shape=out_shape,
        in_specs=[vmem] * len(args),
        out_specs=[vmem] * len(out_shape),
        input_output_aliases={} if first else {3: 0},
        compiler_params=pltpu.CompilerParams(vmem_limit_bytes=24 << 20),
        cost_estimate=pl.CostEstimate(flops=4 * ours.size, bytes_accessed=6 * ours.size, transcendentals=0),
        name="merge_first" if first else "merge_second",
    )(*args)


def my_row():
    return lax.axis_index("dp") * 2 + lax.axis_index("expert")


def blocks_kernel(pieces, width, table, turned_ref, mine_ref, *refs):
    third = width // 3
    me = my_row()
    for n, (x, out_ref) in enumerate(zip(pieces, refs[-len(pieces) :])):
        tall = out_ref.shape[0]
        row, column, strip, strip_column, diagonal = [table[me, FIELDS * n + k] for k in range(FIELDS)]

        def part(out_ref, at, lane, first_row, rows, first_column, columns):
            down = pl.ds(pl.multiple_of(first_row, STRIP), rows)
            along = pl.ds(pl.multiple_of(first_column, 128), columns)
            block = jnp.dot(turned_ref[down, :], mine_ref[:, along], preferred_element_type=F32)
            out_ref[at : at + rows, lane : lane + columns] = block.astype(out_ref.dtype)

        @pl.when(diagonal == 0 if x == 0 else True)
        def _(o=out_ref, r=row * width, c=column * width, s=strip * STRIP, sc=strip_column * width, tall=tall):
            part(o, 0, 0, r, width, c, width)
            part(o, width, 0, s, tall - width, sc, width)

        if x == 0:

            @pl.when(diagonal == 1)
            def _(o=out_ref, r=row * width, c=column * width, s=strip * STRIP, sc=strip_column * width, tall=tall):
                part(o, 0, 0, r, third, c, width)
                part(o, third, 0, r + third, third, c + third, 2 * third)
                part(o, third, 2 * third, r + 2 * third, third, c + 2 * third, third)
                part(o, 2 * third, 0, s, tall - 2 * third, sc, width)


def moment_blocks(table, pieces, turned, mine, width, dtype, name, after=()):
    count = len(pieces)
    smem, vmem, any_ = [pl.BlockSpec(memory_space=m) for m in (pltpu.SMEM, pltpu.VMEM, pl.ANY)]
    piece = (width + STRIP, width)
    return pl.pallas_call(
        functools.partial(blocks_kernel, pieces, width),
        out_shape=[jax.ShapeDtypeStruct(piece, dtype)] * count,
        in_specs=[smem, vmem, vmem] + [any_] * len(after),
        out_specs=[vmem] * count,
        cost_estimate=pl.CostEstimate(
            flops=2 * count * mine.shape[0] * width * piece[0],
            bytes_accessed=0,
            transcendentals=0,
        ),
        compiler_params=pltpu.CompilerParams(vmem_limit_bytes=24 << 20),
        name=name,
    )(table, turned, mine, *after)


STRIP = 32
FIELDS = 5


def is_diagonal(b, e):
    return b // 4 == e


def owned_columns(b, e):
    shift = 0 if is_diagonal(b, e) or e == 1 else 1
    return [(b + shift) % 4, (b + shift + 1) % 4]


def leads(b):
    return b % 4 < 2


def fourth_column(b, e):
    if is_diagonal(b, e):
        return (b + 2) % 4
    return (b + 3) % 4 if e == 1 else b % 4


ROUNDS = (
    ((0, 4), (1, 4), (1, 3), (0, 5)),
    ((0, 3), (1, 5), (1, 2), (0, 6)),
    ((0, 2), (1, 6), (1, 1), (0, 7)),
    ((0, 1), (1, 7), (0, 0), (1, 0)),
)


def job_table(which, width):
    table = np.zeros((8, 2, len(which), FIELDS), np.int32)
    for p, b in enumerate(SNAKE):
        for e in range(2):
            for n, (x, t) in enumerate(which):
                q = SNAKE[(p + t) % 8]
                row, column = q % 4 + (0 if q // 4 == e else 4), owned_columns(q, e)[x]
                if is_diagonal(q, e):
                    lead, other = (q % 4, (q + 2) % 4) if leads(q) else ((q + 2) % 4, q % 4)
                    first = lead * width + (0 if leads(q) else width // 2) + x * (width // 3 + STRIP)
                else:
                    first, other = row * width + x * STRIP, fourth_column(q, e)
                table[b, e, n] = (row, column, first // STRIP, other, is_diagonal(q, e))
    return table.reshape(16, -1)


def ring_perm(direction):
    pairs = [(SNAKE[p], SNAKE[(p + direction) % 8]) for p in range(8)]
    return [(a * 2 + e, b * 2 + e) for a, b in pairs for e in range(2)]


def mirror_perms():
    one, other = [], []
    for b in range(8):
        for e in range(2):
            here = b * 2 + e
            if is_diagonal(b, e):
                one.append((here, (b // 4 * 4 + (b + 1) % 4) * 2 + e))
                other.append((here, (b // 4 * 4 + (b + 2) % 4) * 2 + e))
            elif e == 1:
                other.append((here, (4 + b) * 2))
                one.append((here, (4 + (b + 1) % 4) * 2))
            else:
                other.append((here, (b + 1) % 4 * 2 + 1))
                one.append((here, (b + 2) % 4 * 2 + 1))
    return one, other


def place_table():
    table = np.zeros((8, 2, 5), np.int32)
    for b in range(8):
        for e in range(2):
            diagonal = is_diagonal(b, e)
            mirrored = (b + 2) % 4 if not diagonal and e == 1 else (b + 3) % 4
            kind = (1 if leads(b) else 2) if diagonal else 0
            table[b, e] = (*owned_columns(b, e), mirrored, fourth_column(b, e), kind)
    return table


def total(own, right, left, rows):
    return own[rows, :] + right[rows, :].astype(F32) + left[rows, :].astype(F32)


def outgoing_kernel(scale, place, own0, own1, right0, left1, right1, left0, one, other, share):
    width = one.shape[0]
    third, half = width // 3, width // 2
    tall = width + STRIP
    kind = place[my_row(), 4]
    one[...] = (total(own1, right1, left1, slice(0, width)) * scale).astype(BF16)
    tail = total(own1, right1, left1, slice(width, tall)) * scale

    @pl.when(kind == 0)
    def _():
        share[:STRIP, :] = total(own0, right0, left0, slice(width, tall)) * scale
        share[STRIP : 2 * STRIP, :] = tail
        share[2 * STRIP :, :] = jnp.zeros((half - 2 * STRIP, width), F32)
        turned = (total(own0, right0, left0, slice(0, width)) * scale).T
        other[...] = turned[2 * STRIP :, :].astype(BF16)

    @pl.when(kind > 0)
    def _():
        share[: half - STRIP, :] = total(own0, right0, left0, slice(2 * third, tall)) * scale
        share[half - STRIP :, :] = tail
        other[:half, :] = share[...].astype(BF16)
        other[half:, :] = jnp.zeros((width - 2 * STRIP - half, width), BF16)


def put(place, n, made, out_ref, sem):
    width = made.shape[0]
    at = pl.ds(pl.multiple_of(place[my_row(), n] * width, 128), width)
    return pltpu.make_async_copy(made, out_ref.at[:, at], sem)


def own_kernel(scale, place, own0, own1, right0, left1, right1, left0, out_ref, made, sems):
    width = made.shape[1]
    third = width // 3
    made[1] = total(own1, right1, left1, slice(0, width)) * scale
    copies = [put(place, n, made.at[n], out_ref, sems.at[n]) for n in range(2)]
    copies[1].start()

    @pl.when(place[my_row(), 4] == 0)
    def _():
        made[0] = total(own0, right0, left0, slice(0, width)) * scale

    @pl.when(place[my_row(), 4] > 0)
    def _():
        tiles = total(own0, right0, left0, slice(0, 2 * third)) * scale
        upper = {(0, 0): (0, 0), (0, 1): (0, 1), (0, 2): (0, 2), (1, 1): (1, 0), (1, 2): (1, 1), (2, 2): (1, 2)}
        for (i, j), (r, c) in upper.items():
            tile = tiles[r * third : (r + 1) * third, c * third : (c + 1) * third]
            made[0, i * third : (i + 1) * third, j * third : (j + 1) * third] = tile
            if i != j:
                made[0, j * third : (j + 1) * third, i * third : (i + 1) * third] = tile.T

    copies[0].start()
    for copy in copies:
        copy.wait()


def one_kernel(place, one, result_ref, out_ref, made, sem):
    made[...] = one[...].astype(F32).T
    copy = put(place, 2, made, out_ref, sem)
    copy.start()
    copy.wait()


def other_kernel(place, share, other, result_ref, out_ref, made, sem):
    kind = place[my_row(), 4]
    half = share.shape[0]

    @pl.when(kind == 0)
    def _():
        made[: 2 * STRIP, :] = share[: 2 * STRIP, :]
        made[2 * STRIP :, :] = other[...].astype(F32)

    @pl.when(kind == 1)
    def _():
        made[:half, :] = share[...]
        made[half:, :] = other[:half, :].astype(F32)

    @pl.when(kind == 2)
    def _():
        made[...] = jnp.concatenate([other[:half, :].astype(F32), share[...]], axis=0).T

    copy = put(place, 3, made, out_ref, sem)
    copy.start()
    copy.wait()


def symmetric_moment(mine, turned, total_tokens):
    width = mine.shape[1] // 4
    both = ("dp", "expert")
    blocks = {}

    def compute(which, name, dtype, after=()):
        table = jnp.asarray(job_table(which, width))
        pieces = tuple(x for x, _ in which)
        blocks.update(zip(which, moment_blocks(table, pieces, turned, mine, width, dtype, name, after)))

    def hop(value, key):
        return lax.ppermute(value, both, ring_perm(1 if key[1] <= (4 if key[0] == 0 else 3) else -1))

    compute(ROUNDS[0][:2], "blocks0", BF16)
    compute(ROUNDS[0][2:], "blocks0b", BF16)
    compute(ROUNDS[1], "blocks1", F32)
    moving = {key: blocks[key] for key in ROUNDS[0]}
    arrived = {}
    for n in range(4):
        landed = {}
        for key in ROUNDS[n]:
            if key in moving:
                landed[key] = hop(moving[key], key)
        if n < 2:
            compute(ROUNDS[n + 2], f"blocks{n + 2}", F32, after=(landed[ROUNDS[n][0]],))
        moving = {}
        for (x, t), value in landed.items():
            rightwards = t <= (4 if x == 0 else 3)
            t = t - 1 if rightwards else (t + 1) % 8
            if t == 0:
                arrived[x, rightwards] = value
            else:
                moving[x, t] = (value.astype(F32) + blocks[x, t]).astype(BF16)

    place = jnp.asarray(place_table().reshape(16, -1))
    smem, vmem, any_ = [pl.BlockSpec(memory_space=m) for m in (pltpu.SMEM, pltpu.VMEM, pl.ANY)]
    result = jax.ShapeDtypeStruct((width, 4 * width), F32)
    params = pltpu.CompilerParams(vmem_limit_bytes=24 << 20)
    sums = (blocks[0, 0], blocks[1, 0], arrived[0, True], arrived[1, False], arrived[1, True], arrived[0, False])
    scale = 1.0 / total_tokens
    one, other, share = pl.pallas_call(
        functools.partial(outgoing_kernel, scale),
        out_shape=[
            jax.ShapeDtypeStruct((width, width), BF16),
            jax.ShapeDtypeStruct((width - 2 * STRIP, width), BF16),
            jax.ShapeDtypeStruct((width // 2, width), F32),
        ],
        in_specs=[smem] + [vmem] * 6,
        out_specs=[vmem] * 3,
        compiler_params=params,
        name="outgoing",
    )(place, *sums)
    perm_one, perm_other = mirror_perms()
    one = lax.ppermute(one, both, perm_one)
    other = lax.ppermute(other, both, perm_other)
    partial_result = pl.pallas_call(
        functools.partial(own_kernel, scale),
        out_shape=result,
        in_specs=[smem] + [vmem] * 6,
        out_specs=any_,
        scratch_shapes=[pltpu.VMEM((2, width, width), F32), pltpu.SemaphoreType.DMA((2,))],
        compiler_params=params,
        name="own",
    )(place, *sums)
    for kernel, args, name in ((one_kernel, (one,), "one"), (other_kernel, (share, other), "other")):
        partial_result = pl.pallas_call(
            kernel,
            out_shape=result,
            in_specs=[smem] + [vmem] * len(args) + [any_],
            out_specs=any_,
            scratch_shapes=[pltpu.VMEM((width, width), F32), pltpu.SemaphoreType.DMA],
            input_output_aliases={len(args) + 1: 0},
            compiler_params=params,
            name=name,
        )(place, *args, partial_result)
    return partial_result


def per_device(expert_ids, gates, expert_out):
    tokens, channels = expert_ids.shape[0], expert_out.shape[1]
    dp_size = lax.axis_size("dp")
    member = lax.axis_index("expert")
    half = channels // 2
    swap = [(0, 1), (1, 0)]

    sent, pick, starts, coef = pick_half((expert_ids.T, gates.T), expert_out, tokens, half, True)
    from_peer = lax.ppermute(sent, "expert", swap)
    (kept,) = pick_half((starts, pick, coef), expert_out, tokens, half, False)
    from_peer_too = lax.ppermute(kept, "expert", swap)
    rows, turned = merge(coef, kept, from_peer)
    (turned,) = merge(coef, sent, from_peer_too, turned)

    total_tokens = tokens * dp_size
    if dp_size == 8 and channels == 8 * 384:
        return symmetric_moment(rows, turned, total_tokens)
    slab = jnp.dot(turned, rows, preferred_element_type=F32)
    slab = jnp.where(member == 0, slab, jnp.roll(slab, half, axis=0))
    return lax.psum_scatter(slab, "dp", scatter_dimension=0, tiled=True) / total_tokens


def solution(mesh):
    assert mesh.shape["expert"] == 2
    in_specs = (
        P(("groups", "dp"), None),
        P(("groups", "dp"), None),
        P(("groups", "dp", "expert"), None),
    )
    out_specs = P(("groups", "dp"), "expert")
    return jax.shard_map(
        per_device, mesh=mesh, in_specs=in_specs, out_specs=out_specs, check_vma=False
    )
```

```python
import functools

import jax
import jax.numpy as jnp
import numpy as np
from jax import lax
from jax.experimental import pallas as pl
from jax.experimental.pallas import tpu as pltpu
from jax.sharding import PartitionSpec as P

EXPERTS = 8
CAP = 384
BATCH = 48
WINDOW = 64
SNAKE = (0, 2, 4, 6, 7, 5, 3, 1)
F32, BF16, I32 = jnp.float32, jnp.bfloat16, jnp.int32


def plan_tokens(ids_ref, gates_ref, pick_ref, starts_ref, coef_ref):
    tokens = ids_ref.shape[1]
    local = EXPERTS // 2
    lanes = lax.broadcasted_iota(I32, (tokens, 128), 1)
    rows = jnp.concatenate([ids_ref[...].astype(F32), gates_ref[...], jnp.zeros((4, tokens), F32)], axis=0).T
    ids = [rows[:, k : k + 1].astype(I32) for k in range(2)]
    gates = [rows[:, k : k + 1] for k in (2, 3)]
    hits = [ids[k] == lanes for k in range(2)]
    named = jnp.where(hits[0] | hits[1], 1.0, 0.0).astype(BF16)
    earlier = jnp.where(
        lax.broadcasted_iota(I32, (tokens, tokens), 1) < lax.broadcasted_iota(I32, (tokens, tokens), 0), 1.0, 0.0
    ).astype(BF16)
    before = jnp.dot(earlier, named, preferred_element_type=F32)

    slots = [ids[k] - lax.axis_index("expert") * local for k in range(2)]
    here = [jnp.where((slots[k] >= 0) & (slots[k] < local), 1.0, 0.0) for k in range(2)]
    both = here[0] * here[1]
    neither = (1.0 - here[0]) * (1.0 - here[1])
    mixed = 1.0 - both - neither
    weights = [here[k] * jnp.where(both > 0.5, gates[k], 1.0) for k in range(2)]
    ours = here[0] * gates[0] + here[1] * gates[1]
    theirs = (1.0 - here[0]) * gates[0] + (1.0 - here[1]) * gates[1]
    ours = jnp.where(mixed > 0.5, ours, both)
    theirs = jnp.where(mixed > 0.5, theirs, neither)
    coef_ref[...] = jnp.where(
        lanes == 0, weights[0], jnp.where(lanes == 1, weights[1], jnp.where(lanes == 2, ours, theirs))
    )

    columns = lax.broadcasted_iota(I32, (BATCH, local * WINDOW), 1)
    for b in range(tokens // BATCH):
        rows = slice(b * BATCH, (b + 1) * BATCH)
        start = before[b * BATCH : b * BATCH + 1, :].astype(I32)
        start = jnp.minimum((start >> 4) << 4, CAP - WINDOW)
        starts_ref[b : b + 1, :] = start
        ahead = before[rows] - start.astype(F32)
        for k in range(2):
            offset = jnp.sum(jnp.where(hits[k][rows], ahead, 0.0), axis=1, keepdims=True).astype(I32)
            at = jnp.where(here[k][rows] > 0.5, slots[k][rows] * WINDOW + offset, -1)
            pick_ref[(2 * b + k) * BATCH : (2 * b + k + 1) * BATCH, :] = jnp.where(columns == at, 1.0, 0.0).astype(BF16)


def pick_kernel(first, tiles, *refs):
    if first:
        ids_hbm, gates_hbm, rows_ref, out_ref, held, pick_ref, starts_ref, coef_ref = refs[:8]
        in_sems, starts, ids_ref, gates_ref, small_sems = refs[8:]
    else:
        starts, pick_ref, coef_ref, held = refs[:4]
        out_ref = refs[-1]
    tokens = out_ref.shape[0]
    count, _, tile = held.shape
    local = EXPERTS // 2
    member = lax.axis_index("expert")

    loads = []
    if first:
        small = [
            pltpu.make_async_copy(ids_hbm, ids_ref, small_sems.at[0]),
            pltpu.make_async_copy(gates_hbm, gates_ref, small_sems.at[1]),
        ]
        for copy in small:
            copy.start()
        for j in range(count):
            side = 1 - member if j < count // 2 else member
            at = side * (count // 2 * tile) + j % (count // 2) * tile
            at = pl.ds(pl.multiple_of(at, 128), tile)
            loads.append(pltpu.make_async_copy(rows_ref.at[:, at], held.at[j], in_sems.at[j]))
            loads[-1].start()
        for copy in small:
            copy.wait()
        plan_tokens(ids_ref, gates_ref, pick_ref, starts_ref, coef_ref)
        copy = pltpu.make_async_copy(starts_ref, starts, small_sems.at[2])
        copy.start()
        copy.wait()
    for n, j in enumerate(tiles):
        if first:
            loads[j].wait()
        for b in range(tokens // BATCH):
            windows = []
            for k in range(local):
                at = k * CAP + starts[b, member * local + k]
                windows.append(held[j, pl.ds(pl.multiple_of(at, 16), WINDOW), :])
            picked = jnp.dot(
                pick_ref[2 * b * BATCH : 2 * (b + 1) * BATCH, :],
                jnp.concatenate(windows, axis=0),
                preferred_element_type=F32,
            )
            rows = slice(b * BATCH, (b + 1) * BATCH)
            total = coef_ref[rows, 0:1] * picked[:BATCH] + coef_ref[rows, 1:2] * picked[BATCH:]
            out_ref[rows, n * tile : (n + 1) * tile] = total.astype(BF16)
    for j, load in enumerate(loads):
        if j not in tiles:
            load.wait()


def pick_call(first, tiles, args, out_shape, in_specs, scratch, tile):
    tokens = out_shape[0].shape[0]
    vmem = pl.BlockSpec(memory_space=pltpu.VMEM)
    return pl.pallas_call(
        functools.partial(pick_kernel, first, tiles),
        out_shape=out_shape,
        in_specs=in_specs,
        out_specs=[vmem] * len(out_shape),
        scratch_shapes=scratch,
        cost_estimate=pl.CostEstimate(
            flops=tokens * EXPERTS * WINDOW * len(tiles) * tile, bytes_accessed=0, transcendentals=0
        ),
        compiler_params=pltpu.CompilerParams(vmem_limit_bytes=24 << 20),
        name="pick_first" if first else "pick",
    )(*args)


def pick_rows(ids, gates, rows, tile):
    tokens, (depth, channels) = ids.shape[1], rows.shape
    count = channels // tile
    out_shape = [
        jax.ShapeDtypeStruct((tokens, tile), BF16),
        jax.ShapeDtypeStruct((count, depth, tile), BF16),
        jax.ShapeDtypeStruct((2 * tokens, EXPERTS // 2 * WINDOW), BF16),
        jax.ShapeDtypeStruct((tokens // BATCH, 128), I32),
        jax.ShapeDtypeStruct((tokens, 128), F32),
    ]
    scratch = [
        pltpu.SemaphoreType.DMA((count,)),
        pltpu.SMEM((tokens // BATCH, 128), I32),
        pltpu.VMEM((2, tokens), I32),
        pltpu.VMEM((2, tokens), F32),
        pltpu.SemaphoreType.DMA((3,)),
    ]
    args = [pltpu.with_memory_space_constraint(x, pltpu.HBM) for x in (ids, gates, rows)]
    return pick_call(True, (0,), args, out_shape, [pl.BlockSpec(memory_space=pl.ANY)] * 3, scratch, tile)


def pick_more(tiles, starts, pick, coef, held, after=()):
    tokens, tile = coef.shape[0], held.shape[2]
    vmem = pl.BlockSpec(memory_space=pltpu.VMEM)
    out_shape = [jax.ShapeDtypeStruct((tokens, len(tiles) * tile), BF16)]
    in_specs = [pl.BlockSpec(memory_space=pltpu.SMEM)] + [vmem] * 3
    in_specs += [pl.BlockSpec(memory_space=pl.ANY)] * len(after)
    return pick_call(False, tiles, (starts, pick, coef, held, *after), out_shape, in_specs, [], tile)[0]


def merge_kernel(first, tile, pieces, coef_ref, *refs):
    tokens = coef_ref.shape[0]
    sides = []
    for count in pieces:
        sides.append([ref.at[:, j : j + tile] for ref in refs[:count] for j in range(0, ref.shape[1], tile)])
        refs = refs[count:]
    width = len(sides[0]) * tile
    ours = jnp.broadcast_to(coef_ref[:, 2:3], (tokens, tile))
    theirs = jnp.broadcast_to(coef_ref[:, 3:4], (tokens, tile))
    for j, (a, b) in enumerate(zip(*sides)):
        total = (ours * a[...].astype(F32) + theirs * b[...].astype(F32)).astype(BF16)
        if first:
            refs[0][:, j * tile : (j + 1) * tile] = total
            refs[-1][j * tile : (j + 1) * tile, :] = total.T
        else:
            refs[-1][width + j * tile : width + (j + 1) * tile, :] = total.T


def merge(coef, ours, theirs, width, turned=None, tile=256):
    tokens = coef.shape[0]
    first = turned is None
    vmem = pl.BlockSpec(memory_space=pltpu.VMEM)
    args = [coef, *ours, *theirs] + ([] if first else [turned])
    out_shape = [jax.ShapeDtypeStruct((2 * width, tokens), BF16)]
    if first:
        out_shape.insert(0, jax.ShapeDtypeStruct((tokens, width), BF16))
    return pl.pallas_call(
        functools.partial(merge_kernel, first, tile, (len(ours), len(theirs))),
        out_shape=out_shape,
        in_specs=[vmem] * len(args),
        out_specs=[vmem] * len(out_shape),
        input_output_aliases={} if first else {len(args) - 1: 0},
        compiler_params=pltpu.CompilerParams(vmem_limit_bytes=24 << 20),
        cost_estimate=pl.CostEstimate(flops=4 * tokens * width, bytes_accessed=0, transcendentals=0),
        name="merge_first" if first else "merge_second",
    )(*args)


def my_row():
    return lax.axis_index("dp") * 2 + lax.axis_index("expert")


def blocks_kernel(pieces, width, table, turned_ref, mine_ref, *refs):
    third = width // 3
    me = my_row()
    for n, (x, out_ref) in enumerate(zip(pieces, refs[-len(pieces) :])):
        tall = out_ref.shape[0]
        row, column, strip, strip_column, diagonal = [table[me, FIELDS * n + k] for k in range(FIELDS)]

        def part(out_ref, at, lane, first_row, rows, first_column, columns):
            down = pl.ds(pl.multiple_of(first_row, STRIP), rows)
            along = pl.ds(pl.multiple_of(first_column, 128), columns)
            block = jnp.dot(turned_ref[down, :], mine_ref[:, along], preferred_element_type=F32)
            out_ref[at : at + rows, lane : lane + columns] = block.astype(out_ref.dtype)

        @pl.when(diagonal == 0 if x == 0 else True)
        def _(o=out_ref, r=row * width, c=column * width, s=strip * STRIP, sc=strip_column * width, tall=tall):
            part(o, 0, 0, r, width, c, width)
            part(o, width, 0, s, tall - width, sc, width)

        if x == 0:

            @pl.when(diagonal == 1)
            def _(o=out_ref, r=row * width, c=column * width, s=strip * STRIP, sc=strip_column * width, tall=tall):
                part(o, 0, 0, r, third, c, width)
                part(o, third, 0, r + third, third, c + third, 2 * third)
                part(o, third, 2 * third, r + 2 * third, third, c + 2 * third, third)
                part(o, 2 * third, 0, s, tall - 2 * third, sc, width)


def moment_blocks(table, pieces, turned, mine, width, dtype, name, after=()):
    count = len(pieces)
    smem, vmem, any_ = [pl.BlockSpec(memory_space=m) for m in (pltpu.SMEM, pltpu.VMEM, pl.ANY)]
    piece = (width + STRIP, width)
    return pl.pallas_call(
        functools.partial(blocks_kernel, pieces, width),
        out_shape=[jax.ShapeDtypeStruct(piece, dtype)] * count,
        in_specs=[smem, vmem, vmem] + [any_] * len(after),
        out_specs=[vmem] * count,
        cost_estimate=pl.CostEstimate(
            flops=count * mine.shape[0] * width * width,
            bytes_accessed=0,
            transcendentals=0,
        ),
        compiler_params=pltpu.CompilerParams(vmem_limit_bytes=24 << 20),
        name=name,
    )(table, turned, mine, *after)


STRIP = 32
FIELDS = 5


def is_diagonal(b, e):
    return b // 4 == e


def owned_columns(b, e):
    shift = 0 if is_diagonal(b, e) or e == 1 else 1
    return [(b + shift) % 4, (b + shift + 1) % 4]


def leads(b):
    return b % 4 < 2


def fourth_column(b, e):
    if is_diagonal(b, e):
        return (b + 2) % 4
    return (b + 3) % 4 if e == 1 else b % 4


ROUNDS = (
    ((0, 4), (1, 4), (1, 3), (0, 5)),
    ((0, 3), (1, 5), (1, 2), (0, 6)),
    ((0, 2), (1, 6), (1, 1), (0, 7)),
    ((0, 1), (1, 7), (0, 0), (1, 0)),
)


def job_table(which, width):
    table = np.zeros((8, 2, len(which), FIELDS), np.int32)
    for p, b in enumerate(SNAKE):
        for e in range(2):
            for n, (x, t) in enumerate(which):
                q = SNAKE[(p + t) % 8]
                row, column = q % 4 + (0 if q // 4 == e else 4), owned_columns(q, e)[x]
                if is_diagonal(q, e):
                    lead, other = (q % 4, (q + 2) % 4) if leads(q) else ((q + 2) % 4, q % 4)
                    first = lead * width + (0 if leads(q) else width // 2) + x * (width // 3 + STRIP)
                else:
                    first, other = row * width + x * STRIP, fourth_column(q, e)
                table[b, e, n] = (row, column, first // STRIP, other, is_diagonal(q, e))
    return table.reshape(16, -1)


def ring_perm(direction):
    pairs = [(SNAKE[p], SNAKE[(p + direction) % 8]) for p in range(8)]
    return [(a * 2 + e, b * 2 + e) for a, b in pairs for e in range(2)]


def mirror_perms():
    one, other = [], []
    for b in range(8):
        for e in range(2):
            here = b * 2 + e
            if is_diagonal(b, e):
                one.append((here, (b // 4 * 4 + (b + 1) % 4) * 2 + e))
                other.append((here, (b // 4 * 4 + (b + 2) % 4) * 2 + e))
            elif e == 1:
                other.append((here, (4 + b) * 2))
                one.append((here, (4 + (b + 1) % 4) * 2))
            else:
                other.append((here, (b + 1) % 4 * 2 + 1))
                one.append((here, (b + 2) % 4 * 2 + 1))
    return one, other


def place_table():
    table = np.zeros((8, 2, 5), np.int32)
    for b in range(8):
        for e in range(2):
            diagonal = is_diagonal(b, e)
            mirrored = (b + 2) % 4 if not diagonal and e == 1 else (b + 3) % 4
            kind = (1 if leads(b) else 2) if diagonal else 0
            table[b, e] = (*owned_columns(b, e), mirrored, fourth_column(b, e), kind)
    return table


def total(own, right, left, rows):
    return own[rows, :] + right[rows, :].astype(F32) + left[rows, :].astype(F32)


def outgoing_kernel(scale, place, own0, own1, right0, left1, right1, left0, one, other, share):
    width = one.shape[0]
    third, half = width // 3, width // 2
    tall = width + STRIP
    kind = place[my_row(), 4]
    one[...] = (total(own1, right1, left1, slice(0, width)) * scale).astype(BF16)
    tail = total(own1, right1, left1, slice(width, tall)) * scale

    @pl.when(kind == 0)
    def _():
        share[:STRIP, :] = total(own0, right0, left0, slice(width, tall)) * scale
        share[STRIP : 2 * STRIP, :] = tail
        share[2 * STRIP :, :] = jnp.zeros((half - 2 * STRIP, width), F32)
        turned = (total(own0, right0, left0, slice(0, width)) * scale).T
        other[...] = turned[2 * STRIP :, :].astype(BF16)

    @pl.when(kind > 0)
    def _():
        share[: half - STRIP, :] = total(own0, right0, left0, slice(2 * third, tall)) * scale
        share[half - STRIP :, :] = tail
        other[:half, :] = share[...].astype(BF16)
        other[half:, :] = jnp.zeros((width - 2 * STRIP - half, width), BF16)


def put(place, n, made, out_ref, sem):
    width = made.shape[0]
    at = pl.ds(pl.multiple_of(place[my_row(), n] * width, 128), width)
    return pltpu.make_async_copy(made, out_ref.at[:, at], sem)


def own_kernel(scale, place, own0, own1, right0, left1, right1, left0, out_ref, made, sems):
    width = made.shape[1]
    third = width // 3
    made[1] = total(own1, right1, left1, slice(0, width)) * scale
    copies = [put(place, n, made.at[n], out_ref, sems.at[n]) for n in range(2)]
    copies[1].start()

    @pl.when(place[my_row(), 4] == 0)
    def _():
        made[0] = total(own0, right0, left0, slice(0, width)) * scale

    @pl.when(place[my_row(), 4] > 0)
    def _():
        tiles = total(own0, right0, left0, slice(0, 2 * third)) * scale
        upper = {(0, 0): (0, 0), (0, 1): (0, 1), (0, 2): (0, 2), (1, 1): (1, 0), (1, 2): (1, 1), (2, 2): (1, 2)}
        for (i, j), (r, c) in upper.items():
            tile = tiles[r * third : (r + 1) * third, c * third : (c + 1) * third]
            made[0, i * third : (i + 1) * third, j * third : (j + 1) * third] = tile
            if i != j:
                made[0, j * third : (j + 1) * third, i * third : (i + 1) * third] = tile.T

    copies[0].start()
    for copy in copies:
        copy.wait()


def one_kernel(place, one, result_ref, out_ref, made, sem):
    made[...] = one[...].astype(F32).T
    copy = put(place, 2, made, out_ref, sem)
    copy.start()
    copy.wait()


def other_kernel(place, share, other, result_ref, out_ref, made, sem):
    kind = place[my_row(), 4]
    half = share.shape[0]

    @pl.when(kind == 0)
    def _():
        made[: 2 * STRIP, :] = share[: 2 * STRIP, :]
        made[2 * STRIP :, :] = other[...].astype(F32)

    @pl.when(kind == 1)
    def _():
        made[:half, :] = share[...]
        made[half:, :] = other[:half, :].astype(F32)

    @pl.when(kind == 2)
    def _():
        made[...] = jnp.concatenate([other[:half, :].astype(F32), share[...]], axis=0).T

    copy = put(place, 3, made, out_ref, sem)
    copy.start()
    copy.wait()


def symmetric_moment(mine, turned, total_tokens):
    width = mine.shape[1] // 4
    both = ("dp", "expert")
    blocks = {}

    def compute(which, name, dtype, after=()):
        table = jnp.asarray(job_table(which, width))
        pieces = tuple(x for x, _ in which)
        blocks.update(zip(which, moment_blocks(table, pieces, turned, mine, width, dtype, name, after)))

    def hop(value, key):
        return lax.ppermute(value, both, ring_perm(1 if key[1] <= (4 if key[0] == 0 else 3) else -1))

    compute(ROUNDS[0][:2], "blocks0", BF16)
    compute(ROUNDS[0][2:], "blocks0b", BF16, after=(blocks[0, 4],))
    moving = {key: blocks[key] for key in ROUNDS[0]}
    arrived = {}
    for n in range(4):
        landed = {}
        for key in ROUNDS[n]:
            if key in moving:
                landed[key] = hop(moving[key], key)
        if n < 3:
            early = [landed[key] for key in ROUNDS[n][:2]]
            compute(ROUNDS[n + 1], f"blocks{n + 1}", F32, after=early)
        moving = {}
        for (x, t), value in landed.items():
            rightwards = t <= (4 if x == 0 else 3)
            t = t - 1 if rightwards else (t + 1) % 8
            if t == 0:
                arrived[x, rightwards] = value
            else:
                moving[x, t] = (value.astype(F32) + blocks[x, t]).astype(BF16)

    place = jnp.asarray(place_table().reshape(16, -1))
    smem, vmem, any_ = [pl.BlockSpec(memory_space=m) for m in (pltpu.SMEM, pltpu.VMEM, pl.ANY)]
    result = jax.ShapeDtypeStruct((width, 4 * width), F32)
    params = pltpu.CompilerParams(vmem_limit_bytes=24 << 20)
    sums = (blocks[0, 0], blocks[1, 0], arrived[0, True], arrived[1, False], arrived[1, True], arrived[0, False])
    scale = 1.0 / total_tokens
    one, other, share = pl.pallas_call(
        functools.partial(outgoing_kernel, scale),
        out_shape=[
            jax.ShapeDtypeStruct((width, width), BF16),
            jax.ShapeDtypeStruct((width - 2 * STRIP, width), BF16),
            jax.ShapeDtypeStruct((width // 2, width), F32),
        ],
        in_specs=[smem] + [vmem] * 6,
        out_specs=[vmem] * 3,
        compiler_params=params,
        name="outgoing",
    )(place, *sums)
    perm_one, perm_other = mirror_perms()
    one = lax.ppermute(one, both, perm_one)
    other = lax.ppermute(other, both, perm_other)
    partial_result = pl.pallas_call(
        functools.partial(own_kernel, scale),
        out_shape=result,
        in_specs=[smem] + [vmem] * 6,
        out_specs=any_,
        scratch_shapes=[pltpu.VMEM((2, width, width), F32), pltpu.SemaphoreType.DMA((2,))],
        compiler_params=params,
        name="own",
    )(place, *sums)
    for kernel, args, name in ((one_kernel, (one,), "one"), (other_kernel, (share, other), "other")):
        partial_result = pl.pallas_call(
            kernel,
            out_shape=result,
            in_specs=[smem] + [vmem] * len(args) + [any_],
            out_specs=any_,
            scratch_shapes=[pltpu.VMEM((width, width), F32), pltpu.SemaphoreType.DMA],
            input_output_aliases={len(args) + 1: 0},
            compiler_params=params,
            name=name,
        )(place, *args, partial_result)
    return partial_result


def per_device(expert_ids, gates, expert_out):
    tokens, channels = expert_ids.shape[0], expert_out.shape[1]
    dp_size = lax.axis_size("dp")
    member = lax.axis_index("expert")
    half = channels // 2
    swap = [(0, 1), (1, 0)]

    picked, held, pick, starts, coef = pick_rows(expert_ids.T, gates.T, expert_out, half // 3)
    picked, arrived = [picked], [lax.ppermute(picked, "expert", swap)]
    for tiles in ((1, 2), (3, 4), (5,)):
        after = arrived[:1] if len(picked) == 2 else ()
        picked.append(pick_more(tiles, starts, pick, coef, held, after))
        arrived.append(lax.ppermute(picked[-1], "expert", swap))
    rows, turned = merge(coef, picked[2:], arrived[:2], half)
    (turned,) = merge(coef, picked[:2], arrived[2:], half, turned)

    total_tokens = tokens * dp_size
    if dp_size == 8 and channels == 8 * 384:
        return symmetric_moment(rows, turned, total_tokens)
    slab = jnp.dot(turned, rows, preferred_element_type=F32)
    slab = jnp.where(member == 0, slab, jnp.roll(slab, half, axis=0))
    return lax.psum_scatter(slab, "dp", scatter_dimension=0, tiled=True) / total_tokens


def solution(mesh):
    assert mesh.shape["expert"] == 2
    in_specs = (
        P(("groups", "dp"), None),
        P(("groups", "dp"), None),
        P(("groups", "dp", "expert"), None),
    )
    out_specs = P(("groups", "dp"), "expert")
    return jax.shard_map(
        per_device, mesh=mesh, in_specs=in_specs, out_specs=out_specs, check_vma=False
    )
```

```python
import functools

import jax
import jax.numpy as jnp
import numpy as np
from jax import lax
from jax.experimental import pallas as pl
from jax.experimental.pallas import tpu as pltpu
from jax.sharding import PartitionSpec as P

EXPERTS = 8
CAP = 384
BATCH = 48
WINDOW = 64
SNAKE = (0, 2, 4, 6, 7, 5, 3, 1)
F32, BF16, I32 = jnp.float32, jnp.bfloat16, jnp.int32


def plan_tokens(ids_ref, gates_ref, pick_ref, starts_ref, coef_ref):
    tokens = ids_ref.shape[1]
    local = EXPERTS // 2
    lanes = lax.broadcasted_iota(I32, (tokens, 128), 1)
    rows = jnp.concatenate([ids_ref[...].astype(F32), gates_ref[...], jnp.zeros((4, tokens), F32)], axis=0).T
    ids = [rows[:, k : k + 1].astype(I32) for k in range(2)]
    gates = [rows[:, k : k + 1] for k in (2, 3)]
    hits = [ids[k] == lanes for k in range(2)]
    named = jnp.where(hits[0] | hits[1], 1.0, 0.0).astype(BF16)
    earlier = jnp.where(
        lax.broadcasted_iota(I32, (tokens, tokens), 1) < lax.broadcasted_iota(I32, (tokens, tokens), 0), 1.0, 0.0
    ).astype(BF16)
    before = jnp.dot(earlier, named, preferred_element_type=F32)

    slots = [ids[k] - lax.axis_index("expert") * local for k in range(2)]
    here = [jnp.where((slots[k] >= 0) & (slots[k] < local), 1.0, 0.0) for k in range(2)]
    both = here[0] * here[1]
    neither = (1.0 - here[0]) * (1.0 - here[1])
    mixed = 1.0 - both - neither
    weights = [here[k] * jnp.where(both > 0.5, gates[k], 1.0) for k in range(2)]
    ours = here[0] * gates[0] + here[1] * gates[1]
    theirs = (1.0 - here[0]) * gates[0] + (1.0 - here[1]) * gates[1]
    ours = jnp.where(mixed > 0.5, ours, both)
    theirs = jnp.where(mixed > 0.5, theirs, neither)
    coef_ref[...] = jnp.where(
        lanes == 0, weights[0], jnp.where(lanes == 1, weights[1], jnp.where(lanes == 2, ours, theirs))
    )

    columns = lax.broadcasted_iota(I32, (BATCH, local * WINDOW), 1)
    for b in range(tokens // BATCH):
        rows = slice(b * BATCH, (b + 1) * BATCH)
        start = before[b * BATCH : b * BATCH + 1, :].astype(I32)
        start = jnp.minimum((start >> 4) << 4, CAP - WINDOW)
        starts_ref[b : b + 1, :] = start
        ahead = before[rows] - start.astype(F32)
        for k in range(2):
            offset = jnp.sum(jnp.where(hits[k][rows], ahead, 0.0), axis=1, keepdims=True).astype(I32)
            at = jnp.where(here[k][rows] > 0.5, slots[k][rows] * WINDOW + offset, -1)
            pick_ref[(2 * b + k) * BATCH : (2 * b + k + 1) * BATCH, :] = jnp.where(columns == at, 1.0, 0.0).astype(BF16)


def start_loads(rows_ref, held, sems, side):
    tile = held.shape[2]
    loads = []
    for j in range(held.shape[0]):
        at = pl.ds(pl.multiple_of((side * held.shape[0] + j) * tile, 128), tile)
        loads.append(pltpu.make_async_copy(rows_ref.at[:, at], held.at[j], sems.at[j]))
        loads[-1].start()
    return loads


def pick_tiles(tiles, starts, pick_ref, coef_ref, held, out_ref, loads=None):
    tokens, tile = out_ref.shape[0], held.shape[2]
    local = EXPERTS // 2
    member = lax.axis_index("expert")
    for n, j in enumerate(tiles):
        if loads is not None:
            loads[j].wait()
        for b in range(tokens // BATCH):
            windows = []
            for k in range(local):
                at = k * CAP + starts[b, member * local + k]
                windows.append(held[j, pl.ds(pl.multiple_of(at, 16), WINDOW), :])
            picked = jnp.dot(
                pick_ref[2 * b * BATCH : 2 * (b + 1) * BATCH, :],
                jnp.concatenate(windows, axis=0),
                preferred_element_type=F32,
            )
            rows = slice(b * BATCH, (b + 1) * BATCH)
            total = coef_ref[rows, 0:1] * picked[:BATCH] + coef_ref[rows, 1:2] * picked[BATCH:]
            out_ref[rows, n * tile : (n + 1) * tile] = total.astype(BF16)


def pick_first_kernel(ids_hbm, gates_hbm, rows_ref, out_ref, held, pick_ref, starts_ref, coef_ref, *scratch):
    in_sems, starts, ids_ref, gates_ref, small_sems = scratch
    small = [
        pltpu.make_async_copy(ids_hbm, ids_ref, small_sems.at[0]),
        pltpu.make_async_copy(gates_hbm, gates_ref, small_sems.at[1]),
    ]
    for copy in small:
        copy.start()
    loads = start_loads(rows_ref, held, in_sems, 1 - lax.axis_index("expert"))
    for copy in small:
        copy.wait()
    plan_tokens(ids_ref, gates_ref, pick_ref, starts_ref, coef_ref)
    copy = pltpu.make_async_copy(starts_ref, starts, small_sems.at[2])
    copy.start()
    copy.wait()
    pick_tiles((0,), starts, pick_ref, coef_ref, held, out_ref, loads)
    for load in loads[1:]:
        load.wait()


def pick_rest_kernel(starts, pick_ref, coef_ref, held, rows_ref, out_ref, next_held, in_sems):
    loads = start_loads(rows_ref, next_held, in_sems, lax.axis_index("expert"))
    pick_tiles(range(1, held.shape[0]), starts, pick_ref, coef_ref, held, out_ref)
    for load in loads:
        load.wait()


def pick_mine_kernel(tiles, starts, pick_ref, coef_ref, held, *refs):
    pick_tiles(tiles, starts, pick_ref, coef_ref, held, refs[-1])


def pick_call(kernel, count, args, out_shape, in_specs, scratch, tile, name):
    tokens = out_shape[0].shape[0]
    vmem = pl.BlockSpec(memory_space=pltpu.VMEM)
    return pl.pallas_call(
        kernel,
        out_shape=out_shape,
        in_specs=in_specs,
        out_specs=[vmem] * len(out_shape),
        scratch_shapes=scratch,
        cost_estimate=pl.CostEstimate(
            flops=tokens * EXPERTS * WINDOW * count * tile, bytes_accessed=0, transcendentals=0
        ),
        compiler_params=pltpu.CompilerParams(vmem_limit_bytes=24 << 20),
        name=name,
    )(*args)


def in_hbm(x):
    return pltpu.with_memory_space_constraint(x, pltpu.HBM)


def pick_first(ids, gates, rows, tile):
    tokens, (depth, channels) = ids.shape[1], rows.shape
    count = channels // 2 // tile
    out_shape = [
        jax.ShapeDtypeStruct((tokens, tile), BF16),
        jax.ShapeDtypeStruct((count, depth, tile), BF16),
        jax.ShapeDtypeStruct((2 * tokens, EXPERTS // 2 * WINDOW), BF16),
        jax.ShapeDtypeStruct((tokens // BATCH, 128), I32),
        jax.ShapeDtypeStruct((tokens, 128), F32),
    ]
    scratch = [
        pltpu.SemaphoreType.DMA((count,)),
        pltpu.SMEM((tokens // BATCH, 128), I32),
        pltpu.VMEM((2, tokens), I32),
        pltpu.VMEM((2, tokens), F32),
        pltpu.SemaphoreType.DMA((3,)),
    ]
    args = [in_hbm(x) for x in (ids, gates, rows)]
    any_ = pl.BlockSpec(memory_space=pl.ANY)
    return pick_call(pick_first_kernel, 1, args, out_shape, [any_] * 3, scratch, tile, "pick_first")


def pick_rest(starts, pick, coef, held, rows):
    tokens, (count, _, tile) = coef.shape[0], held.shape
    smem, vmem, any_ = [pl.BlockSpec(memory_space=m) for m in (pltpu.SMEM, pltpu.VMEM, pl.ANY)]
    out_shape = [
        jax.ShapeDtypeStruct((tokens, (count - 1) * tile), BF16),
        jax.ShapeDtypeStruct(held.shape, BF16),
    ]
    args = (starts, pick, coef, held, in_hbm(rows))
    scratch = [pltpu.SemaphoreType.DMA((count,))]
    return pick_call(
        pick_rest_kernel, count - 1, args, out_shape, [smem] + [vmem] * 3 + [any_], scratch, tile, "pick_rest"
    )


def pick_mine(tiles, starts, pick, coef, held, after=()):
    tokens, tile = coef.shape[0], held.shape[2]
    smem, vmem, any_ = [pl.BlockSpec(memory_space=m) for m in (pltpu.SMEM, pltpu.VMEM, pl.ANY)]
    out_shape = [jax.ShapeDtypeStruct((tokens, len(tiles) * tile), BF16)]
    in_specs = [smem] + [vmem] * 3 + [any_] * len(after)
    kernel = functools.partial(pick_mine_kernel, tiles)
    args = (starts, pick, coef, held, *after)
    return pick_call(kernel, len(tiles), args, out_shape, in_specs, [], tile, "pick_mine")[0]


def merge_kernel(first, tile, pieces, coef_ref, *refs):
    tokens = coef_ref.shape[0]
    sides = []
    for count in pieces:
        sides.append([ref.at[:, j : j + tile] for ref in refs[:count] for j in range(0, ref.shape[1], tile)])
        refs = refs[count:]
    width = len(sides[0]) * tile
    ours = jnp.broadcast_to(coef_ref[:, 2:3], (tokens, tile))
    theirs = jnp.broadcast_to(coef_ref[:, 3:4], (tokens, tile))
    for j, (a, b) in enumerate(zip(*sides)):
        total = (ours * a[...].astype(F32) + theirs * b[...].astype(F32)).astype(BF16)
        if first:
            refs[0][:, j * tile : (j + 1) * tile] = total
            refs[-1][j * tile : (j + 1) * tile, :] = total.T
        else:
            refs[-1][width + j * tile : width + (j + 1) * tile, :] = total.T


def merge(coef, ours, theirs, width, turned=None, tile=256):
    tokens = coef.shape[0]
    first = turned is None
    vmem = pl.BlockSpec(memory_space=pltpu.VMEM)
    args = [coef, *ours, *theirs] + ([] if first else [turned])
    out_shape = [jax.ShapeDtypeStruct((2 * width, tokens), BF16)]
    if first:
        out_shape.insert(0, jax.ShapeDtypeStruct((tokens, width), BF16))
    return pl.pallas_call(
        functools.partial(merge_kernel, first, tile, (len(ours), len(theirs))),
        out_shape=out_shape,
        in_specs=[vmem] * len(args),
        out_specs=[vmem] * len(out_shape),
        input_output_aliases={} if first else {len(args) - 1: 0},
        compiler_params=pltpu.CompilerParams(vmem_limit_bytes=24 << 20),
        cost_estimate=pl.CostEstimate(flops=4 * tokens * width, bytes_accessed=0, transcendentals=0),
        name="merge_first" if first else "merge_second",
    )(*args)


def my_row():
    return lax.axis_index("dp") * 2 + lax.axis_index("expert")


def blocks_kernel(pieces, width, table, turned_ref, mine_ref, *refs):
    third = width // 3
    me = my_row()
    for n, (x, out_ref) in enumerate(zip(pieces, refs[-len(pieces) :])):
        tall = out_ref.shape[0]
        row, column, strip, strip_column, diagonal = [table[me, FIELDS * n + k] for k in range(FIELDS)]

        def part(out_ref, at, lane, first_row, rows, first_column, columns):
            down = pl.ds(pl.multiple_of(first_row, STRIP), rows)
            along = pl.ds(pl.multiple_of(first_column, 128), columns)
            block = jnp.dot(turned_ref[down, :], mine_ref[:, along], preferred_element_type=F32)
            out_ref[at : at + rows, lane : lane + columns] = block.astype(out_ref.dtype)

        @pl.when(diagonal == 0 if x == 0 else True)
        def _(o=out_ref, r=row * width, c=column * width, s=strip * STRIP, sc=strip_column * width, tall=tall):
            part(o, 0, 0, r, width, c, width)
            part(o, width, 0, s, tall - width, sc, width)

        if x == 0:

            @pl.when(diagonal == 1)
            def _(o=out_ref, r=row * width, c=column * width, s=strip * STRIP, sc=strip_column * width, tall=tall):
                part(o, 0, 0, r, third, c, width)
                part(o, third, 0, r + third, third, c + third, 2 * third)
                part(o, third, 2 * third, r + 2 * third, third, c + 2 * third, third)
                part(o, 2 * third, 0, s, tall - 2 * third, sc, width)


def moment_blocks(table, pieces, turned, mine, width, dtype, name, after=()):
    count = len(pieces)
    smem, vmem, any_ = [pl.BlockSpec(memory_space=m) for m in (pltpu.SMEM, pltpu.VMEM, pl.ANY)]
    piece = (width + STRIP, width)
    return pl.pallas_call(
        functools.partial(blocks_kernel, pieces, width),
        out_shape=[jax.ShapeDtypeStruct(piece, dtype)] * count,
        in_specs=[smem, vmem, vmem] + [any_] * len(after),
        out_specs=[vmem] * count,
        cost_estimate=pl.CostEstimate(
            flops=count * mine.shape[0] * width * width,
            bytes_accessed=0,
            transcendentals=0,
        ),
        compiler_params=pltpu.CompilerParams(vmem_limit_bytes=24 << 20),
        name=name,
    )(table, turned, mine, *after)


STRIP = 32
FIELDS = 5


def is_diagonal(b, e):
    return b // 4 == e


def owned_columns(b, e):
    shift = 0 if is_diagonal(b, e) or e == 1 else 1
    return [(b + shift) % 4, (b + shift + 1) % 4]


def leads(b):
    return b % 4 < 2


def fourth_column(b, e):
    if is_diagonal(b, e):
        return (b + 2) % 4
    return (b + 3) % 4 if e == 1 else b % 4


ROUNDS = (
    ((0, 4), (1, 4), (1, 3), (0, 5)),
    ((0, 3), (1, 5), (1, 2), (0, 6)),
    ((0, 2), (1, 6), (1, 1), (0, 7)),
    ((0, 1), (1, 7), (0, 0), (1, 0)),
)


def job_table(which, width):
    table = np.zeros((8, 2, len(which), FIELDS), np.int32)
    for p, b in enumerate(SNAKE):
        for e in range(2):
            for n, (x, t) in enumerate(which):
                q = SNAKE[(p + t) % 8]
                row, column = q % 4 + (0 if q // 4 == e else 4), owned_columns(q, e)[x]
                if is_diagonal(q, e):
                    lead, other = (q % 4, (q + 2) % 4) if leads(q) else ((q + 2) % 4, q % 4)
                    first = lead * width + (0 if leads(q) else width // 2) + x * (width // 3 + STRIP)
                else:
                    first, other = row * width + x * STRIP, fourth_column(q, e)
                table[b, e, n] = (row, column, first // STRIP, other, is_diagonal(q, e))
    return table.reshape(16, -1)


def ring_perm(direction):
    pairs = [(SNAKE[p], SNAKE[(p + direction) % 8]) for p in range(8)]
    return [(a * 2 + e, b * 2 + e) for a, b in pairs for e in range(2)]


def mirror_perms():
    one, other = [], []
    for b in range(8):
        for e in range(2):
            here = b * 2 + e
            if is_diagonal(b, e):
                one.append((here, (b // 4 * 4 + (b + 1) % 4) * 2 + e))
                other.append((here, (b // 4 * 4 + (b + 2) % 4) * 2 + e))
            elif e == 1:
                other.append((here, (4 + b) * 2))
                one.append((here, (4 + (b + 1) % 4) * 2))
            else:
                other.append((here, (b + 1) % 4 * 2 + 1))
                one.append((here, (b + 2) % 4 * 2 + 1))
    return one, other


def place_table():
    table = np.zeros((8, 2, 5), np.int32)
    for b in range(8):
        for e in range(2):
            diagonal = is_diagonal(b, e)
            mirrored = (b + 2) % 4 if not diagonal and e == 1 else (b + 3) % 4
            kind = (1 if leads(b) else 2) if diagonal else 0
            table[b, e] = (*owned_columns(b, e), mirrored, fourth_column(b, e), kind)
    return table


def total(own, right, left, rows):
    return own[rows, :] + right[rows, :].astype(F32) + left[rows, :].astype(F32)


def outgoing_kernel(scale, place, own0, own1, right0, left1, right1, left0, one, other, share):
    width = one.shape[0]
    third, half = width // 3, width // 2
    tall = width + STRIP
    kind = place[my_row(), 4]
    one[...] = (total(own1, right1, left1, slice(0, width)) * scale).astype(BF16)
    tail = total(own1, right1, left1, slice(width, tall)) * scale

    @pl.when(kind == 0)
    def _():
        share[:STRIP, :] = total(own0, right0, left0, slice(width, tall)) * scale
        share[STRIP : 2 * STRIP, :] = tail
        share[2 * STRIP :, :] = jnp.zeros((half - 2 * STRIP, width), F32)
        turned = (total(own0, right0, left0, slice(0, width)) * scale).T
        other[...] = turned[2 * STRIP :, :].astype(BF16)

    @pl.when(kind > 0)
    def _():
        share[: half - STRIP, :] = total(own0, right0, left0, slice(2 * third, tall)) * scale
        share[half - STRIP :, :] = tail
        other[:half, :] = share[...].astype(BF16)
        other[half:, :] = jnp.zeros((width - 2 * STRIP - half, width), BF16)


def put(place, n, made, out_ref, sem):
    width = made.shape[0]
    at = pl.ds(pl.multiple_of(place[my_row(), n] * width, 128), width)
    return pltpu.make_async_copy(made, out_ref.at[:, at], sem)


def own_kernel(scale, place, own0, own1, right0, left1, right1, left0, out_ref, made, sems):
    width = made.shape[1]
    third = width // 3
    made[1] = total(own1, right1, left1, slice(0, width)) * scale
    copies = [put(place, n, made.at[n], out_ref, sems.at[n]) for n in range(2)]
    copies[1].start()

    @pl.when(place[my_row(), 4] == 0)
    def _():
        made[0] = total(own0, right0, left0, slice(0, width)) * scale

    @pl.when(place[my_row(), 4] > 0)
    def _():
        tiles = total(own0, right0, left0, slice(0, 2 * third)) * scale
        upper = {(0, 0): (0, 0), (0, 1): (0, 1), (0, 2): (0, 2), (1, 1): (1, 0), (1, 2): (1, 1), (2, 2): (1, 2)}
        for (i, j), (r, c) in upper.items():
            tile = tiles[r * third : (r + 1) * third, c * third : (c + 1) * third]
            made[0, i * third : (i + 1) * third, j * third : (j + 1) * third] = tile
            if i != j:
                made[0, j * third : (j + 1) * third, i * third : (i + 1) * third] = tile.T

    copies[0].start()
    for copy in copies:
        copy.wait()


def one_kernel(place, one, result_ref, out_ref, made, sem):
    made[...] = one[...].astype(F32).T
    copy = put(place, 2, made, out_ref, sem)
    copy.start()
    copy.wait()


def other_kernel(place, share, other, result_ref, out_ref, made, sem):
    kind = place[my_row(), 4]
    half = share.shape[0]

    @pl.when(kind == 0)
    def _():
        made[: 2 * STRIP, :] = share[: 2 * STRIP, :]
        made[2 * STRIP :, :] = other[...].astype(F32)

    @pl.when(kind == 1)
    def _():
        made[:half, :] = share[...]
        made[half:, :] = other[:half, :].astype(F32)

    @pl.when(kind == 2)
    def _():
        made[...] = jnp.concatenate([other[:half, :].astype(F32), share[...]], axis=0).T

    copy = put(place, 3, made, out_ref, sem)
    copy.start()
    copy.wait()


def symmetric_moment(mine, turned, total_tokens):
    width = mine.shape[1] // 4
    both = ("dp", "expert")
    blocks = {}

    def compute(which, name, dtype, after=()):
        table = jnp.asarray(job_table(which, width))
        pieces = tuple(x for x, _ in which)
        blocks.update(zip(which, moment_blocks(table, pieces, turned, mine, width, dtype, name, after)))

    def hop(value, key):
        return lax.ppermute(value, both, ring_perm(1 if key[1] <= (4 if key[0] == 0 else 3) else -1))

    compute(ROUNDS[0][:2], "blocks0", BF16)
    compute(ROUNDS[0][2:], "blocks0b", BF16, after=(blocks[0, 4],))
    moving = {key: blocks[key] for key in ROUNDS[0]}
    arrived = {}
    before = ()
    for n in range(4):
        landed = {}
        for key in ROUNDS[n]:
            if key in moving:
                landed[key] = hop(moving[key], key)
        if n < 3:
            early = [landed[key] for key in ROUNDS[n][:2]]
            if n == 0:
                compute(ROUNDS[1], "blocks1", F32, after=early)
            else:
                compute(ROUNDS[n + 1][:2], f"blocks{n + 1}", F32, after=before)
                compute(ROUNDS[n + 1][2:], f"blocks{n + 1}b", F32, after=early)
            before = early
        moving = {}
        for (x, t), value in landed.items():
            rightwards = t <= (4 if x == 0 else 3)
            t = t - 1 if rightwards else (t + 1) % 8
            if t == 0:
                arrived[x, rightwards] = value
            else:
                moving[x, t] = (value.astype(F32) + blocks[x, t]).astype(BF16)

    place = jnp.asarray(place_table().reshape(16, -1))
    smem, vmem, any_ = [pl.BlockSpec(memory_space=m) for m in (pltpu.SMEM, pltpu.VMEM, pl.ANY)]
    result = jax.ShapeDtypeStruct((width, 4 * width), F32)
    params = pltpu.CompilerParams(vmem_limit_bytes=24 << 20)
    sums = (blocks[0, 0], blocks[1, 0], arrived[0, True], arrived[1, False], arrived[1, True], arrived[0, False])
    scale = 1.0 / total_tokens
    one, other, share = pl.pallas_call(
        functools.partial(outgoing_kernel, scale),
        out_shape=[
            jax.ShapeDtypeStruct((width, width), BF16),
            jax.ShapeDtypeStruct((width - 2 * STRIP, width), BF16),
            jax.ShapeDtypeStruct((width // 2, width), F32),
        ],
        in_specs=[smem] + [vmem] * 6,
        out_specs=[vmem] * 3,
        compiler_params=params,
        name="outgoing",
    )(place, *sums)
    perm_one, perm_other = mirror_perms()
    one = lax.ppermute(one, both, perm_one)
    other = lax.ppermute(other, both, perm_other)
    partial_result = pl.pallas_call(
        functools.partial(own_kernel, scale),
        out_shape=result,
        in_specs=[smem] + [vmem] * 6,
        out_specs=any_,
        scratch_shapes=[pltpu.VMEM((2, width, width), F32), pltpu.SemaphoreType.DMA((2,))],
        compiler_params=params,
        name="own",
    )(place, *sums)
    for kernel, args, name in ((one_kernel, (one,), "one"), (other_kernel, (share, other), "other")):
        partial_result = pl.pallas_call(
            kernel,
            out_shape=result,
            in_specs=[smem] + [vmem] * len(args) + [any_],
            out_specs=any_,
            scratch_shapes=[pltpu.VMEM((width, width), F32), pltpu.SemaphoreType.DMA],
            input_output_aliases={len(args) + 1: 0},
            compiler_params=params,
            name=name,
        )(place, *args, partial_result)
    return partial_result


def per_device(expert_ids, gates, expert_out):
    tokens, channels = expert_ids.shape[0], expert_out.shape[1]
    dp_size = lax.axis_size("dp")
    member = lax.axis_index("expert")
    half = channels // 2
    swap = [(0, 1), (1, 0)]

    send = lambda x: lax.ppermute(x, "expert", swap)
    first, held, pick, starts, coef = pick_first(expert_ids.T, gates.T, expert_out, half // 3)
    picked, arrived = [first], [send(first)]
    rest, held = pick_rest(starts, pick, coef, held, expert_out)
    picked.append(rest)
    arrived.append(send(rest))
    for tiles in ((0, 1), (2,)):
        picked.append(pick_mine(tiles, starts, pick, coef, held, arrived[:1] if tiles[0] == 0 else ()))
        arrived.append(send(picked[-1]))
    rows, turned = merge(coef, picked[2:], arrived[:2], half)
    (turned,) = merge(coef, picked[:2], arrived[2:], half, turned)

    total_tokens = tokens * dp_size
    if dp_size == 8 and channels == 8 * 384:
        return symmetric_moment(rows, turned, total_tokens)
    slab = jnp.dot(turned, rows, preferred_element_type=F32)
    slab = jnp.where(member == 0, slab, jnp.roll(slab, half, axis=0))
    return lax.psum_scatter(slab, "dp", scatter_dimension=0, tiled=True) / total_tokens


def solution(mesh):
    assert mesh.shape["expert"] == 2
    in_specs = (
        P(("groups", "dp"), None),
        P(("groups", "dp"), None),
        P(("groups", "dp", "expert"), None),
    )
    out_specs = P(("groups", "dp"), "expert")
    return jax.shard_map(
        per_device, mesh=mesh, in_specs=in_specs, out_specs=out_specs, check_vma=False
    )
```

```python
import functools

import jax
import jax.numpy as jnp
import numpy as np
from jax import lax
from jax.experimental import pallas as pl
from jax.experimental.pallas import tpu as pltpu
from jax.sharding import PartitionSpec as P

EXPERTS = 8
CAP = 384
BATCH = 48
WINDOW = 64
SNAKE = (0, 2, 4, 6, 7, 5, 3, 1)
F32, BF16, I32 = jnp.float32, jnp.bfloat16, jnp.int32


def plan_tokens(ids_ref, gates_ref, pick_ref, starts_ref, coef_ref):
    tokens = ids_ref.shape[1]
    local = EXPERTS // 2
    lanes = lax.broadcasted_iota(I32, (tokens, 128), 1)
    rows = jnp.concatenate([ids_ref[...].astype(F32), gates_ref[...], jnp.zeros((4, tokens), F32)], axis=0).T
    ids = [rows[:, k : k + 1].astype(I32) for k in range(2)]
    gates = [rows[:, k : k + 1] for k in (2, 3)]
    hits = [ids[k] == lanes for k in range(2)]
    named = jnp.where(hits[0] | hits[1], 1.0, 0.0).astype(BF16)
    earlier = jnp.where(
        lax.broadcasted_iota(I32, (tokens, tokens), 1) < lax.broadcasted_iota(I32, (tokens, tokens), 0), 1.0, 0.0
    ).astype(BF16)
    before = jnp.dot(earlier, named, preferred_element_type=F32)

    slots = [ids[k] - lax.axis_index("expert") * local for k in range(2)]
    here = [jnp.where((slots[k] >= 0) & (slots[k] < local), 1.0, 0.0) for k in range(2)]
    both = here[0] * here[1]
    neither = (1.0 - here[0]) * (1.0 - here[1])
    mixed = 1.0 - both - neither
    weights = [here[k] * jnp.where(both > 0.5, gates[k], 1.0) for k in range(2)]
    ours = here[0] * gates[0] + here[1] * gates[1]
    theirs = (1.0 - here[0]) * gates[0] + (1.0 - here[1]) * gates[1]
    ours = jnp.where(mixed > 0.5, ours, both)
    theirs = jnp.where(mixed > 0.5, theirs, neither)
    coef_ref[...] = jnp.where(
        lanes == 0, weights[0], jnp.where(lanes == 1, weights[1], jnp.where(lanes == 2, ours, theirs))
    )

    columns = lax.broadcasted_iota(I32, (BATCH, local * WINDOW), 1)
    for b in range(tokens // BATCH):
        rows = slice(b * BATCH, (b + 1) * BATCH)
        start = before[b * BATCH : b * BATCH + 1, :].astype(I32)
        start = jnp.minimum((start >> 4) << 4, CAP - WINDOW)
        starts_ref[b : b + 1, :] = start
        ahead = before[rows] - start.astype(F32)
        for k in range(2):
            offset = jnp.sum(jnp.where(hits[k][rows], ahead, 0.0), axis=1, keepdims=True).astype(I32)
            at = jnp.where(here[k][rows] > 0.5, slots[k][rows] * WINDOW + offset, -1)
            pick_ref[(2 * b + k) * BATCH : (2 * b + k + 1) * BATCH, :] = jnp.where(columns == at, 1.0, 0.0).astype(BF16)


def pick_kernel(first, *refs):
    if first:
        ids_hbm, gates_hbm, rows_ref, out_ref, pick_ref, starts_ref, coef_ref = refs[:7]
        held, in_sems, starts, ids_ref, gates_ref, small_sems = refs[7:]
    else:
        starts, pick_ref, coef_ref, rows_ref, out_ref, held, in_sems = refs
    tokens, width = out_ref.shape
    tiles, _, tile = held.shape
    local = EXPERTS // 2
    member = lax.axis_index("expert")
    base = (1 - member if first else member) * width

    if first:
        small = [
            pltpu.make_async_copy(ids_hbm, ids_ref, small_sems.at[0]),
            pltpu.make_async_copy(gates_hbm, gates_ref, small_sems.at[1]),
        ]
        for copy in small:
            copy.start()
    loads = []
    for j in range(tiles):
        at = pl.ds(pl.multiple_of(base + j * tile, 128), tile)
        loads.append(pltpu.make_async_copy(rows_ref.at[:, at], held.at[j], in_sems.at[j]))
        loads[-1].start()
    if first:
        for copy in small:
            copy.wait()
        plan_tokens(ids_ref, gates_ref, pick_ref, starts_ref, coef_ref)
        copy = pltpu.make_async_copy(starts_ref, starts, small_sems.at[2])
        copy.start()
        copy.wait()
    for j in range(tiles):
        loads[j].wait()
        for b in range(tokens // BATCH):
            windows = []
            for k in range(local):
                at = k * CAP + starts[b, member * local + k]
                windows.append(held[j, pl.ds(pl.multiple_of(at, 16), WINDOW), :])
            picked = jnp.dot(
                pick_ref[2 * b * BATCH : 2 * (b + 1) * BATCH, :],
                jnp.concatenate(windows, axis=0),
                preferred_element_type=F32,
            )
            rows = slice(b * BATCH, (b + 1) * BATCH)
            total = coef_ref[rows, 0:1] * picked[:BATCH] + coef_ref[rows, 1:2] * picked[BATCH:]
            out_ref[rows, j * tile : (j + 1) * tile] = total.astype(BF16)


def pick_half(args, rows, tokens, width, first, tile=512):
    tiles = width // tile
    depth = EXPERTS // 2 * WINDOW
    any_, vmem = pl.BlockSpec(memory_space=pl.ANY), pl.BlockSpec(memory_space=pltpu.VMEM)
    in_hbm = lambda x: pltpu.with_memory_space_constraint(x, pltpu.HBM)
    out_shape = [jax.ShapeDtypeStruct((tokens, width), BF16)]
    scratch = [pltpu.VMEM((tiles, rows.shape[0], tile), BF16), pltpu.SemaphoreType.DMA((tiles,))]
    if first:
        out_shape += [
            jax.ShapeDtypeStruct((2 * tokens, depth), BF16),
            jax.ShapeDtypeStruct((tokens // BATCH, 128), I32),
            jax.ShapeDtypeStruct((tokens, 128), F32),
        ]
        args = [in_hbm(x) for x in args]
        in_specs = [any_] * 3
        scratch += [
            pltpu.SMEM((tokens // BATCH, 128), I32),
            pltpu.VMEM((2, tokens), I32),
            pltpu.VMEM((2, tokens), F32),
            pltpu.SemaphoreType.DMA((3,)),
        ]
    else:
        in_specs = [pl.BlockSpec(memory_space=pltpu.SMEM), vmem, vmem, any_]
    return pl.pallas_call(
        functools.partial(pick_kernel, first),
        out_shape=out_shape,
        in_specs=in_specs,
        out_specs=[vmem] * len(out_shape),
        scratch_shapes=scratch,
        cost_estimate=pl.CostEstimate(
            flops=4 * tokens * depth * width, bytes_accessed=2 * (rows.shape[0] + tokens) * width, transcendentals=0
        ),
        compiler_params=pltpu.CompilerParams(vmem_limit_bytes=24 << 20),
        name="pick_first" if first else "pick_second",
    )(*args, in_hbm(rows))


def merge_kernel(first, tile, pieces, coef_ref, *refs):
    tokens = coef_ref.shape[0]
    sides = []
    for count in pieces:
        sides.append([ref.at[:, j : j + tile] for ref in refs[:count] for j in range(0, ref.shape[1], tile)])
        refs = refs[count:]
    width = len(sides[0]) * tile
    ours = jnp.broadcast_to(coef_ref[:, 2:3], (tokens, tile))
    theirs = jnp.broadcast_to(coef_ref[:, 3:4], (tokens, tile))
    for j, (a, b) in enumerate(zip(*sides)):
        total = (ours * a[...].astype(F32) + theirs * b[...].astype(F32)).astype(BF16)
        if first:
            refs[0][:, j * tile : (j + 1) * tile] = total
            refs[-1][j * tile : (j + 1) * tile, :] = total.T
        else:
            refs[-1][width + j * tile : width + (j + 1) * tile, :] = total.T


def merge(coef, ours, theirs, width, turned=None, tile=256):
    tokens = coef.shape[0]
    first = turned is None
    vmem = pl.BlockSpec(memory_space=pltpu.VMEM)
    args = [coef, *ours, *theirs] + ([] if first else [turned])
    out_shape = [jax.ShapeDtypeStruct((2 * width, tokens), BF16)]
    if first:
        out_shape.insert(0, jax.ShapeDtypeStruct((tokens, width), BF16))
    return pl.pallas_call(
        functools.partial(merge_kernel, first, tile, (len(ours), len(theirs))),
        out_shape=out_shape,
        in_specs=[vmem] * len(args),
        out_specs=[vmem] * len(out_shape),
        input_output_aliases={} if first else {len(args) - 1: 0},
        compiler_params=pltpu.CompilerParams(vmem_limit_bytes=24 << 20),
        cost_estimate=pl.CostEstimate(flops=4 * tokens * width, bytes_accessed=0, transcendentals=0),
        name="merge_first" if first else "merge_second",
    )(*args)


def my_row():
    return lax.axis_index("dp") * 2 + lax.axis_index("expert")


def blocks_kernel(pieces, width, table, turned_ref, mine_ref, *refs):
    third = width // 3
    me = my_row()
    for n, (x, out_ref) in enumerate(zip(pieces, refs[-len(pieces) :])):
        tall = out_ref.shape[0]
        row, column, strip, strip_column, diagonal = [table[me, FIELDS * n + k] for k in range(FIELDS)]

        def part(out_ref, at, lane, first_row, rows, first_column, columns):
            down = pl.ds(pl.multiple_of(first_row, STRIP), rows)
            along = pl.ds(pl.multiple_of(first_column, 128), columns)
            block = jnp.dot(turned_ref[down, :], mine_ref[:, along], preferred_element_type=F32)
            out_ref[at : at + rows, lane : lane + columns] = block.astype(out_ref.dtype)

        @pl.when(diagonal == 0 if x == 0 else True)
        def _(o=out_ref, r=row * width, c=column * width, s=strip * STRIP, sc=strip_column * width, tall=tall):
            part(o, 0, 0, r, width, c, width)
            part(o, width, 0, s, tall - width, sc, width)

        if x == 0:

            @pl.when(diagonal == 1)
            def _(o=out_ref, r=row * width, c=column * width, s=strip * STRIP, sc=strip_column * width, tall=tall):
                part(o, 0, 0, r, third, c, width)
                part(o, third, 0, r + third, third, c + third, 2 * third)
                part(o, third, 2 * third, r + 2 * third, third, c + 2 * third, third)
                part(o, 2 * third, 0, s, tall - 2 * third, sc, width)


def moment_blocks(table, pieces, turned, mine, width, dtype, name, after=()):
    count = len(pieces)
    smem, vmem, any_ = [pl.BlockSpec(memory_space=m) for m in (pltpu.SMEM, pltpu.VMEM, pl.ANY)]
    piece = (width + STRIP, width)
    return pl.pallas_call(
        functools.partial(blocks_kernel, pieces, width),
        out_shape=[jax.ShapeDtypeStruct(piece, dtype)] * count,
        in_specs=[smem, vmem, vmem] + [any_] * len(after),
        out_specs=[vmem] * count,
        cost_estimate=pl.CostEstimate(
            flops=count * mine.shape[0] * width * width,
            bytes_accessed=0,
            transcendentals=0,
        ),
        compiler_params=pltpu.CompilerParams(vmem_limit_bytes=24 << 20),
        name=name,
    )(table, turned, mine, *after)


STRIP = 32
FIELDS = 5


def is_diagonal(b, e):
    return b // 4 == e


def owned_columns(b, e):
    shift = 0 if is_diagonal(b, e) or e == 1 else 1
    return [(b + shift) % 4, (b + shift + 1) % 4]


def leads(b):
    return b % 4 < 2


def fourth_column(b, e):
    if is_diagonal(b, e):
        return (b + 2) % 4
    return (b + 3) % 4 if e == 1 else b % 4


ROUNDS = (
    ((0, 4), (1, 4), (1, 3), (0, 5)),
    ((0, 3), (1, 5), (1, 2), (0, 6)),
    ((0, 2), (1, 6), (1, 1), (0, 7)),
    ((0, 1), (1, 7), (0, 0), (1, 0)),
)


def job_table(which, width):
    table = np.zeros((8, 2, len(which), FIELDS), np.int32)
    for p, b in enumerate(SNAKE):
        for e in range(2):
            for n, (x, t) in enumerate(which):
                q = SNAKE[(p + t) % 8]
                row, column = q % 4 + (0 if q // 4 == e else 4), owned_columns(q, e)[x]
                if is_diagonal(q, e):
                    lead, other = (q % 4, (q + 2) % 4) if leads(q) else ((q + 2) % 4, q % 4)
                    first = lead * width + (0 if leads(q) else width // 2) + x * (width // 3 + STRIP)
                else:
                    first, other = row * width + x * STRIP, fourth_column(q, e)
                table[b, e, n] = (row, column, first // STRIP, other, is_diagonal(q, e))
    return table.reshape(16, -1)


def ring_perm(direction):
    pairs = [(SNAKE[p], SNAKE[(p + direction) % 8]) for p in range(8)]
    return [(a * 2 + e, b * 2 + e) for a, b in pairs for e in range(2)]


def mirror_perms():
    one, other = [], []
    for b in range(8):
        for e in range(2):
            here = b * 2 + e
            if is_diagonal(b, e):
                one.append((here, (b // 4 * 4 + (b + 1) % 4) * 2 + e))
                other.append((here, (b // 4 * 4 + (b + 2) % 4) * 2 + e))
            elif e == 1:
                other.append((here, (4 + b) * 2))
                one.append((here, (4 + (b + 1) % 4) * 2))
            else:
                other.append((here, (b + 1) % 4 * 2 + 1))
                one.append((here, (b + 2) % 4 * 2 + 1))
    return one, other


def place_table():
    table = np.zeros((8, 2, 5), np.int32)
    for b in range(8):
        for e in range(2):
            diagonal = is_diagonal(b, e)
            mirrored = (b + 2) % 4 if not diagonal and e == 1 else (b + 3) % 4
            kind = (1 if leads(b) else 2) if diagonal else 0
            table[b, e] = (*owned_columns(b, e), mirrored, fourth_column(b, e), kind)
    return table


def total(own, right, left, rows):
    return own[rows, :] + right[rows, :].astype(F32) + left[rows, :].astype(F32)


def outgoing_kernel(scale, place, own0, own1, right0, left1, right1, left0, one, other, share):
    width = one.shape[0]
    third, half = width // 3, width // 2
    tall = width + STRIP
    kind = place[my_row(), 4]
    one[...] = (total(own1, right1, left1, slice(0, width)) * scale).astype(BF16)
    tail = total(own1, right1, left1, slice(width, tall)) * scale

    @pl.when(kind == 0)
    def _():
        share[:STRIP, :] = total(own0, right0, left0, slice(width, tall)) * scale
        share[STRIP : 2 * STRIP, :] = tail
        share[2 * STRIP :, :] = jnp.zeros((half - 2 * STRIP, width), F32)
        turned = (total(own0, right0, left0, slice(0, width)) * scale).T
        other[...] = turned[2 * STRIP :, :].astype(BF16)

    @pl.when(kind > 0)
    def _():
        share[: half - STRIP, :] = total(own0, right0, left0, slice(2 * third, tall)) * scale
        share[half - STRIP :, :] = tail
        other[:half, :] = share[...].astype(BF16)
        other[half:, :] = jnp.zeros((width - 2 * STRIP - half, width), BF16)


def put(place, n, made, out_ref, sem):
    width = made.shape[0]
    at = pl.ds(pl.multiple_of(place[my_row(), n] * width, 128), width)
    return pltpu.make_async_copy(made, out_ref.at[:, at], sem)


def own_kernel(scale, place, own0, own1, right0, left1, right1, left0, out_ref, made, sems):
    width = made.shape[1]
    third = width // 3
    made[1] = total(own1, right1, left1, slice(0, width)) * scale
    copies = [put(place, n, made.at[n], out_ref, sems.at[n]) for n in range(2)]
    copies[1].start()

    @pl.when(place[my_row(), 4] == 0)
    def _():
        made[0] = total(own0, right0, left0, slice(0, width)) * scale

    @pl.when(place[my_row(), 4] > 0)
    def _():
        tiles = total(own0, right0, left0, slice(0, 2 * third)) * scale
        upper = {(0, 0): (0, 0), (0, 1): (0, 1), (0, 2): (0, 2), (1, 1): (1, 0), (1, 2): (1, 1), (2, 2): (1, 2)}
        for (i, j), (r, c) in upper.items():
            tile = tiles[r * third : (r + 1) * third, c * third : (c + 1) * third]
            made[0, i * third : (i + 1) * third, j * third : (j + 1) * third] = tile
            if i != j:
                made[0, j * third : (j + 1) * third, i * third : (i + 1) * third] = tile.T

    copies[0].start()
    for copy in copies:
        copy.wait()


def one_kernel(place, one, result_ref, out_ref, made, sem):
    made[...] = one[...].astype(F32).T
    copy = put(place, 2, made, out_ref, sem)
    copy.start()
    copy.wait()


def other_kernel(place, share, other, result_ref, out_ref, made, sem):
    kind = place[my_row(), 4]
    half = share.shape[0]

    @pl.when(kind == 0)
    def _():
        made[: 2 * STRIP, :] = share[: 2 * STRIP, :]
        made[2 * STRIP :, :] = other[...].astype(F32)

    @pl.when(kind == 1)
    def _():
        made[:half, :] = share[...]
        made[half:, :] = other[:half, :].astype(F32)

    @pl.when(kind == 2)
    def _():
        made[...] = jnp.concatenate([other[:half, :].astype(F32), share[...]], axis=0).T

    copy = put(place, 3, made, out_ref, sem)
    copy.start()
    copy.wait()


def symmetric_moment(mine, turned, total_tokens):
    width = mine.shape[1] // 4
    both = ("dp", "expert")
    blocks = {}

    def compute(which, name, dtype, after=()):
        table = jnp.asarray(job_table(which, width))
        pieces = tuple(x for x, _ in which)
        blocks.update(zip(which, moment_blocks(table, pieces, turned, mine, width, dtype, name, after)))

    def hop(value, key):
        return lax.ppermute(value, both, ring_perm(1 if key[1] <= (4 if key[0] == 0 else 3) else -1))

    compute(ROUNDS[0][:2], "blocks0", BF16)
    compute(ROUNDS[0][2:], "blocks0b", BF16, after=(blocks[0, 4],))
    moving = {key: blocks[key] for key in ROUNDS[0]}
    arrived = {}
    before = ()
    for n in range(4):
        landed = {}
        for key in ROUNDS[n]:
            if key in moving:
                landed[key] = hop(moving[key], key)
        if n < 3:
            early = [landed[key] for key in ROUNDS[n][:2]]
            compute(ROUNDS[n + 1][:2], f"blocks{n + 1}", F32, after=(blocks[ROUNDS[n][3]], *before))
            compute(ROUNDS[n + 1][2:], f"blocks{n + 1}b", F32, after=early[:1])
            before = early
        moving = {}
        for (x, t), value in landed.items():
            rightwards = t <= (4 if x == 0 else 3)
            t = t - 1 if rightwards else (t + 1) % 8
            if t == 0:
                arrived[x, rightwards] = value
            else:
                moving[x, t] = (value.astype(F32) + blocks[x, t]).astype(BF16)

    place = jnp.asarray(place_table().reshape(16, -1))
    smem, vmem, any_ = [pl.BlockSpec(memory_space=m) for m in (pltpu.SMEM, pltpu.VMEM, pl.ANY)]
    result = jax.ShapeDtypeStruct((width, 4 * width), F32)
    params = pltpu.CompilerParams(vmem_limit_bytes=24 << 20)
    sums = (blocks[0, 0], blocks[1, 0], arrived[0, True], arrived[1, False], arrived[1, True], arrived[0, False])
    scale = 1.0 / total_tokens
    one, other, share = pl.pallas_call(
        functools.partial(outgoing_kernel, scale),
        out_shape=[
            jax.ShapeDtypeStruct((width, width), BF16),
            jax.ShapeDtypeStruct((width - 2 * STRIP, width), BF16),
            jax.ShapeDtypeStruct((width // 2, width), F32),
        ],
        in_specs=[smem] + [vmem] * 6,
        out_specs=[vmem] * 3,
        compiler_params=params,
        name="outgoing",
    )(place, *sums)
    perm_one, perm_other = mirror_perms()
    one = lax.ppermute(one, both, perm_one)
    other = lax.ppermute(other, both, perm_other)
    partial_result = pl.pallas_call(
        functools.partial(own_kernel, scale),
        out_shape=result,
        in_specs=[smem] + [vmem] * 6,
        out_specs=any_,
        scratch_shapes=[pltpu.VMEM((2, width, width), F32), pltpu.SemaphoreType.DMA((2,))],
        compiler_params=params,
        name="own",
    )(place, *sums)
    for kernel, args, name in ((one_kernel, (one,), "one"), (other_kernel, (share, other), "other")):
        partial_result = pl.pallas_call(
            kernel,
            out_shape=result,
            in_specs=[smem] + [vmem] * len(args) + [any_],
            out_specs=any_,
            scratch_shapes=[pltpu.VMEM((width, width), F32), pltpu.SemaphoreType.DMA],
            input_output_aliases={len(args) + 1: 0},
            compiler_params=params,
            name=name,
        )(place, *args, partial_result)
    return partial_result


def per_device(expert_ids, gates, expert_out):
    tokens, channels = expert_ids.shape[0], expert_out.shape[1]
    dp_size = lax.axis_size("dp")
    member = lax.axis_index("expert")
    half = channels // 2
    swap = [(0, 1), (1, 0)]

    sent, pick, starts, coef = pick_half((expert_ids.T, gates.T), expert_out, tokens, half, True)
    from_peer = lax.ppermute(sent, "expert", swap)
    (kept,) = pick_half((starts, pick, coef), expert_out, tokens, half, False)
    from_peer_too = lax.ppermute(kept, "expert", swap)
    rows, turned = merge(coef, [kept], [from_peer], half)
    (turned,) = merge(coef, [sent], [from_peer_too], half, turned)

    total_tokens = tokens * dp_size
    if dp_size == 8 and channels == 8 * 384:
        return symmetric_moment(rows, turned, total_tokens)
    slab = jnp.dot(turned, rows, preferred_element_type=F32)
    slab = jnp.where(member == 0, slab, jnp.roll(slab, half, axis=0))
    return lax.psum_scatter(slab, "dp", scatter_dimension=0, tiled=True) / total_tokens


def solution(mesh):
    assert mesh.shape["expert"] == 2
    in_specs = (
        P(("groups", "dp"), None),
        P(("groups", "dp"), None),
        P(("groups", "dp", "expert"), None),
    )
    out_specs = P(("groups", "dp"), "expert")
    return jax.shard_map(
        per_device, mesh=mesh, in_specs=in_specs, out_specs=out_specs, check_vma=False
    )
```

```python
import functools

import jax
import jax.numpy as jnp
import numpy as np
from jax import lax
from jax.experimental import pallas as pl
from jax.experimental.pallas import tpu as pltpu
from jax.sharding import PartitionSpec as P

EXPERTS = 8
CAP = 384
BATCH = 48
WINDOW = 64
SNAKE = (0, 2, 4, 6, 7, 5, 3, 1)
F32, BF16, I32 = jnp.float32, jnp.bfloat16, jnp.int32


def plan_tokens(ids_ref, gates_ref, pick_ref, starts_ref, coef_ref, starts_copy):
    tokens = ids_ref.shape[1]
    local = EXPERTS // 2
    lanes = lax.broadcasted_iota(I32, (tokens, 128), 1)
    rows = jnp.concatenate([ids_ref[...].astype(F32), gates_ref[...], jnp.zeros((4, tokens), F32)], axis=0).T
    ids = [rows[:, k : k + 1].astype(I32) for k in range(2)]
    gates = [rows[:, k : k + 1] for k in (2, 3)]
    hits = [ids[k] == lanes for k in range(2)]
    named = jnp.where(hits[0] | hits[1], 1.0, 0.0).astype(BF16)
    earlier = jnp.where(
        lax.broadcasted_iota(I32, (tokens, tokens), 1) < lax.broadcasted_iota(I32, (tokens, tokens), 0), 1.0, 0.0
    ).astype(BF16)
    before = jnp.dot(earlier, named, preferred_element_type=F32)
    firsts = []
    for b in range(tokens // BATCH):
        start = before[b * BATCH : b * BATCH + 1, :].astype(I32)
        firsts.append(jnp.minimum((start >> 4) << 4, CAP - WINDOW))
        starts_ref[b : b + 1, :] = firsts[-1]
    starts_copy.start()

    slots = [ids[k] - lax.axis_index("expert") * local for k in range(2)]
    here = [jnp.where((slots[k] >= 0) & (slots[k] < local), 1.0, 0.0) for k in range(2)]
    both = here[0] * here[1]
    neither = (1.0 - here[0]) * (1.0 - here[1])
    mixed = 1.0 - both - neither
    weights = [here[k] * jnp.where(both > 0.5, gates[k], 1.0) for k in range(2)]
    ours = here[0] * gates[0] + here[1] * gates[1]
    theirs = (1.0 - here[0]) * gates[0] + (1.0 - here[1]) * gates[1]
    ours = jnp.where(mixed > 0.5, ours, both)
    theirs = jnp.where(mixed > 0.5, theirs, neither)
    coef_ref[...] = jnp.where(
        lanes == 0, weights[0], jnp.where(lanes == 1, weights[1], jnp.where(lanes == 2, ours, theirs))
    )

    columns = lax.broadcasted_iota(I32, (BATCH, local * WINDOW), 1)
    for b in range(tokens // BATCH):
        rows = slice(b * BATCH, (b + 1) * BATCH)
        ahead = before[rows] - firsts[b].astype(F32)
        for k in range(2):
            offset = jnp.sum(jnp.where(hits[k][rows], ahead, 0.0), axis=1, keepdims=True).astype(I32)
            at = jnp.where(here[k][rows] > 0.5, slots[k][rows] * WINDOW + offset, -1)
            pick_ref[(2 * b + k) * BATCH : (2 * b + k + 1) * BATCH, :] = jnp.where(columns == at, 1.0, 0.0).astype(BF16)


def pick_kernel(first, *refs):
    if first:
        ids_hbm, gates_hbm, rows_ref, out_ref, pick_ref, starts_ref, coef_ref = refs[:7]
        held, in_sems, starts, ids_ref, gates_ref, small_sems = refs[7:]
    else:
        starts, pick_ref, coef_ref, rows_ref, out_ref, held, in_sems = refs
    tokens, width = out_ref.shape
    tiles, _, tile = held.shape
    local = EXPERTS // 2
    member = lax.axis_index("expert")
    base = (1 - member if first else member) * width

    if first:
        small = [
            pltpu.make_async_copy(ids_hbm, ids_ref, small_sems.at[0]),
            pltpu.make_async_copy(gates_hbm, gates_ref, small_sems.at[1]),
        ]
        for copy in small:
            copy.start()
    loads = []
    for j in range(tiles):
        at = pl.ds(pl.multiple_of(base + j * tile, 128), tile)
        loads.append(pltpu.make_async_copy(rows_ref.at[:, at], held.at[j], in_sems.at[j]))
        loads[-1].start()
    if first:
        for copy in small:
            copy.wait()
        copy = pltpu.make_async_copy(starts_ref, starts, small_sems.at[2])
        plan_tokens(ids_ref, gates_ref, pick_ref, starts_ref, coef_ref, copy)
        copy.wait()
    for j in range(tiles):
        loads[j].wait()
        for b in range(tokens // BATCH):
            windows = []
            for k in range(local):
                at = k * CAP + starts[b, member * local + k]
                windows.append(held[j, pl.ds(pl.multiple_of(at, 16), WINDOW), :])
            picked = jnp.dot(
                pick_ref[2 * b * BATCH : 2 * (b + 1) * BATCH, :],
                jnp.concatenate(windows, axis=0),
                preferred_element_type=F32,
            )
            rows = slice(b * BATCH, (b + 1) * BATCH)
            total = coef_ref[rows, 0:1] * picked[:BATCH] + coef_ref[rows, 1:2] * picked[BATCH:]
            out_ref[rows, j * tile : (j + 1) * tile] = total.astype(BF16)


def pick_half(args, rows, tokens, width, first, tile=512):
    tiles = width // tile
    depth = EXPERTS // 2 * WINDOW
    any_, vmem = pl.BlockSpec(memory_space=pl.ANY), pl.BlockSpec(memory_space=pltpu.VMEM)
    in_hbm = lambda x: pltpu.with_memory_space_constraint(x, pltpu.HBM)
    out_shape = [jax.ShapeDtypeStruct((tokens, width), BF16)]
    scratch = [pltpu.VMEM((tiles, rows.shape[0], tile), BF16), pltpu.SemaphoreType.DMA((tiles,))]
    if first:
        out_shape += [
            jax.ShapeDtypeStruct((2 * tokens, depth), BF16),
            jax.ShapeDtypeStruct((tokens // BATCH, 128), I32),
            jax.ShapeDtypeStruct((tokens, 128), F32),
        ]
        args = [in_hbm(x) for x in args]
        in_specs = [any_] * 3
        scratch += [
            pltpu.SMEM((tokens // BATCH, 128), I32),
            pltpu.VMEM((2, tokens), I32),
            pltpu.VMEM((2, tokens), F32),
            pltpu.SemaphoreType.DMA((3,)),
        ]
    else:
        in_specs = [pl.BlockSpec(memory_space=pltpu.SMEM), vmem, vmem, any_]
    return pl.pallas_call(
        functools.partial(pick_kernel, first),
        out_shape=out_shape,
        in_specs=in_specs,
        out_specs=[vmem] * len(out_shape),
        scratch_shapes=scratch,
        cost_estimate=pl.CostEstimate(
            flops=4 * tokens * depth * width, bytes_accessed=2 * (rows.shape[0] + tokens) * width, transcendentals=0
        ),
        compiler_params=pltpu.CompilerParams(vmem_limit_bytes=24 << 20),
        name="pick_first" if first else "pick_second",
    )(*args, in_hbm(rows))


def merge_kernel(first, tile, pieces, coef_ref, *refs):
    tokens = coef_ref.shape[0]
    sides = []
    for count in pieces:
        sides.append([ref.at[:, j : j + tile] for ref in refs[:count] for j in range(0, ref.shape[1], tile)])
        refs = refs[count:]
    width = len(sides[0]) * tile
    ours = jnp.broadcast_to(coef_ref[:, 2:3], (tokens, tile))
    theirs = jnp.broadcast_to(coef_ref[:, 3:4], (tokens, tile))
    for j, (a, b) in enumerate(zip(*sides)):
        total = (ours * a[...].astype(F32) + theirs * b[...].astype(F32)).astype(BF16)
        if first:
            refs[0][:, j * tile : (j + 1) * tile] = total
            refs[-1][j * tile : (j + 1) * tile, :] = total.T
        else:
            refs[-1][width + j * tile : width + (j + 1) * tile, :] = total.T


def merge(coef, ours, theirs, width, turned=None, tile=256):
    tokens = coef.shape[0]
    first = turned is None
    vmem = pl.BlockSpec(memory_space=pltpu.VMEM)
    args = [coef, *ours, *theirs] + ([] if first else [turned])
    out_shape = [jax.ShapeDtypeStruct((2 * width, tokens), BF16)]
    if first:
        out_shape.insert(0, jax.ShapeDtypeStruct((tokens, width), BF16))
    return pl.pallas_call(
        functools.partial(merge_kernel, first, tile, (len(ours), len(theirs))),
        out_shape=out_shape,
        in_specs=[vmem] * len(args),
        out_specs=[vmem] * len(out_shape),
        input_output_aliases={} if first else {len(args) - 1: 0},
        compiler_params=pltpu.CompilerParams(vmem_limit_bytes=24 << 20),
        cost_estimate=pl.CostEstimate(flops=4 * tokens * width, bytes_accessed=0, transcendentals=0),
        name="merge_first" if first else "merge_second",
    )(*args)


def my_row():
    return lax.axis_index("dp") * 2 + lax.axis_index("expert")


def blocks_kernel(pieces, width, table, turned_ref, mine_ref, *refs):
    third = width // 3
    me = my_row()
    for n, (x, out_ref) in enumerate(zip(pieces, refs[-len(pieces) :])):
        tall = out_ref.shape[0]
        row, column, strip, strip_column, diagonal = [table[me, FIELDS * n + k] for k in range(FIELDS)]

        def part(out_ref, at, lane, first_row, rows, first_column, columns):
            down = pl.ds(pl.multiple_of(first_row, STRIP), rows)
            along = pl.ds(pl.multiple_of(first_column, 128), columns)
            block = jnp.dot(turned_ref[down, :], mine_ref[:, along], preferred_element_type=F32)
            out_ref[at : at + rows, lane : lane + columns] = block.astype(out_ref.dtype)

        @pl.when(diagonal == 0 if x == 0 else True)
        def _(o=out_ref, r=row * width, c=column * width, s=strip * STRIP, sc=strip_column * width, tall=tall):
            part(o, 0, 0, r, width, c, width)
            part(o, width, 0, s, tall - width, sc, width)

        if x == 0:

            @pl.when(diagonal == 1)
            def _(o=out_ref, r=row * width, c=column * width, s=strip * STRIP, sc=strip_column * width, tall=tall):
                part(o, 0, 0, r, third, c, width)
                part(o, third, 0, r + third, third, c + third, 2 * third)
                part(o, third, 2 * third, r + 2 * third, third, c + 2 * third, third)
                part(o, 2 * third, 0, s, tall - 2 * third, sc, width)


def moment_blocks(table, pieces, turned, mine, width, dtype, name, after=()):
    count = len(pieces)
    smem, vmem, any_ = [pl.BlockSpec(memory_space=m) for m in (pltpu.SMEM, pltpu.VMEM, pl.ANY)]
    piece = (width + STRIP, width)
    return pl.pallas_call(
        functools.partial(blocks_kernel, pieces, width),
        out_shape=[jax.ShapeDtypeStruct(piece, dtype)] * count,
        in_specs=[smem, vmem, vmem] + [any_] * len(after),
        out_specs=[vmem] * count,
        cost_estimate=pl.CostEstimate(
            flops=count * mine.shape[0] * width * width,
            bytes_accessed=0,
            transcendentals=0,
        ),
        compiler_params=pltpu.CompilerParams(vmem_limit_bytes=24 << 20),
        name=name,
    )(table, turned, mine, *after)


STRIP = 32
FIELDS = 5


def is_diagonal(b, e):
    return b // 4 == e


def owned_columns(b, e):
    shift = 0 if is_diagonal(b, e) or e == 1 else 1
    return [(b + shift) % 4, (b + shift + 1) % 4]


def leads(b):
    return b % 4 < 2


def fourth_column(b, e):
    if is_diagonal(b, e):
        return (b + 2) % 4
    return (b + 3) % 4 if e == 1 else b % 4


ROUNDS = (
    ((0, 4), (1, 4), (1, 3), (0, 5)),
    ((0, 3), (1, 5), (1, 2), (0, 6)),
    ((0, 2), (1, 6), (1, 1), (0, 7)),
    ((0, 1), (1, 7), (0, 0), (1, 0)),
)


def job_table(which, width):
    table = np.zeros((8, 2, len(which), FIELDS), np.int32)
    for p, b in enumerate(SNAKE):
        for e in range(2):
            for n, (x, t) in enumerate(which):
                q = SNAKE[(p + t) % 8]
                row, column = q % 4 + (0 if q // 4 == e else 4), owned_columns(q, e)[x]
                if is_diagonal(q, e):
                    lead, other = (q % 4, (q + 2) % 4) if leads(q) else ((q + 2) % 4, q % 4)
                    first = lead * width + (0 if leads(q) else width // 2) + x * (width // 3 + STRIP)
                else:
                    first, other = row * width + x * STRIP, fourth_column(q, e)
                table[b, e, n] = (row, column, first // STRIP, other, is_diagonal(q, e))
    return table.reshape(16, -1)


def ring_perm(direction):
    pairs = [(SNAKE[p], SNAKE[(p + direction) % 8]) for p in range(8)]
    return [(a * 2 + e, b * 2 + e) for a, b in pairs for e in range(2)]


def mirror_perms():
    one, other = [], []
    for b in range(8):
        for e in range(2):
            here = b * 2 + e
            if is_diagonal(b, e):
                one.append((here, (b // 4 * 4 + (b + 1) % 4) * 2 + e))
                other.append((here, (b // 4 * 4 + (b + 2) % 4) * 2 + e))
            elif e == 1:
                other.append((here, (4 + b) * 2))
                one.append((here, (4 + (b + 1) % 4) * 2))
            else:
                other.append((here, (b + 1) % 4 * 2 + 1))
                one.append((here, (b + 2) % 4 * 2 + 1))
    return one, other


def place_table():
    table = np.zeros((8, 2, 5), np.int32)
    for b in range(8):
        for e in range(2):
            diagonal = is_diagonal(b, e)
            mirrored = (b + 2) % 4 if not diagonal and e == 1 else (b + 3) % 4
            kind = (1 if leads(b) else 2) if diagonal else 0
            table[b, e] = (*owned_columns(b, e), mirrored, fourth_column(b, e), kind)
    return table


def total(own, right, left, rows):
    return own[rows, :] + right[rows, :].astype(F32) + left[rows, :].astype(F32)


def outgoing_one_kernel(scale, own1, right1, left1, one):
    one[...] = (total(own1, right1, left1, slice(0, one.shape[0])) * scale).astype(BF16)


def outgoing_other_kernel(scale, place, own0, own1, right0, left1, right1, left0, after, other, share):
    half, width = share.shape
    third, tall = width // 3, width + STRIP
    kind = place[my_row(), 4]
    tail = total(own1, right1, left1, slice(width, tall)) * scale

    @pl.when(kind == 0)
    def _():
        share[:STRIP, :] = total(own0, right0, left0, slice(width, tall)) * scale
        share[STRIP : 2 * STRIP, :] = tail
        share[2 * STRIP :, :] = jnp.zeros((half - 2 * STRIP, width), F32)
        turned = (total(own0, right0, left0, slice(0, width)) * scale).T
        other[...] = turned[2 * STRIP :, :].astype(BF16)

    @pl.when(kind > 0)
    def _():
        share[: half - STRIP, :] = total(own0, right0, left0, slice(2 * third, tall)) * scale
        share[half - STRIP :, :] = tail
        other[:half, :] = share[...].astype(BF16)
        other[half:, :] = jnp.zeros((width - 2 * STRIP - half, width), BF16)


def put(place, n, made, out_ref, sem):
    width = made.shape[0]
    at = pl.ds(pl.multiple_of(place[my_row(), n] * width, 128), width)
    return pltpu.make_async_copy(made, out_ref.at[:, at], sem)


def own_kernel(scale, place, own0, own1, right0, left1, right1, left0, out_ref, made, sems):
    width = made.shape[1]
    third = width // 3
    made[1] = total(own1, right1, left1, slice(0, width)) * scale
    copies = [put(place, n, made.at[n], out_ref, sems.at[n]) for n in range(2)]
    copies[1].start()

    @pl.when(place[my_row(), 4] == 0)
    def _():
        made[0] = total(own0, right0, left0, slice(0, width)) * scale

    @pl.when(place[my_row(), 4] > 0)
    def _():
        tiles = total(own0, right0, left0, slice(0, 2 * third)) * scale
        upper = {(0, 0): (0, 0), (0, 1): (0, 1), (0, 2): (0, 2), (1, 1): (1, 0), (1, 2): (1, 1), (2, 2): (1, 2)}
        for (i, j), (r, c) in upper.items():
            tile = tiles[r * third : (r + 1) * third, c * third : (c + 1) * third]
            made[0, i * third : (i + 1) * third, j * third : (j + 1) * third] = tile
            if i != j:
                made[0, j * third : (j + 1) * third, i * third : (i + 1) * third] = tile.T

    copies[0].start()
    for copy in copies:
        copy.wait()


def one_kernel(place, one, result_ref, out_ref, made, sem):
    made[...] = one[...].astype(F32).T
    copy = put(place, 2, made, out_ref, sem)
    copy.start()
    copy.wait()


def other_kernel(place, share, other, result_ref, out_ref, made, sem):
    kind = place[my_row(), 4]
    half = share.shape[0]

    @pl.when(kind == 0)
    def _():
        made[: 2 * STRIP, :] = share[: 2 * STRIP, :]
        made[2 * STRIP :, :] = other[...].astype(F32)

    @pl.when(kind == 1)
    def _():
        made[:half, :] = share[...]
        made[half:, :] = other[:half, :].astype(F32)

    @pl.when(kind == 2)
    def _():
        made[...] = jnp.concatenate([other[:half, :].astype(F32), share[...]], axis=0).T

    copy = put(place, 3, made, out_ref, sem)
    copy.start()
    copy.wait()


def symmetric_moment(mine, turned, total_tokens):
    width = mine.shape[1] // 4
    both = ("dp", "expert")
    blocks = {}

    def compute(which, name, dtype, after=()):
        table = jnp.asarray(job_table(which, width))
        pieces = tuple(x for x, _ in which)
        blocks.update(zip(which, moment_blocks(table, pieces, turned, mine, width, dtype, name, after)))

    def hop(value, key):
        return lax.ppermute(value, both, ring_perm(1 if key[1] <= (4 if key[0] == 0 else 3) else -1))

    compute(ROUNDS[0][:2], "blocks0", BF16)
    compute(ROUNDS[0][2:], "blocks0b", BF16, after=(blocks[0, 4],))
    moving = {key: blocks[key] for key in ROUNDS[0]}
    arrived = {}
    before = ()
    for n in range(4):
        landed = {}
        for key in ROUNDS[n]:
            if key in moving:
                landed[key] = hop(moving[key], key)
        if n < 3:
            early = [landed[key] for key in ROUNDS[n][:2]]
            compute(ROUNDS[n + 1][:2], f"blocks{n + 1}", F32, after=(blocks[ROUNDS[n][3]], *before))
            compute(ROUNDS[n + 1][2:], f"blocks{n + 1}b", F32, after=early[:1])
            before = early
        moving = {}
        for (x, t), value in landed.items():
            rightwards = t <= (4 if x == 0 else 3)
            t = t - 1 if rightwards else (t + 1) % 8
            if t == 0:
                arrived[x, rightwards] = value
            else:
                moving[x, t] = (value.astype(F32) + blocks[x, t]).astype(BF16)

    place = jnp.asarray(place_table().reshape(16, -1))
    smem, vmem, any_ = [pl.BlockSpec(memory_space=m) for m in (pltpu.SMEM, pltpu.VMEM, pl.ANY)]
    result = jax.ShapeDtypeStruct((width, 4 * width), F32)
    params = pltpu.CompilerParams(vmem_limit_bytes=24 << 20)
    sums = (blocks[0, 0], blocks[1, 0], arrived[0, True], arrived[1, False], arrived[1, True], arrived[0, False])
    scale = 1.0 / total_tokens
    perm_one, perm_other = mirror_perms()
    one = pl.pallas_call(
        functools.partial(outgoing_one_kernel, scale),
        out_shape=jax.ShapeDtypeStruct((width, width), BF16),
        in_specs=[vmem] * 3,
        out_specs=vmem,
        compiler_params=params,
        name="outgoing_one",
    )(sums[1], sums[4], sums[3])
    other, share = pl.pallas_call(
        functools.partial(outgoing_other_kernel, scale),
        out_shape=[
            jax.ShapeDtypeStruct((width - 2 * STRIP, width), BF16),
            jax.ShapeDtypeStruct((width // 2, width), F32),
        ],
        in_specs=[smem] + [vmem] * 6 + [any_],
        out_specs=[vmem] * 2,
        compiler_params=params,
        name="outgoing_other",
    )(place, *sums, one)
    one = lax.ppermute(one, both, perm_one)
    other = lax.ppermute(other, both, perm_other)
    partial_result = pl.pallas_call(
        functools.partial(own_kernel, scale),
        out_shape=result,
        in_specs=[smem] + [vmem] * 6,
        out_specs=any_,
        scratch_shapes=[pltpu.VMEM((2, width, width), F32), pltpu.SemaphoreType.DMA((2,))],
        compiler_params=params,
        name="own",
    )(place, *sums)
    for kernel, args, name in ((one_kernel, (one,), "one"), (other_kernel, (share, other), "other")):
        partial_result = pl.pallas_call(
            kernel,
            out_shape=result,
            in_specs=[smem] + [vmem] * len(args) + [any_],
            out_specs=any_,
            scratch_shapes=[pltpu.VMEM((width, width), F32), pltpu.SemaphoreType.DMA],
            input_output_aliases={len(args) + 1: 0},
            compiler_params=params,
            name=name,
        )(place, *args, partial_result)
    return partial_result


def per_device(expert_ids, gates, expert_out):
    tokens, channels = expert_ids.shape[0], expert_out.shape[1]
    dp_size = lax.axis_size("dp")
    member = lax.axis_index("expert")
    half = channels // 2
    swap = [(0, 1), (1, 0)]

    sent, pick, starts, coef = pick_half((expert_ids.T, gates.T), expert_out, tokens, half, True)
    from_peer = lax.ppermute(sent, "expert", swap)
    (kept,) = pick_half((starts, pick, coef), expert_out, tokens, half, False)
    from_peer_too = lax.ppermute(kept, "expert", swap)
    rows, turned = merge(coef, [kept], [from_peer], half)
    (turned,) = merge(coef, [sent], [from_peer_too], half, turned)

    total_tokens = tokens * dp_size
    if dp_size == 8 and channels == 8 * 384:
        return symmetric_moment(rows, turned, total_tokens)
    slab = jnp.dot(turned, rows, preferred_element_type=F32)
    slab = jnp.where(member == 0, slab, jnp.roll(slab, half, axis=0))
    return lax.psum_scatter(slab, "dp", scatter_dimension=0, tiled=True) / total_tokens


def solution(mesh):
    assert mesh.shape["expert"] == 2
    in_specs = (
        P(("groups", "dp"), None),
        P(("groups", "dp"), None),
        P(("groups", "dp", "expert"), None),
    )
    out_specs = P(("groups", "dp"), "expert")
    return jax.shard_map(
        per_device, mesh=mesh, in_specs=in_specs, out_specs=out_specs, check_vma=False
    )
```

```python
import functools

import jax
import jax.numpy as jnp
import numpy as np
from jax import lax
from jax.experimental import pallas as pl
from jax.experimental.pallas import tpu as pltpu
from jax.sharding import PartitionSpec as P

EXPERTS = 8
CAP = 384
BATCH = 48
WINDOW = 64
SNAKE = (0, 2, 4, 6, 7, 5, 3, 1)
F32, BF16, I32 = jnp.float32, jnp.bfloat16, jnp.int32


def plan_tokens(ids_ref, gates_ref, pick_ref, starts_ref, coef_ref, earlier_ref, inputs, starts_copy):
    tokens = ids_ref.shape[1]
    local = EXPERTS // 2
    earlier_ref[...] = jnp.where(
        lax.broadcasted_iota(I32, (tokens, tokens), 1) < lax.broadcasted_iota(I32, (tokens, tokens), 0), 1.0, 0.0
    ).astype(BF16)
    for copy in inputs:
        copy.wait()
    lanes = lax.broadcasted_iota(I32, (tokens, 128), 1)
    rows = jnp.concatenate([ids_ref[...].astype(F32), gates_ref[...], jnp.zeros((4, tokens), F32)], axis=0).T
    ids = [rows[:, k : k + 1].astype(I32) for k in range(2)]
    gates = [rows[:, k : k + 1] for k in (2, 3)]
    hits = [ids[k] == lanes for k in range(2)]
    named = jnp.where(hits[0] | hits[1], 1.0, 0.0).astype(BF16)
    before = jnp.dot(earlier_ref[...], named, preferred_element_type=F32)
    firsts = []
    for b in range(tokens // BATCH):
        start = before[b * BATCH : b * BATCH + 1, :].astype(I32)
        firsts.append(jnp.minimum((start >> 4) << 4, CAP - WINDOW))
        starts_ref[b : b + 1, :] = firsts[-1]
    starts_copy.start()

    slots = [ids[k] - lax.axis_index("expert") * local for k in range(2)]
    here = [jnp.where((slots[k] >= 0) & (slots[k] < local), 1.0, 0.0) for k in range(2)]
    both = here[0] * here[1]
    neither = (1.0 - here[0]) * (1.0 - here[1])
    mixed = 1.0 - both - neither
    weights = [here[k] * jnp.where(both > 0.5, gates[k], 1.0) for k in range(2)]
    ours = here[0] * gates[0] + here[1] * gates[1]
    theirs = (1.0 - here[0]) * gates[0] + (1.0 - here[1]) * gates[1]
    ours = jnp.where(mixed > 0.5, ours, both)
    theirs = jnp.where(mixed > 0.5, theirs, neither)
    coef_ref[...] = jnp.where(
        lanes == 0, weights[0], jnp.where(lanes == 1, weights[1], jnp.where(lanes == 2, ours, theirs))
    )

    columns = lax.broadcasted_iota(I32, (BATCH, local * WINDOW), 1)
    for b in range(tokens // BATCH):
        rows = slice(b * BATCH, (b + 1) * BATCH)
        ahead = before[rows] - firsts[b].astype(F32)
        for k in range(2):
            offset = jnp.sum(jnp.where(hits[k][rows], ahead, 0.0), axis=1, keepdims=True).astype(I32)
            at = jnp.where(here[k][rows] > 0.5, slots[k][rows] * WINDOW + offset, -1)
            pick_ref[(2 * b + k) * BATCH : (2 * b + k + 1) * BATCH, :] = jnp.where(columns == at, 1.0, 0.0).astype(BF16)


def pick_kernel(first, *refs):
    if first:
        ids_hbm, gates_hbm, rows_ref, out_ref, pick_ref, starts_ref, coef_ref = refs[:7]
        held, in_sems, starts, small_sems, ids_ref, gates_ref, earlier_ref = refs[7:]
    else:
        starts_ref, pick_ref, coef_ref, rows_ref, out_ref, held, in_sems, starts, small_sems = refs
    tokens, width = out_ref.shape
    tiles, _, tile = held.shape
    local = EXPERTS // 2
    member = lax.axis_index("expert")
    base = (1 - member if first else member) * width

    if first:
        small = [
            pltpu.make_async_copy(ids_hbm, ids_ref, small_sems.at[0]),
            pltpu.make_async_copy(gates_hbm, gates_ref, small_sems.at[1]),
        ]
        for copy in small:
            copy.start()
    loads = []
    for j in range(tiles):
        at = pl.ds(pl.multiple_of(base + j * tile, 128), tile)
        loads.append(pltpu.make_async_copy(rows_ref.at[:, at], held.at[j], in_sems.at[j]))
        loads[-1].start()
    copy = pltpu.make_async_copy(starts_ref, starts, small_sems.at[2])
    if first:
        plan_tokens(ids_ref, gates_ref, pick_ref, starts_ref, coef_ref, earlier_ref, small, copy)
    else:
        copy.start()
    copy.wait()
    for j in range(tiles):
        loads[j].wait()
        for b in range(tokens // BATCH):
            windows = []
            for k in range(local):
                at = k * CAP + starts[b, member * local + k]
                windows.append(held[j, pl.ds(pl.multiple_of(at, 16), WINDOW), :])
            picked = jnp.dot(
                pick_ref[2 * b * BATCH : 2 * (b + 1) * BATCH, :],
                jnp.concatenate(windows, axis=0),
                preferred_element_type=F32,
            )
            rows = slice(b * BATCH, (b + 1) * BATCH)
            total = coef_ref[rows, 0:1] * picked[:BATCH] + coef_ref[rows, 1:2] * picked[BATCH:]
            out_ref[rows, j * tile : (j + 1) * tile] = total.astype(BF16)


def pick_half(args, rows, tokens, width, first, tile=512):
    tiles = width // tile
    depth = EXPERTS // 2 * WINDOW
    any_, vmem = pl.BlockSpec(memory_space=pl.ANY), pl.BlockSpec(memory_space=pltpu.VMEM)
    in_hbm = lambda x: pltpu.with_memory_space_constraint(x, pltpu.HBM)
    out_shape = [jax.ShapeDtypeStruct((tokens, width), BF16)]
    scratch = [
        pltpu.VMEM((tiles, rows.shape[0], tile), BF16),
        pltpu.SemaphoreType.DMA((tiles,)),
        pltpu.SMEM((tokens // BATCH, 128), I32),
        pltpu.SemaphoreType.DMA((3,)),
    ]
    if first:
        out_shape += [
            jax.ShapeDtypeStruct((2 * tokens, depth), BF16),
            jax.ShapeDtypeStruct((tokens // BATCH, 128), I32),
            jax.ShapeDtypeStruct((tokens, 128), F32),
        ]
        args = [in_hbm(x) for x in args]
        in_specs = [any_] * 3
        scratch += [
            pltpu.VMEM((2, tokens), I32),
            pltpu.VMEM((2, tokens), F32),
            pltpu.VMEM((tokens, tokens), BF16),
        ]
    else:
        in_specs = [vmem, vmem, vmem, any_]
    return pl.pallas_call(
        functools.partial(pick_kernel, first),
        out_shape=out_shape,
        in_specs=in_specs,
        out_specs=[vmem] * len(out_shape),
        scratch_shapes=scratch,
        cost_estimate=pl.CostEstimate(
            flops=4 * tokens * depth * width, bytes_accessed=2 * (rows.shape[0] + tokens) * width, transcendentals=0
        ),
        compiler_params=pltpu.CompilerParams(vmem_limit_bytes=24 << 20),
        name="pick_first" if first else "pick_second",
    )(*args, in_hbm(rows))


def merge_kernel(first, tile, pieces, coef_ref, *refs):
    tokens = coef_ref.shape[0]
    sides = []
    for count in pieces:
        sides.append([ref.at[:, j : j + tile] for ref in refs[:count] for j in range(0, ref.shape[1], tile)])
        refs = refs[count:]
    width = len(sides[0]) * tile
    ours = jnp.broadcast_to(coef_ref[:, 2:3], (tokens, tile))
    theirs = jnp.broadcast_to(coef_ref[:, 3:4], (tokens, tile))
    for j, (a, b) in enumerate(zip(*sides)):
        total = (ours * a[...].astype(F32) + theirs * b[...].astype(F32)).astype(BF16)
        if first:
            refs[0][:, j * tile : (j + 1) * tile] = total
            refs[-1][j * tile : (j + 1) * tile, :] = total.T
        else:
            refs[-1][width + j * tile : width + (j + 1) * tile, :] = total.T


def merge(coef, ours, theirs, width, turned=None, tile=256):
    tokens = coef.shape[0]
    first = turned is None
    vmem = pl.BlockSpec(memory_space=pltpu.VMEM)
    args = [coef, *ours, *theirs] + ([] if first else [turned])
    out_shape = [jax.ShapeDtypeStruct((2 * width, tokens), BF16)]
    if first:
        out_shape.insert(0, jax.ShapeDtypeStruct((tokens, width), BF16))
    return pl.pallas_call(
        functools.partial(merge_kernel, first, tile, (len(ours), len(theirs))),
        out_shape=out_shape,
        in_specs=[vmem] * len(args),
        out_specs=[vmem] * len(out_shape),
        input_output_aliases={} if first else {len(args) - 1: 0},
        compiler_params=pltpu.CompilerParams(vmem_limit_bytes=24 << 20),
        cost_estimate=pl.CostEstimate(flops=4 * tokens * width, bytes_accessed=0, transcendentals=0),
        name="merge_first" if first else "merge_second",
    )(*args)


def my_row():
    return lax.axis_index("dp") * 2 + lax.axis_index("expert")


def blocks_kernel(pieces, width, table, turned_ref, mine_ref, *refs):
    third = width // 3
    me = my_row()
    for n, (x, out_ref) in enumerate(zip(pieces, refs[-len(pieces) :])):
        tall = out_ref.shape[0]
        row, column, strip, strip_column, diagonal = [table[me, FIELDS * n + k] for k in range(FIELDS)]

        def part(out_ref, at, lane, first_row, rows, first_column, columns):
            down = pl.ds(pl.multiple_of(first_row, STRIP), rows)
            along = pl.ds(pl.multiple_of(first_column, 128), columns)
            block = jnp.dot(turned_ref[down, :], mine_ref[:, along], preferred_element_type=F32)
            out_ref[at : at + rows, lane : lane + columns] = block.astype(out_ref.dtype)

        @pl.when(diagonal == 0 if x == 0 else True)
        def _(o=out_ref, r=row * width, c=column * width, s=strip * STRIP, sc=strip_column * width, tall=tall):
            part(o, 0, 0, r, width, c, width)
            part(o, width, 0, s, tall - width, sc, width)

        if x == 0:

            @pl.when(diagonal == 1)
            def _(o=out_ref, r=row * width, c=column * width, s=strip * STRIP, sc=strip_column * width, tall=tall):
                part(o, 0, 0, r, third, c, width)
                part(o, third, 0, r + third, third, c + third, 2 * third)
                part(o, third, 2 * third, r + 2 * third, third, c + 2 * third, third)
                part(o, 2 * third, 0, s, tall - 2 * third, sc, width)


def moment_blocks(table, pieces, turned, mine, width, dtype, name, after=()):
    count = len(pieces)
    smem, vmem, any_ = [pl.BlockSpec(memory_space=m) for m in (pltpu.SMEM, pltpu.VMEM, pl.ANY)]
    piece = (width + STRIP, width)
    return pl.pallas_call(
        functools.partial(blocks_kernel, pieces, width),
        out_shape=[jax.ShapeDtypeStruct(piece, dtype)] * count,
        in_specs=[smem, vmem, vmem] + [any_] * len(after),
        out_specs=[vmem] * count,
        cost_estimate=pl.CostEstimate(
            flops=count * mine.shape[0] * width * width,
            bytes_accessed=0,
            transcendentals=0,
        ),
        compiler_params=pltpu.CompilerParams(vmem_limit_bytes=24 << 20),
        name=name,
    )(table, turned, mine, *after)


STRIP = 32
FIELDS = 5


def is_diagonal(b, e):
    return b // 4 == e


def owned_columns(b, e):
    shift = 0 if is_diagonal(b, e) or e == 1 else 1
    return [(b + shift) % 4, (b + shift + 1) % 4]


def leads(b):
    return b % 4 < 2


def fourth_column(b, e):
    if is_diagonal(b, e):
        return (b + 2) % 4
    return (b + 3) % 4 if e == 1 else b % 4


ROUNDS = (
    ((0, 4), (1, 4), (1, 3), (0, 5)),
    ((0, 3), (1, 5), (1, 2), (0, 6)),
    ((0, 2), (1, 6), (1, 1), (0, 7)),
    ((0, 1), (1, 7), (0, 0), (1, 0)),
)


def job_table(which, width):
    table = np.zeros((8, 2, len(which), FIELDS), np.int32)
    for p, b in enumerate(SNAKE):
        for e in range(2):
            for n, (x, t) in enumerate(which):
                q = SNAKE[(p + t) % 8]
                row, column = q % 4 + (0 if q // 4 == e else 4), owned_columns(q, e)[x]
                if is_diagonal(q, e):
                    lead, other = (q % 4, (q + 2) % 4) if leads(q) else ((q + 2) % 4, q % 4)
                    first = lead * width + (0 if leads(q) else width // 2) + x * (width // 3 + STRIP)
                else:
                    first, other = row * width + x * STRIP, fourth_column(q, e)
                table[b, e, n] = (row, column, first // STRIP, other, is_diagonal(q, e))
    return table.reshape(16, -1)


def ring_perm(direction):
    pairs = [(SNAKE[p], SNAKE[(p + direction) % 8]) for p in range(8)]
    return [(a * 2 + e, b * 2 + e) for a, b in pairs for e in range(2)]


def mirror_perms():
    one, other = [], []
    for b in range(8):
        for e in range(2):
            here = b * 2 + e
            if is_diagonal(b, e):
                one.append((here, (b // 4 * 4 + (b + 1) % 4) * 2 + e))
                other.append((here, (b // 4 * 4 + (b + 2) % 4) * 2 + e))
            elif e == 1:
                other.append((here, (4 + b) * 2))
                one.append((here, (4 + (b + 1) % 4) * 2))
            else:
                other.append((here, (b + 1) % 4 * 2 + 1))
                one.append((here, (b + 2) % 4 * 2 + 1))
    return one, other


def place_table():
    table = np.zeros((8, 2, 5), np.int32)
    for b in range(8):
        for e in range(2):
            diagonal = is_diagonal(b, e)
            mirrored = (b + 2) % 4 if not diagonal and e == 1 else (b + 3) % 4
            kind = (1 if leads(b) else 2) if diagonal else 0
            table[b, e] = (*owned_columns(b, e), mirrored, fourth_column(b, e), kind)
    return table


def total(own, right, left, rows):
    return own[rows, :] + right[rows, :].astype(F32) + left[rows, :].astype(F32)


def outgoing_one_kernel(scale, own1, right1, left1, one):
    one[...] = (total(own1, right1, left1, slice(0, one.shape[0])) * scale).astype(BF16)


def outgoing_other_kernel(scale, place, own0, own1, right0, left1, right1, left0, after, other, share):
    half, width = share.shape
    third, tall = width // 3, width + STRIP
    kind = place[my_row(), 4]
    tail = total(own1, right1, left1, slice(width, tall)) * scale

    @pl.when(kind == 0)
    def _():
        share[:STRIP, :] = total(own0, right0, left0, slice(width, tall)) * scale
        share[STRIP : 2 * STRIP, :] = tail
        share[2 * STRIP :, :] = jnp.zeros((half - 2 * STRIP, width), F32)
        turned = (total(own0, right0, left0, slice(0, width)) * scale).T
        other[...] = turned[2 * STRIP :, :].astype(BF16)

    @pl.when(kind > 0)
    def _():
        share[: half - STRIP, :] = total(own0, right0, left0, slice(2 * third, tall)) * scale
        share[half - STRIP :, :] = tail
        other[:half, :] = share[...].astype(BF16)
        other[half:, :] = jnp.zeros((width - 2 * STRIP - half, width), BF16)


def put(place, n, made, out_ref, sem):
    width = made.shape[0]
    at = pl.ds(pl.multiple_of(place[my_row(), n] * width, 128), width)
    return pltpu.make_async_copy(made, out_ref.at[:, at], sem)


def own_kernel(scale, place, own0, own1, right0, left1, right1, left0, out_ref, made, sems):
    width = made.shape[1]
    third = width // 3
    made[1] = total(own1, right1, left1, slice(0, width)) * scale
    copies = [put(place, n, made.at[n], out_ref, sems.at[n]) for n in range(2)]
    copies[1].start()

    @pl.when(place[my_row(), 4] == 0)
    def _():
        made[0] = total(own0, right0, left0, slice(0, width)) * scale

    @pl.when(place[my_row(), 4] > 0)
    def _():
        tiles = total(own0, right0, left0, slice(0, 2 * third)) * scale
        upper = {(0, 0): (0, 0), (0, 1): (0, 1), (0, 2): (0, 2), (1, 1): (1, 0), (1, 2): (1, 1), (2, 2): (1, 2)}
        for (i, j), (r, c) in upper.items():
            tile = tiles[r * third : (r + 1) * third, c * third : (c + 1) * third]
            made[0, i * third : (i + 1) * third, j * third : (j + 1) * third] = tile
            if i != j:
                made[0, j * third : (j + 1) * third, i * third : (i + 1) * third] = tile.T

    copies[0].start()
    for copy in copies:
        copy.wait()


def one_kernel(place, one, result_ref, out_ref, made, sem):
    made[...] = one[...].astype(F32).T
    copy = put(place, 2, made, out_ref, sem)
    copy.start()
    copy.wait()


def other_kernel(place, share, other, result_ref, out_ref, made, sem):
    kind = place[my_row(), 4]
    half = share.shape[0]

    @pl.when(kind == 0)
    def _():
        made[: 2 * STRIP, :] = share[: 2 * STRIP, :]
        made[2 * STRIP :, :] = other[...].astype(F32)

    @pl.when(kind == 1)
    def _():
        made[:half, :] = share[...]
        made[half:, :] = other[:half, :].astype(F32)

    @pl.when(kind == 2)
    def _():
        made[...] = jnp.concatenate([other[:half, :].astype(F32), share[...]], axis=0).T

    copy = put(place, 3, made, out_ref, sem)
    copy.start()
    copy.wait()


def symmetric_moment(mine, turned, total_tokens):
    width = mine.shape[1] // 4
    both = ("dp", "expert")
    blocks = {}

    def compute(which, name, dtype, after=()):
        table = jnp.asarray(job_table(which, width))
        pieces = tuple(x for x, _ in which)
        blocks.update(zip(which, moment_blocks(table, pieces, turned, mine, width, dtype, name, after)))

    def hop(value, key):
        return lax.ppermute(value, both, ring_perm(1 if key[1] <= (4 if key[0] == 0 else 3) else -1))

    compute(ROUNDS[0][:2], "blocks0", BF16)
    compute(ROUNDS[0][2:], "blocks0b", BF16, after=(blocks[0, 4],))
    moving = {key: blocks[key] for key in ROUNDS[0]}
    arrived = {}
    before = ()
    for n in range(4):
        landed = {}
        for key in ROUNDS[n]:
            if key in moving:
                landed[key] = hop(moving[key], key)
        if n < 3:
            early = [landed[key] for key in ROUNDS[n][:2]]
            compute(ROUNDS[n + 1][:2], f"blocks{n + 1}", F32, after=(blocks[ROUNDS[n][3]], *before))
            compute(ROUNDS[n + 1][2:], f"blocks{n + 1}b", F32, after=early[:1])
            before = early
        moving = {}
        for (x, t), value in landed.items():
            rightwards = t <= (4 if x == 0 else 3)
            t = t - 1 if rightwards else (t + 1) % 8
            if t == 0:
                arrived[x, rightwards] = value
            else:
                moving[x, t] = (value.astype(F32) + blocks[x, t]).astype(BF16)

    place = jnp.asarray(place_table().reshape(16, -1))
    smem, vmem, any_ = [pl.BlockSpec(memory_space=m) for m in (pltpu.SMEM, pltpu.VMEM, pl.ANY)]
    result = jax.ShapeDtypeStruct((width, 4 * width), F32)
    params = pltpu.CompilerParams(vmem_limit_bytes=24 << 20)
    sums = (blocks[0, 0], blocks[1, 0], arrived[0, True], arrived[1, False], arrived[1, True], arrived[0, False])
    scale = 1.0 / total_tokens
    perm_one, perm_other = mirror_perms()
    one = pl.pallas_call(
        functools.partial(outgoing_one_kernel, scale),
        out_shape=jax.ShapeDtypeStruct((width, width), BF16),
        in_specs=[vmem] * 3,
        out_specs=vmem,
        compiler_params=params,
        name="outgoing_one",
    )(sums[1], sums[4], sums[3])
    other, share = pl.pallas_call(
        functools.partial(outgoing_other_kernel, scale),
        out_shape=[
            jax.ShapeDtypeStruct((width - 2 * STRIP, width), BF16),
            jax.ShapeDtypeStruct((width // 2, width), F32),
        ],
        in_specs=[smem] + [vmem] * 6 + [any_],
        out_specs=[vmem] * 2,
        compiler_params=params,
        name="outgoing_other",
    )(place, *sums, one)
    one = lax.ppermute(one, both, perm_one)
    other = lax.ppermute(other, both, perm_other)
    partial_result = pl.pallas_call(
        functools.partial(own_kernel, scale),
        out_shape=result,
        in_specs=[smem] + [vmem] * 6,
        out_specs=any_,
        scratch_shapes=[pltpu.VMEM((2, width, width), F32), pltpu.SemaphoreType.DMA((2,))],
        compiler_params=params,
        name="own",
    )(place, *sums)
    for kernel, args, name in ((one_kernel, (one,), "one"), (other_kernel, (share, other), "other")):
        partial_result = pl.pallas_call(
            kernel,
            out_shape=result,
            in_specs=[smem] + [vmem] * len(args) + [any_],
            out_specs=any_,
            scratch_shapes=[pltpu.VMEM((width, width), F32), pltpu.SemaphoreType.DMA],
            input_output_aliases={len(args) + 1: 0},
            compiler_params=params,
            name=name,
        )(place, *args, partial_result)
    return partial_result


def per_device(expert_ids, gates, expert_out):
    tokens, channels = expert_ids.shape[0], expert_out.shape[1]
    dp_size = lax.axis_size("dp")
    member = lax.axis_index("expert")
    half = channels // 2
    swap = [(0, 1), (1, 0)]

    sent, pick, starts, coef = pick_half((expert_ids.T, gates.T), expert_out, tokens, half, True)
    from_peer = lax.ppermute(sent, "expert", swap)
    (kept,) = pick_half((starts, pick, coef), expert_out, tokens, half, False)
    from_peer_too = lax.ppermute(kept, "expert", swap)
    rows, turned = merge(coef, [kept], [from_peer], half)
    (turned,) = merge(coef, [sent], [from_peer_too], half, turned)

    total_tokens = tokens * dp_size
    if dp_size == 8 and channels == 8 * 384:
        return symmetric_moment(rows, turned, total_tokens)
    slab = jnp.dot(turned, rows, preferred_element_type=F32)
    slab = jnp.where(member == 0, slab, jnp.roll(slab, half, axis=0))
    return lax.psum_scatter(slab, "dp", scatter_dimension=0, tiled=True) / total_tokens


def solution(mesh):
    assert mesh.shape["expert"] == 2
    in_specs = (
        P(("groups", "dp"), None),
        P(("groups", "dp"), None),
        P(("groups", "dp", "expert"), None),
    )
    out_specs = P(("groups", "dp"), "expert")
    return jax.shard_map(
        per_device, mesh=mesh, in_specs=in_specs, out_specs=out_specs, check_vma=False
    )
```

```python
import functools

import jax
import jax.numpy as jnp
import numpy as np
from jax import lax
from jax.experimental import pallas as pl
from jax.experimental.pallas import tpu as pltpu
from jax.sharding import PartitionSpec as P

EXPERTS = 8
CAP = 384
BATCH = 48
WINDOW = 64
SNAKE = (0, 2, 4, 6, 7, 5, 3, 1)
F32, BF16, I32 = jnp.float32, jnp.bfloat16, jnp.int32


def plan_tokens(ids_ref, gates_ref, pick_ref, starts_ref, coef_ref, earlier_ref, inputs, starts_copy):
    tokens = ids_ref.shape[1]
    local = EXPERTS // 2
    earlier_ref[...] = jnp.where(
        lax.broadcasted_iota(I32, (tokens, tokens), 1) < lax.broadcasted_iota(I32, (tokens, tokens), 0), 1.0, 0.0
    ).astype(BF16)
    for copy in inputs:
        copy.wait()
    slots = [ids_ref[k : k + 1, :] - lax.axis_index("expert") * local for k in range(2)]
    gates = [gates_ref[k : k + 1, :] for k in range(2)]
    here = [jnp.where((slots[k] >= 0) & (slots[k] < local), 1.0, 0.0) for k in range(2)]
    both = here[0] * here[1]
    neither = (1.0 - here[0]) * (1.0 - here[1])
    mixed = 1.0 - both - neither
    weights = [here[k] * jnp.where(both > 0.5, gates[k], 1.0) for k in range(2)]
    ours = here[0] * gates[0] + here[1] * gates[1]
    theirs = (1.0 - here[0]) * gates[0] + (1.0 - here[1]) * gates[1]
    ours = jnp.where(mixed > 0.5, ours, both)
    theirs = jnp.where(mixed > 0.5, theirs, neither)
    bases = [jnp.where(here[k] > 0.5, (slots[k] * WINDOW).astype(F32), -4.0 * CAP) for k in range(2)]
    columns = jnp.concatenate([*weights, ours, theirs, ids_ref[...].astype(F32), *bases], axis=0).T
    coef_ref[...] = columns
    lanes = lax.broadcasted_iota(I32, (tokens, 128), 1)
    hits = [columns[:, 4 + k : 5 + k].astype(I32) == lanes for k in range(2)]
    named = jnp.where(hits[0] | hits[1], 1.0, 0.0).astype(BF16)
    before = jnp.dot(earlier_ref[...], named, preferred_element_type=F32)
    firsts = []
    for b in range(tokens // BATCH):
        start = before[b * BATCH : b * BATCH + 1, :].astype(I32)
        firsts.append(jnp.minimum((start >> 4) << 4, CAP - WINDOW))
        starts_ref[b : b + 1, :] = firsts[-1]
    starts_copy.start()

    places = lax.broadcasted_iota(I32, (BATCH, local * WINDOW), 1)
    for b in range(tokens // BATCH):
        rows = slice(b * BATCH, (b + 1) * BATCH)
        ahead = before[rows] - firsts[b].astype(F32)
        for k in range(2):
            offset = jnp.sum(jnp.where(hits[k][rows], ahead, 0.0), axis=1, keepdims=True)
            at = (columns[rows, 6 + k : 7 + k] + offset).astype(I32)
            pick_ref[(2 * b + k) * BATCH : (2 * b + k + 1) * BATCH, :] = jnp.where(places == at, 1.0, 0.0).astype(BF16)


def pick_kernel(first, *refs):
    if first:
        ids_hbm, gates_hbm, rows_ref, out_ref, pick_ref, starts_ref, coef_ref = refs[:7]
        held, in_sems, starts, small_sems, ids_ref, gates_ref, earlier_ref = refs[7:]
    else:
        starts_ref, pick_ref, coef_ref, rows_ref, out_ref, held, in_sems, starts, small_sems = refs
    tokens, width = out_ref.shape
    tiles, _, tile = held.shape
    local = EXPERTS // 2
    member = lax.axis_index("expert")
    base = (1 - member if first else member) * width

    if first:
        small = [
            pltpu.make_async_copy(ids_hbm, ids_ref, small_sems.at[0]),
            pltpu.make_async_copy(gates_hbm, gates_ref, small_sems.at[1]),
        ]
        for copy in small:
            copy.start()
    loads = []
    for j in range(tiles):
        at = pl.ds(pl.multiple_of(base + j * tile, 128), tile)
        loads.append(pltpu.make_async_copy(rows_ref.at[:, at], held.at[j], in_sems.at[j]))
        loads[-1].start()
    copy = pltpu.make_async_copy(starts_ref, starts, small_sems.at[2])
    if first:
        plan_tokens(ids_ref, gates_ref, pick_ref, starts_ref, coef_ref, earlier_ref, small, copy)
    else:
        copy.start()
    copy.wait()
    for j in range(tiles):
        loads[j].wait()
        for b in range(tokens // BATCH):
            windows = []
            for k in range(local):
                at = k * CAP + starts[b, member * local + k]
                windows.append(held[j, pl.ds(pl.multiple_of(at, 16), WINDOW), :])
            picked = jnp.dot(
                pick_ref[2 * b * BATCH : 2 * (b + 1) * BATCH, :],
                jnp.concatenate(windows, axis=0),
                preferred_element_type=F32,
            )
            rows = slice(b * BATCH, (b + 1) * BATCH)
            total = coef_ref[rows, 0:1] * picked[:BATCH] + coef_ref[rows, 1:2] * picked[BATCH:]
            out_ref[rows, j * tile : (j + 1) * tile] = total.astype(BF16)


def pick_half(args, rows, tokens, width, first, tile=512):
    tiles = width // tile
    depth = EXPERTS // 2 * WINDOW
    any_, vmem = pl.BlockSpec(memory_space=pl.ANY), pl.BlockSpec(memory_space=pltpu.VMEM)
    in_hbm = lambda x: pltpu.with_memory_space_constraint(x, pltpu.HBM)
    out_shape = [jax.ShapeDtypeStruct((tokens, width), BF16)]
    scratch = [
        pltpu.VMEM((tiles, rows.shape[0], tile), BF16),
        pltpu.SemaphoreType.DMA((tiles,)),
        pltpu.SMEM((tokens // BATCH, 128), I32),
        pltpu.SemaphoreType.DMA((3,)),
    ]
    if first:
        out_shape += [
            jax.ShapeDtypeStruct((2 * tokens, depth), BF16),
            jax.ShapeDtypeStruct((tokens // BATCH, 128), I32),
            jax.ShapeDtypeStruct((tokens, 8), F32),
        ]
        args = [in_hbm(x) for x in args]
        in_specs = [any_] * 3
        scratch += [
            pltpu.VMEM((2, tokens), I32),
            pltpu.VMEM((2, tokens), F32),
            pltpu.VMEM((tokens, tokens), BF16),
        ]
    else:
        in_specs = [vmem, vmem, vmem, any_]
    return pl.pallas_call(
        functools.partial(pick_kernel, first),
        out_shape=out_shape,
        in_specs=in_specs,
        out_specs=[vmem] * len(out_shape),
        scratch_shapes=scratch,
        cost_estimate=pl.CostEstimate(
            flops=4 * tokens * depth * width, bytes_accessed=2 * (rows.shape[0] + tokens) * width, transcendentals=0
        ),
        compiler_params=pltpu.CompilerParams(vmem_limit_bytes=24 << 20),
        name="pick_first" if first else "pick_second",
    )(*args, in_hbm(rows))


def merge_kernel(first, tile, pieces, coef_ref, *refs):
    tokens = coef_ref.shape[0]
    sides = []
    for count in pieces:
        sides.append([ref.at[:, j : j + tile] for ref in refs[:count] for j in range(0, ref.shape[1], tile)])
        refs = refs[count:]
    width = len(sides[0]) * tile
    ours = jnp.broadcast_to(coef_ref[:, 2:3], (tokens, tile))
    theirs = jnp.broadcast_to(coef_ref[:, 3:4], (tokens, tile))
    for j, (a, b) in enumerate(zip(*sides)):
        total = (ours * a[...].astype(F32) + theirs * b[...].astype(F32)).astype(BF16)
        if first:
            refs[0][:, j * tile : (j + 1) * tile] = total
            refs[-1][j * tile : (j + 1) * tile, :] = total.T
        else:
            refs[-1][width + j * tile : width + (j + 1) * tile, :] = total.T


def merge(coef, ours, theirs, width, turned=None, tile=256):
    tokens = coef.shape[0]
    first = turned is None
    vmem = pl.BlockSpec(memory_space=pltpu.VMEM)
    args = [coef, *ours, *theirs] + ([] if first else [turned])
    out_shape = [jax.ShapeDtypeStruct((2 * width, tokens), BF16)]
    if first:
        out_shape.insert(0, jax.ShapeDtypeStruct((tokens, width), BF16))
    return pl.pallas_call(
        functools.partial(merge_kernel, first, tile, (len(ours), len(theirs))),
        out_shape=out_shape,
        in_specs=[vmem] * len(args),
        out_specs=[vmem] * len(out_shape),
        input_output_aliases={} if first else {len(args) - 1: 0},
        compiler_params=pltpu.CompilerParams(vmem_limit_bytes=24 << 20),
        cost_estimate=pl.CostEstimate(flops=4 * tokens * width, bytes_accessed=0, transcendentals=0),
        name="merge_first" if first else "merge_second",
    )(*args)


def my_row():
    return lax.axis_index("dp") * 2 + lax.axis_index("expert")


def blocks_kernel(pieces, width, table, turned_ref, mine_ref, *refs):
    third = width // 3
    me = my_row()
    for n, (x, out_ref) in enumerate(zip(pieces, refs[-len(pieces) :])):
        tall = out_ref.shape[0]
        row, column, strip, strip_column, diagonal = [table[me, FIELDS * n + k] for k in range(FIELDS)]

        def part(out_ref, at, lane, first_row, rows, first_column, columns):
            down = pl.ds(pl.multiple_of(first_row, STRIP), rows)
            along = pl.ds(pl.multiple_of(first_column, 128), columns)
            block = jnp.dot(turned_ref[down, :], mine_ref[:, along], preferred_element_type=F32)
            out_ref[at : at + rows, lane : lane + columns] = block.astype(out_ref.dtype)

        @pl.when(diagonal == 0 if x == 0 else True)
        def _(o=out_ref, r=row * width, c=column * width, s=strip * STRIP, sc=strip_column * width, tall=tall):
            part(o, 0, 0, r, width, c, width)
            part(o, width, 0, s, tall - width, sc, width)

        if x == 0:

            @pl.when(diagonal == 1)
            def _(o=out_ref, r=row * width, c=column * width, s=strip * STRIP, sc=strip_column * width, tall=tall):
                part(o, 0, 0, r, third, c, width)
                part(o, third, 0, r + third, third, c + third, 2 * third)
                part(o, third, 2 * third, r + 2 * third, third, c + 2 * third, third)
                part(o, 2 * third, 0, s, tall - 2 * third, sc, width)


def moment_blocks(table, pieces, turned, mine, width, dtype, name, after=()):
    count = len(pieces)
    smem, vmem, any_ = [pl.BlockSpec(memory_space=m) for m in (pltpu.SMEM, pltpu.VMEM, pl.ANY)]
    piece = (width + STRIP, width)
    return pl.pallas_call(
        functools.partial(blocks_kernel, pieces, width),
        out_shape=[jax.ShapeDtypeStruct(piece, dtype)] * count,
        in_specs=[smem, vmem, vmem] + [any_] * len(after),
        out_specs=[vmem] * count,
        cost_estimate=pl.CostEstimate(
            flops=count * mine.shape[0] * width * width,
            bytes_accessed=0,
            transcendentals=0,
        ),
        compiler_params=pltpu.CompilerParams(vmem_limit_bytes=24 << 20),
        name=name,
    )(table, turned, mine, *after)


STRIP = 32
FIELDS = 5


def is_diagonal(b, e):
    return b // 4 == e


def owned_columns(b, e):
    shift = 0 if is_diagonal(b, e) or e == 1 else 1
    return [(b + shift) % 4, (b + shift + 1) % 4]


def leads(b):
    return b % 4 < 2


def fourth_column(b, e):
    if is_diagonal(b, e):
        return (b + 2) % 4
    return (b + 3) % 4 if e == 1 else b % 4


ROUNDS = (
    ((0, 4), (1, 4), (1, 3), (0, 5)),
    ((0, 3), (1, 5), (1, 2), (0, 6)),
    ((0, 2), (1, 6), (1, 1), (0, 7)),
    ((0, 1), (1, 7), (0, 0), (1, 0)),
)


def job_table(which, width):
    table = np.zeros((8, 2, len(which), FIELDS), np.int32)
    for p, b in enumerate(SNAKE):
        for e in range(2):
            for n, (x, t) in enumerate(which):
                q = SNAKE[(p + t) % 8]
                row, column = q % 4 + (0 if q // 4 == e else 4), owned_columns(q, e)[x]
                if is_diagonal(q, e):
                    lead, other = (q % 4, (q + 2) % 4) if leads(q) else ((q + 2) % 4, q % 4)
                    first = lead * width + (0 if leads(q) else width // 2) + x * (width // 3 + STRIP)
                else:
                    first, other = row * width + x * STRIP, fourth_column(q, e)
                table[b, e, n] = (row, column, first // STRIP, other, is_diagonal(q, e))
    return table.reshape(16, -1)


def ring_perm(direction):
    pairs = [(SNAKE[p], SNAKE[(p + direction) % 8]) for p in range(8)]
    return [(a * 2 + e, b * 2 + e) for a, b in pairs for e in range(2)]


def mirror_perms():
    one, other = [], []
    for b in range(8):
        for e in range(2):
            here = b * 2 + e
            if is_diagonal(b, e):
                one.append((here, (b // 4 * 4 + (b + 1) % 4) * 2 + e))
                other.append((here, (b // 4 * 4 + (b + 2) % 4) * 2 + e))
            elif e == 1:
                other.append((here, (4 + b) * 2))
                one.append((here, (4 + (b + 1) % 4) * 2))
            else:
                other.append((here, (b + 1) % 4 * 2 + 1))
                one.append((here, (b + 2) % 4 * 2 + 1))
    return one, other


def place_table():
    table = np.zeros((8, 2, 5), np.int32)
    for b in range(8):
        for e in range(2):
            diagonal = is_diagonal(b, e)
            mirrored = (b + 2) % 4 if not diagonal and e == 1 else (b + 3) % 4
            kind = (1 if leads(b) else 2) if diagonal else 0
            table[b, e] = (*owned_columns(b, e), mirrored, fourth_column(b, e), kind)
    return table


def total(own, right, left, rows):
    return own[rows, :] + right[rows, :].astype(F32) + left[rows, :].astype(F32)


def outgoing_one_kernel(scale, own1, right1, left1, one):
    one[...] = (total(own1, right1, left1, slice(0, one.shape[0])) * scale).astype(BF16)


def outgoing_other_kernel(scale, place, own0, own1, right0, left1, right1, left0, after, other, share):
    half, width = share.shape
    third, tall = width // 3, width + STRIP
    kind = place[my_row(), 4]
    tail = total(own1, right1, left1, slice(width, tall)) * scale

    @pl.when(kind == 0)
    def _():
        share[:STRIP, :] = total(own0, right0, left0, slice(width, tall)) * scale
        share[STRIP : 2 * STRIP, :] = tail
        share[2 * STRIP :, :] = jnp.zeros((half - 2 * STRIP, width), F32)
        turned = (total(own0, right0, left0, slice(0, width)) * scale).T
        other[...] = turned[2 * STRIP :, :].astype(BF16)

    @pl.when(kind > 0)
    def _():
        share[: half - STRIP, :] = total(own0, right0, left0, slice(2 * third, tall)) * scale
        share[half - STRIP :, :] = tail
        other[:half, :] = share[...].astype(BF16)
        other[half:, :] = jnp.zeros((width - 2 * STRIP - half, width), BF16)


def put(place, n, made, out_ref, sem):
    width = made.shape[0]
    at = pl.ds(pl.multiple_of(place[my_row(), n] * width, 128), width)
    return pltpu.make_async_copy(made, out_ref.at[:, at], sem)


def own_kernel(scale, place, own0, own1, right0, left1, right1, left0, out_ref, made, sems):
    width = made.shape[1]
    third = width // 3
    made[1] = total(own1, right1, left1, slice(0, width)) * scale
    copies = [put(place, n, made.at[n], out_ref, sems.at[n]) for n in range(2)]
    copies[1].start()

    @pl.when(place[my_row(), 4] == 0)
    def _():
        made[0] = total(own0, right0, left0, slice(0, width)) * scale

    @pl.when(place[my_row(), 4] > 0)
    def _():
        tiles = total(own0, right0, left0, slice(0, 2 * third)) * scale
        upper = {(0, 0): (0, 0), (0, 1): (0, 1), (0, 2): (0, 2), (1, 1): (1, 0), (1, 2): (1, 1), (2, 2): (1, 2)}
        for (i, j), (r, c) in upper.items():
            tile = tiles[r * third : (r + 1) * third, c * third : (c + 1) * third]
            made[0, i * third : (i + 1) * third, j * third : (j + 1) * third] = tile
            if i != j:
                made[0, j * third : (j + 1) * third, i * third : (i + 1) * third] = tile.T

    copies[0].start()
    for copy in copies:
        copy.wait()


def one_kernel(place, one, result_ref, out_ref, made, sem):
    made[...] = one[...].astype(F32).T
    copy = put(place, 2, made, out_ref, sem)
    copy.start()
    copy.wait()


def other_kernel(place, share, other, result_ref, out_ref, made, sem):
    kind = place[my_row(), 4]
    half = share.shape[0]

    @pl.when(kind == 0)
    def _():
        made[: 2 * STRIP, :] = share[: 2 * STRIP, :]
        made[2 * STRIP :, :] = other[...].astype(F32)

    @pl.when(kind == 1)
    def _():
        made[:half, :] = share[...]
        made[half:, :] = other[:half, :].astype(F32)

    @pl.when(kind == 2)
    def _():
        made[...] = jnp.concatenate([other[:half, :].astype(F32), share[...]], axis=0).T

    copy = put(place, 3, made, out_ref, sem)
    copy.start()
    copy.wait()


def symmetric_moment(mine, turned, total_tokens):
    width = mine.shape[1] // 4
    both = ("dp", "expert")
    blocks = {}

    def compute(which, name, dtype, after=()):
        table = jnp.asarray(job_table(which, width))
        pieces = tuple(x for x, _ in which)
        blocks.update(zip(which, moment_blocks(table, pieces, turned, mine, width, dtype, name, after)))

    def hop(value, key):
        return lax.ppermute(value, both, ring_perm(1 if key[1] <= (4 if key[0] == 0 else 3) else -1))

    compute(ROUNDS[0][:2], "blocks0", BF16)
    compute(ROUNDS[0][2:], "blocks0b", BF16, after=(blocks[0, 4],))
    moving = {key: blocks[key] for key in ROUNDS[0]}
    arrived = {}
    before = ()
    for n in range(4):
        landed = {}
        for key in ROUNDS[n]:
            if key in moving:
                landed[key] = hop(moving[key], key)
        if n < 3:
            early = [landed[key] for key in ROUNDS[n][:2]]
            compute(ROUNDS[n + 1][:2], f"blocks{n + 1}", F32, after=(blocks[ROUNDS[n][3]], *before))
            compute(ROUNDS[n + 1][2:], f"blocks{n + 1}b", F32, after=early[:1])
            before = early
        moving = {}
        for (x, t), value in landed.items():
            rightwards = t <= (4 if x == 0 else 3)
            t = t - 1 if rightwards else (t + 1) % 8
            if t == 0:
                arrived[x, rightwards] = value
            else:
                moving[x, t] = (value.astype(F32) + blocks[x, t]).astype(BF16)

    place = jnp.asarray(place_table().reshape(16, -1))
    smem, vmem, any_ = [pl.BlockSpec(memory_space=m) for m in (pltpu.SMEM, pltpu.VMEM, pl.ANY)]
    result = jax.ShapeDtypeStruct((width, 4 * width), F32)
    params = pltpu.CompilerParams(vmem_limit_bytes=24 << 20)
    sums = (blocks[0, 0], blocks[1, 0], arrived[0, True], arrived[1, False], arrived[1, True], arrived[0, False])
    scale = 1.0 / total_tokens
    perm_one, perm_other = mirror_perms()
    one = pl.pallas_call(
        functools.partial(outgoing_one_kernel, scale),
        out_shape=jax.ShapeDtypeStruct((width, width), BF16),
        in_specs=[vmem] * 3,
        out_specs=vmem,
        compiler_params=params,
        name="outgoing_one",
    )(sums[1], sums[4], sums[3])
    other, share = pl.pallas_call(
        functools.partial(outgoing_other_kernel, scale),
        out_shape=[
            jax.ShapeDtypeStruct((width - 2 * STRIP, width), BF16),
            jax.ShapeDtypeStruct((width // 2, width), F32),
        ],
        in_specs=[smem] + [vmem] * 6 + [any_],
        out_specs=[vmem] * 2,
        compiler_params=params,
        name="outgoing_other",
    )(place, *sums, one)
    one = lax.ppermute(one, both, perm_one)
    other = lax.ppermute(other, both, perm_other)
    partial_result = pl.pallas_call(
        functools.partial(own_kernel, scale),
        out_shape=result,
        in_specs=[smem] + [vmem] * 6,
        out_specs=any_,
        scratch_shapes=[pltpu.VMEM((2, width, width), F32), pltpu.SemaphoreType.DMA((2,))],
        compiler_params=params,
        name="own",
    )(place, *sums)
    for kernel, args, name in ((one_kernel, (one,), "one"), (other_kernel, (share, other), "other")):
        partial_result = pl.pallas_call(
            kernel,
            out_shape=result,
            in_specs=[smem] + [vmem] * len(args) + [any_],
            out_specs=any_,
            scratch_shapes=[pltpu.VMEM((width, width), F32), pltpu.SemaphoreType.DMA],
            input_output_aliases={len(args) + 1: 0},
            compiler_params=params,
            name=name,
        )(place, *args, partial_result)
    return partial_result


def per_device(expert_ids, gates, expert_out):
    tokens, channels = expert_ids.shape[0], expert_out.shape[1]
    dp_size = lax.axis_size("dp")
    member = lax.axis_index("expert")
    half = channels // 2
    swap = [(0, 1), (1, 0)]

    sent, pick, starts, coef = pick_half((expert_ids.T, gates.T), expert_out, tokens, half, True)
    from_peer = lax.ppermute(sent, "expert", swap)
    (kept,) = pick_half((starts, pick, coef), expert_out, tokens, half, False)
    from_peer_too = lax.ppermute(kept, "expert", swap)
    rows, turned = merge(coef, [kept], [from_peer], half)
    (turned,) = merge(coef, [sent], [from_peer_too], half, turned)

    total_tokens = tokens * dp_size
    if dp_size == 8 and channels == 8 * 384:
        return symmetric_moment(rows, turned, total_tokens)
    slab = jnp.dot(turned, rows, preferred_element_type=F32)
    slab = jnp.where(member == 0, slab, jnp.roll(slab, half, axis=0))
    return lax.psum_scatter(slab, "dp", scatter_dimension=0, tiled=True) / total_tokens


def solution(mesh):
    assert mesh.shape["expert"] == 2
    in_specs = (
        P(("groups", "dp"), None),
        P(("groups", "dp"), None),
        P(("groups", "dp", "expert"), None),
    )
    out_specs = P(("groups", "dp"), "expert")
    return jax.shard_map(
        per_device, mesh=mesh, in_specs=in_specs, out_specs=out_specs, check_vma=False
    )
```

```python
import functools

import jax
import jax.numpy as jnp
import numpy as np
from jax import lax
from jax.experimental import pallas as pl
from jax.experimental.pallas import tpu as pltpu
from jax.sharding import PartitionSpec as P

EXPERTS = 8
CAP = 384
BATCH = 48
WINDOW = 64
SNAKE = (0, 2, 4, 6, 7, 5, 3, 1)
F32, BF16, I32 = jnp.float32, jnp.bfloat16, jnp.int32


def plan_tokens(ids_ref, gates_ref, pick_ref, starts_ref, coef_ref, earlier_ref, inputs, starts_copy):
    tokens = ids_ref.shape[1]
    local = EXPERTS // 2
    earlier_ref[...] = jnp.where(
        lax.broadcasted_iota(I32, (tokens, tokens), 1) < lax.broadcasted_iota(I32, (tokens, tokens), 0), 1.0, 0.0
    ).astype(BF16)
    for copy in inputs:
        copy.wait()
    slots = [ids_ref[k : k + 1, :] - lax.axis_index("expert") * local for k in range(2)]
    gates = [gates_ref[k : k + 1, :] for k in range(2)]
    here = [jnp.where((slots[k] >= 0) & (slots[k] < local), 1.0, 0.0) for k in range(2)]
    both = here[0] * here[1]
    neither = (1.0 - here[0]) * (1.0 - here[1])
    mixed = 1.0 - both - neither
    weights = [here[k] * jnp.where(both > 0.5, gates[k], 1.0) for k in range(2)]
    ours = here[0] * gates[0] + here[1] * gates[1]
    theirs = (1.0 - here[0]) * gates[0] + (1.0 - here[1]) * gates[1]
    ours = jnp.where(mixed > 0.5, ours, both)
    theirs = jnp.where(mixed > 0.5, theirs, neither)
    bases = [jnp.where(here[k] > 0.5, (slots[k] * WINDOW).astype(F32), -4.0 * CAP) for k in range(2)]
    columns = jnp.concatenate([*weights, ours, theirs, ids_ref[...].astype(F32), *bases], axis=0).T
    coef_ref[...] = columns
    lanes = lax.broadcasted_iota(I32, (tokens, 128), 1)
    hits = [columns[:, 4 + k : 5 + k].astype(I32) == lanes for k in range(2)]
    named = jnp.where(hits[0] | hits[1], 1.0, 0.0).astype(BF16)
    before = jnp.dot(earlier_ref[...], named, preferred_element_type=F32)
    firsts = []
    for b in range(tokens // BATCH):
        start = before[b * BATCH : b * BATCH + 1, :].astype(I32)
        firsts.append(jnp.minimum((start >> 4) << 4, CAP - WINDOW))
        starts_ref[b : b + 1, :] = firsts[-1]
    starts_copy.start()

    places = lax.broadcasted_iota(I32, (BATCH, local * WINDOW), 1)
    for b in range(tokens // BATCH):
        rows = slice(b * BATCH, (b + 1) * BATCH)
        ahead = before[rows] - firsts[b].astype(F32)
        for k in range(2):
            offset = jnp.sum(jnp.where(hits[k][rows], ahead, 0.0), axis=1, keepdims=True)
            at = (columns[rows, 6 + k : 7 + k] + offset).astype(I32)
            pick_ref[(2 * b + k) * BATCH : (2 * b + k + 1) * BATCH, :] = jnp.where(places == at, 1.0, 0.0).astype(BF16)


def pick_kernel(first, *refs):
    if first:
        ids_hbm, gates_hbm, rows_ref, out_ref, pick_ref, starts_ref, coef_ref = refs[:7]
        held, in_sems, starts, small_sems, ids_ref, gates_ref, earlier_ref = refs[7:]
    else:
        starts_ref, pick_ref, coef_ref, rows_ref, out_ref, held, in_sems, starts, small_sems = refs
    tokens, width = out_ref.shape
    tiles, _, tile = held.shape
    local = EXPERTS // 2
    member = lax.axis_index("expert")
    base = (1 - member if first else member) * width

    if first:
        small = [
            pltpu.make_async_copy(ids_hbm, ids_ref, small_sems.at[0]),
            pltpu.make_async_copy(gates_hbm, gates_ref, small_sems.at[1]),
        ]
        for copy in small:
            copy.start()
    loads = []
    for j in range(tiles):
        at = pl.ds(pl.multiple_of(base + j * tile, 128), tile)
        loads.append(pltpu.make_async_copy(rows_ref.at[:, at], held.at[j], in_sems.at[j]))
        loads[-1].start()
    copy = pltpu.make_async_copy(starts_ref, starts, small_sems.at[2])
    if first:
        plan_tokens(ids_ref, gates_ref, pick_ref, starts_ref, coef_ref, earlier_ref, small, copy)
    else:
        copy.start()
    copy.wait()
    for j in range(tiles):
        loads[j].wait()
        for b in range(tokens // BATCH):
            windows = []
            for k in range(local):
                at = k * CAP + starts[b, member * local + k]
                windows.append(held[j, pl.ds(pl.multiple_of(at, 16), WINDOW), :])
            picked = jnp.dot(
                pick_ref[2 * b * BATCH : 2 * (b + 1) * BATCH, :],
                jnp.concatenate(windows, axis=0),
                preferred_element_type=F32,
            )
            rows = slice(b * BATCH, (b + 1) * BATCH)
            total = coef_ref[rows, 0:1] * picked[:BATCH] + coef_ref[rows, 1:2] * picked[BATCH:]
            out_ref[rows, j * tile : (j + 1) * tile] = total.astype(BF16)


def pick_half(args, rows, tokens, width, first, tile=512):
    tiles = width // tile
    depth = EXPERTS // 2 * WINDOW
    any_, vmem = pl.BlockSpec(memory_space=pl.ANY), pl.BlockSpec(memory_space=pltpu.VMEM)
    in_hbm = lambda x: pltpu.with_memory_space_constraint(x, pltpu.HBM)
    out_shape = [jax.ShapeDtypeStruct((tokens, width), BF16)]
    scratch = [
        pltpu.VMEM((tiles, rows.shape[0], tile), BF16),
        pltpu.SemaphoreType.DMA((tiles,)),
        pltpu.SMEM((tokens // BATCH, 128), I32),
        pltpu.SemaphoreType.DMA((3,)),
    ]
    if first:
        out_shape += [
            jax.ShapeDtypeStruct((2 * tokens, depth), BF16),
            jax.ShapeDtypeStruct((tokens // BATCH, 128), I32),
            jax.ShapeDtypeStruct((tokens, 8), F32),
        ]
        args = [in_hbm(x) for x in args]
        in_specs = [any_] * 3
        scratch += [
            pltpu.VMEM((2, tokens), I32),
            pltpu.VMEM((2, tokens), F32),
            pltpu.VMEM((tokens, tokens), BF16),
        ]
    else:
        in_specs = [vmem, vmem, vmem, any_]
    return pl.pallas_call(
        functools.partial(pick_kernel, first),
        out_shape=out_shape,
        in_specs=in_specs,
        out_specs=[vmem] * len(out_shape),
        scratch_shapes=scratch,
        cost_estimate=pl.CostEstimate(
            flops=4 * tokens * depth * width, bytes_accessed=2 * (rows.shape[0] + tokens) * width, transcendentals=0
        ),
        compiler_params=pltpu.CompilerParams(vmem_limit_bytes=24 << 20),
        name="pick_first" if first else "pick_second",
    )(*args, in_hbm(rows))


def merge_kernel(first, tile, pieces, coef_ref, *refs):
    tokens = coef_ref.shape[0]
    sides = []
    for count in pieces:
        sides.append([ref.at[:, j : j + tile] for ref in refs[:count] for j in range(0, ref.shape[1], tile)])
        refs = refs[count:]
    width = len(sides[0]) * tile
    ours = jnp.broadcast_to(coef_ref[:, 2:3], (tokens, tile))
    theirs = jnp.broadcast_to(coef_ref[:, 3:4], (tokens, tile))
    for j, (a, b) in enumerate(zip(*sides)):
        total = (ours * a[...].astype(F32) + theirs * b[...].astype(F32)).astype(BF16)
        if first:
            refs[0][:, j * tile : (j + 1) * tile] = total
            refs[-1][j * tile : (j + 1) * tile, :] = total.T
        else:
            refs[-1][width + j * tile : width + (j + 1) * tile, :] = total.T


def merge(coef, ours, theirs, width, turned=None, tile=256):
    tokens = coef.shape[0]
    first = turned is None
    vmem = pl.BlockSpec(memory_space=pltpu.VMEM)
    args = [coef, *ours, *theirs] + ([] if first else [turned])
    out_shape = [jax.ShapeDtypeStruct((2 * width, tokens), BF16)]
    if first:
        out_shape.insert(0, jax.ShapeDtypeStruct((tokens, width), BF16))
    return pl.pallas_call(
        functools.partial(merge_kernel, first, tile, (len(ours), len(theirs))),
        out_shape=out_shape,
        in_specs=[vmem] * len(args),
        out_specs=[vmem] * len(out_shape),
        input_output_aliases={} if first else {len(args) - 1: 0},
        compiler_params=pltpu.CompilerParams(vmem_limit_bytes=24 << 20),
        cost_estimate=pl.CostEstimate(flops=4 * tokens * width, bytes_accessed=0, transcendentals=0),
        name="merge_first" if first else "merge_second",
    )(*args)


def my_row():
    return lax.axis_index("dp") * 2 + lax.axis_index("expert")


def blocks_kernel(pieces, width, table, turned_ref, mine_ref, *refs):
    third = width // 3
    me = my_row()
    for n, (x, out_ref) in enumerate(zip(pieces, refs[-len(pieces) :])):
        tall = out_ref.shape[0]
        row, column, strip, strip_column, diagonal = [table[me, FIELDS * n + k] for k in range(FIELDS)]

        def part(out_ref, at, lane, first_row, rows, first_column, columns):
            down = pl.ds(pl.multiple_of(first_row, STRIP), rows)
            along = pl.ds(pl.multiple_of(first_column, 128), columns)
            block = jnp.dot(turned_ref[down, :], mine_ref[:, along], preferred_element_type=F32)
            out_ref[at : at + rows, lane : lane + columns] = block.astype(out_ref.dtype)

        @pl.when(diagonal == 0 if x == 0 else True)
        def _(o=out_ref, r=row * width, c=column * width, s=strip * STRIP, sc=strip_column * width, tall=tall):
            part(o, 0, 0, r, width, c, width)
            part(o, width, 0, s, tall - width, sc, width)

        if x == 0:

            @pl.when(diagonal == 1)
            def _(o=out_ref, r=row * width, c=column * width, s=strip * STRIP, sc=strip_column * width, tall=tall):
                part(o, 0, 0, r, third, c, width)
                part(o, third, 0, r + third, third, c + third, 2 * third)
                part(o, third, 2 * third, r + 2 * third, third, c + 2 * third, third)
                part(o, 2 * third, 0, s, tall - 2 * third, sc, width)


def moment_blocks(table, pieces, turned, mine, width, dtype, name, after=()):
    count = len(pieces)
    smem, vmem, any_ = [pl.BlockSpec(memory_space=m) for m in (pltpu.SMEM, pltpu.VMEM, pl.ANY)]
    piece = (width + STRIP, width)
    return pl.pallas_call(
        functools.partial(blocks_kernel, pieces, width),
        out_shape=[jax.ShapeDtypeStruct(piece, dtype)] * count,
        in_specs=[smem, vmem, vmem] + [any_] * len(after),
        out_specs=[vmem] * count,
        cost_estimate=pl.CostEstimate(
            flops=count * mine.shape[0] * width * width,
            bytes_accessed=0,
            transcendentals=0,
        ),
        compiler_params=pltpu.CompilerParams(vmem_limit_bytes=24 << 20),
        name=name,
    )(table, turned, mine, *after)


STRIP = 32
FIELDS = 5


def is_diagonal(b, e):
    return b // 4 == e


def owned_columns(b, e):
    shift = 0 if is_diagonal(b, e) or e == 1 else 1
    return [(b + shift) % 4, (b + shift + 1) % 4]


def leads(b):
    return b % 4 < 2


def fourth_column(b, e):
    if is_diagonal(b, e):
        return (b + 2) % 4
    return (b + 3) % 4 if e == 1 else b % 4


ROUNDS = (
    ((0, 4), (1, 4), (1, 3), (0, 5)),
    ((0, 3), (1, 5), (1, 2), (0, 6)),
    ((0, 2), (1, 6), (1, 1), (0, 7)),
    ((0, 1), (1, 7), (0, 0), (1, 0)),
)


def job_table(which, width):
    table = np.zeros((8, 2, len(which), FIELDS), np.int32)
    for p, b in enumerate(SNAKE):
        for e in range(2):
            for n, (x, t) in enumerate(which):
                q = SNAKE[(p + t) % 8]
                row, column = q % 4 + (0 if q // 4 == e else 4), owned_columns(q, e)[x]
                if is_diagonal(q, e):
                    lead, other = (q % 4, (q + 2) % 4) if leads(q) else ((q + 2) % 4, q % 4)
                    first = lead * width + (0 if leads(q) else width // 2) + x * (width // 3 + STRIP)
                else:
                    first, other = row * width + x * STRIP, fourth_column(q, e)
                table[b, e, n] = (row, column, first // STRIP, other, is_diagonal(q, e))
    return table.reshape(16, -1)


def ring_perm(direction):
    pairs = [(SNAKE[p], SNAKE[(p + direction) % 8]) for p in range(8)]
    return [(a * 2 + e, b * 2 + e) for a, b in pairs for e in range(2)]


def mirror_perms():
    one, other = [], []
    for b in range(8):
        for e in range(2):
            here = b * 2 + e
            if is_diagonal(b, e):
                one.append((here, (b // 4 * 4 + (b + 1) % 4) * 2 + e))
                other.append((here, (b // 4 * 4 + (b + 2) % 4) * 2 + e))
            elif e == 1:
                other.append((here, (4 + b) * 2))
                one.append((here, (4 + (b + 1) % 4) * 2))
            else:
                other.append((here, (b + 1) % 4 * 2 + 1))
                one.append((here, (b + 2) % 4 * 2 + 1))
    return one, other


def place_table():
    table = np.zeros((8, 2, 5), np.int32)
    for b in range(8):
        for e in range(2):
            diagonal = is_diagonal(b, e)
            mirrored = (b + 2) % 4 if not diagonal and e == 1 else (b + 3) % 4
            kind = (1 if leads(b) else 2) if diagonal else 0
            table[b, e] = (*owned_columns(b, e), mirrored, fourth_column(b, e), kind)
    return table


def total(own, right, left, rows):
    return own[rows, :] + right[rows, :].astype(F32) + left[rows, :].astype(F32)


def outgoing_one_kernel(scale, own1, right1, left1, one):
    one[...] = (total(own1, right1, left1, slice(0, one.shape[0])) * scale).astype(BF16)


def outgoing_other_kernel(scale, place, own0, own1, right0, left1, right1, left0, after, other, share):
    half, width = share.shape
    third, tall = width // 3, width + STRIP
    kind = place[my_row(), 4]
    tail = total(own1, right1, left1, slice(width, tall)) * scale

    @pl.when(kind == 0)
    def _():
        share[:STRIP, :] = total(own0, right0, left0, slice(width, tall)) * scale
        share[STRIP : 2 * STRIP, :] = tail
        share[2 * STRIP :, :] = jnp.zeros((half - 2 * STRIP, width), F32)
        turned = (total(own0, right0, left0, slice(0, width)) * scale).T
        other[...] = turned[2 * STRIP :, :].astype(BF16)

    @pl.when(kind > 0)
    def _():
        share[: half - STRIP, :] = total(own0, right0, left0, slice(2 * third, tall)) * scale
        share[half - STRIP :, :] = tail
        other[:half, :] = share[...].astype(BF16)
        other[half:, :] = jnp.zeros((width - 2 * STRIP - half, width), BF16)


def put(place, n, made, out_ref, sem):
    width = made.shape[0]
    at = pl.ds(pl.multiple_of(place[my_row(), n] * width, 128), width)
    return pltpu.make_async_copy(made, out_ref.at[:, at], sem)


def own_kernel(scale, place, own0, own1, right0, left1, right1, left0, out_ref, made, sems):
    width = made.shape[1]
    third = width // 3
    made[1] = total(own1, right1, left1, slice(0, width)) * scale
    copies = [put(place, n, made.at[n], out_ref, sems.at[n]) for n in range(2)]
    copies[1].start()

    @pl.when(place[my_row(), 4] == 0)
    def _():
        made[0] = total(own0, right0, left0, slice(0, width)) * scale

    @pl.when(place[my_row(), 4] > 0)
    def _():
        tiles = total(own0, right0, left0, slice(0, 2 * third)) * scale
        upper = {(0, 0): (0, 0), (0, 1): (0, 1), (0, 2): (0, 2), (1, 1): (1, 0), (1, 2): (1, 1), (2, 2): (1, 2)}
        for (i, j), (r, c) in upper.items():
            tile = tiles[r * third : (r + 1) * third, c * third : (c + 1) * third]
            made[0, i * third : (i + 1) * third, j * third : (j + 1) * third] = tile
            if i != j:
                made[0, j * third : (j + 1) * third, i * third : (i + 1) * third] = tile.T

    copies[0].start()
    for copy in copies:
        copy.wait()


def one_kernel(place, one, result_ref, out_ref, made, sem):
    made[...] = one[...].astype(F32).T
    copy = put(place, 2, made, out_ref, sem.at[0])
    copy.start()
    copy.wait()


def other_kernel(place, share, other, result_ref, out_ref, made, sem):
    kind = place[my_row(), 4]
    half = share.shape[0]

    @pl.when(kind == 0)
    def _():
        made[: 2 * STRIP, :] = share[: 2 * STRIP, :]
        made[2 * STRIP : half, :] = other[: half - 2 * STRIP, :].astype(F32)

    @pl.when(kind == 1)
    def _():
        made[:half, :] = share[...]

    @pl.when(kind == 2)
    def _():
        made[...] = jnp.concatenate([other[:half, :].astype(F32), share[...]], axis=0).T

    width = made.shape[0]
    at = pl.ds(pl.multiple_of(place[my_row(), 3] * width, 128), width)
    copies = [
        pltpu.make_async_copy(made.at[rows], out_ref.at[rows, at], sem.at[n])
        for n, rows in enumerate((slice(0, half), slice(half, width)))
    ]
    copies[0].start()

    @pl.when(kind == 0)
    def _():
        made[half:, :] = other[half - 2 * STRIP :, :].astype(F32)

    @pl.when(kind == 1)
    def _():
        made[half:, :] = other[:half, :].astype(F32)

    copies[1].start()
    for copy in copies:
        copy.wait()


def symmetric_moment(mine, turned, total_tokens):
    width = mine.shape[1] // 4
    both = ("dp", "expert")
    blocks = {}

    def compute(which, name, dtype, after=()):
        table = jnp.asarray(job_table(which, width))
        pieces = tuple(x for x, _ in which)
        blocks.update(zip(which, moment_blocks(table, pieces, turned, mine, width, dtype, name, after)))

    def hop(value, key):
        return lax.ppermute(value, both, ring_perm(1 if key[1] <= (4 if key[0] == 0 else 3) else -1))

    compute(ROUNDS[0][:2], "blocks0", BF16)
    compute(ROUNDS[0][2:], "blocks0b", BF16, after=(blocks[0, 4],))
    moving = {key: blocks[key] for key in ROUNDS[0]}
    arrived = {}
    before = ()
    for n in range(4):
        landed = {}
        for key in ROUNDS[n]:
            if key in moving:
                landed[key] = hop(moving[key], key)
        if n < 3:
            early = [landed[key] for key in ROUNDS[n][:2]]
            compute(ROUNDS[n + 1][:2], f"blocks{n + 1}", F32, after=(blocks[ROUNDS[n][3]], *before))
            compute(ROUNDS[n + 1][2:], f"blocks{n + 1}b", F32, after=early[:1])
            before = early
        moving = {}
        for (x, t), value in landed.items():
            rightwards = t <= (4 if x == 0 else 3)
            t = t - 1 if rightwards else (t + 1) % 8
            if t == 0:
                arrived[x, rightwards] = value
            else:
                moving[x, t] = (value.astype(F32) + blocks[x, t]).astype(BF16)

    place = jnp.asarray(place_table().reshape(16, -1))
    smem, vmem, any_ = [pl.BlockSpec(memory_space=m) for m in (pltpu.SMEM, pltpu.VMEM, pl.ANY)]
    result = jax.ShapeDtypeStruct((width, 4 * width), F32)
    params = pltpu.CompilerParams(vmem_limit_bytes=24 << 20)
    sums = (blocks[0, 0], blocks[1, 0], arrived[0, True], arrived[1, False], arrived[1, True], arrived[0, False])
    scale = 1.0 / total_tokens
    perm_one, perm_other = mirror_perms()
    one = pl.pallas_call(
        functools.partial(outgoing_one_kernel, scale),
        out_shape=jax.ShapeDtypeStruct((width, width), BF16),
        in_specs=[vmem] * 3,
        out_specs=vmem,
        compiler_params=params,
        name="outgoing_one",
    )(sums[1], sums[4], sums[3])
    other, share = pl.pallas_call(
        functools.partial(outgoing_other_kernel, scale),
        out_shape=[
            jax.ShapeDtypeStruct((width - 2 * STRIP, width), BF16),
            jax.ShapeDtypeStruct((width // 2, width), F32),
        ],
        in_specs=[smem] + [vmem] * 6 + [any_],
        out_specs=[vmem] * 2,
        compiler_params=params,
        name="outgoing_other",
    )(place, *sums, one)
    one = lax.ppermute(one, both, perm_one)
    other = lax.ppermute(other, both, perm_other)
    partial_result = pl.pallas_call(
        functools.partial(own_kernel, scale),
        out_shape=result,
        in_specs=[smem] + [vmem] * 6,
        out_specs=any_,
        scratch_shapes=[pltpu.VMEM((2, width, width), F32), pltpu.SemaphoreType.DMA((2,))],
        compiler_params=params,
        name="own",
    )(place, *sums)
    for kernel, args, name in ((one_kernel, (one,), "one"), (other_kernel, (share, other), "other")):
        partial_result = pl.pallas_call(
            kernel,
            out_shape=result,
            in_specs=[smem] + [vmem] * len(args) + [any_],
            out_specs=any_,
            scratch_shapes=[pltpu.VMEM((width, width), F32), pltpu.SemaphoreType.DMA((2,))],
            input_output_aliases={len(args) + 1: 0},
            compiler_params=params,
            name=name,
        )(place, *args, partial_result)
    return partial_result


def per_device(expert_ids, gates, expert_out):
    tokens, channels = expert_ids.shape[0], expert_out.shape[1]
    dp_size = lax.axis_size("dp")
    member = lax.axis_index("expert")
    half = channels // 2
    swap = [(0, 1), (1, 0)]

    sent, pick, starts, coef = pick_half((expert_ids.T, gates.T), expert_out, tokens, half, True)
    from_peer = lax.ppermute(sent, "expert", swap)
    (kept,) = pick_half((starts, pick, coef), expert_out, tokens, half, False)
    from_peer_too = lax.ppermute(kept, "expert", swap)
    rows, turned = merge(coef, [kept], [from_peer], half)
    (turned,) = merge(coef, [sent], [from_peer_too], half, turned)

    total_tokens = tokens * dp_size
    if dp_size == 8 and channels == 8 * 384:
        return symmetric_moment(rows, turned, total_tokens)
    slab = jnp.dot(turned, rows, preferred_element_type=F32)
    slab = jnp.where(member == 0, slab, jnp.roll(slab, half, axis=0))
    return lax.psum_scatter(slab, "dp", scatter_dimension=0, tiled=True) / total_tokens


def solution(mesh):
    assert mesh.shape["expert"] == 2
    in_specs = (
        P(("groups", "dp"), None),
        P(("groups", "dp"), None),
        P(("groups", "dp", "expert"), None),
    )
    out_specs = P(("groups", "dp"), "expert")
    return jax.shard_map(
        per_device, mesh=mesh, in_specs=in_specs, out_specs=out_specs, check_vma=False
    )
```
